32 devices in a mesh: dp: 8 (over y, x, core), seq: 4 (over z).
Axes of the slice: x: 2, y: 2, z: 4, core: 2. Of those that a mesh axis runs over, the one named last changes fastest.
Arguments:
- hidden_in: bfloat16 [8, 1024, 1536], P('dp', 'seq'), may hold values from -6 to 6
- segment_ids: int32 [8, 1024], P('dp'), may hold values from 0 to 8, as said below
- gain_attn: bfloat16 [1536], P(('dp', 'seq')), may hold values from 0.5 to 1.5
- w_query: bfloat16 [1536, 768], P(('dp', 'seq')), may hold values from -0.0625 to 0.0625
- w_key: bfloat16 [1536, 768], P(('dp', 'seq')), may hold values from -0.0625 to 0.0625
- w_value: bfloat16 [1536, 768], P(('dp', 'seq')), may hold values from -0.15625 to 0.15625
- w_out: bfloat16 [768, 1536], P(None, ('dp', 'seq')), may hold values from -0.875 to 0.875
- rel_table: bfloat16 [32, 12], replicated, may hold values from -4 to 4
- gain_ff: bfloat16 [1536], P(('dp', 'seq')), may hold values from 0.5 to 1.5
- w_gate: bfloat16 [1536, 3968], P(('dp', 'seq')), may hold values from -0.15625 to 0.15625
- w_up: bfloat16 [1536, 3968], P(('dp', 'seq')), may hold values from -0.15625 to 0.15625
- w_down: bfloat16 [3968, 1536], P(None, ('dp', 'seq')), may hold values from -0.09375 to 0.09375
- cotangent: bfloat16 [8, 1024, 1536], P('dp', 'seq'), may hold values from -6 to 6
Outputs:
- block_out: float32 [8, 1024, 1536], P('dp', 'seq')
- grad_in: float32 [8, 1024, 1536], P('dp', 'seq')
- grad_gain_attn: float32 [1536], P(('dp', 'seq'))
- grad_w_query: float32 [1536, 768], P(('dp', 'seq'))
- grad_w_key: float32 [1536, 768], P(('dp', 'seq'))
- grad_w_value: float32 [1536, 768], P(('dp', 'seq'))
- grad_w_out: float32 [768, 1536], P(None, ('dp', 'seq'))
- grad_rel_table: float32 [32, 12], replicated
- grad_gain_ff: float32 [1536], P(('dp', 'seq'))
- grad_w_gate: float32 [1536, 3968], P(('dp', 'seq'))
- grad_w_up: float32 [1536, 3968], P(('dp', 'seq'))
- grad_w_down: float32 [3968, 1536], P(None, ('dp', 'seq'))
The draws below stay inside these ranges and needn't reach their ends.
Inputs may be any that keep to these rules, and one draw needn't show every extreme that they name: `segment_ids`: along each row the documents are numbered from 1 upward and never fall, each document contiguous; 8 documents are begun in each row before a tail of at most 128 bytes is set to padding (0), so a document may be cut short or covered entirely by the padding.
All inputs are finite; a program needn't handle non-finite values.
Results may differ from the reference program's by a relative error of at most 0.018.
Values may be sent and summed in bfloat16 or wider, within the bound.
A program may use at most 256 MiB of HBM per device.

```python
import jax
import jax.numpy as jnp
from jax import lax

D = 1536
HEADS = 12
KV = 64
FF = 3968
BUCKETS = 32
LENGTH = 1024
INNER = 768
ROWS = 8
DOCS = 8


def draw_segment_ids(key, part):
    key_cut = jax.random.fold_in(key, 11)
    key_pad = jax.random.fold_in(key, 23)
    row_keys = jax.random.split(key_cut, ROWS)
    place = jnp.arange(LENGTH, dtype=jnp.int32)

    def row_starts(row_key):
        order = jax.random.permutation(row_key, LENGTH - 1).astype(jnp.int32)
        chosen = order[:DOCS - 1] + 1
        marks = jnp.zeros((LENGTH,), jnp.int32).at[chosen].set(1)
        return jnp.where(place == 0, 1, marks).astype(jnp.int32)
    starts = jax.vmap(row_starts)(row_keys)
    numbers = jnp.cumsum(starts, axis=1).astype(jnp.int32)
    padding = jax.random.randint(key_pad, (ROWS, 1), 0, LENGTH // 8 + 1)
    first_row = jnp.arange(ROWS, dtype=jnp.int32)[:, None] == 0
    padding = jnp.where(first_row, 0, padding).astype(jnp.int32)
    return jnp.where(place[None, :] >= LENGTH - padding, 0, numbers).astype(jnp.int32)


def block_levels(own_key, shape, cuts, low, largest):
    level = 1.0
    for dim, shards_of in cuts:
        steps = jax.random.uniform(jax.random.fold_in(jax.random.fold_in(own_key, 6), dim), (shards_of,), jnp.float32, low / len(cuts), largest / len(cuts))
        level = level * jnp.repeat(jnp.exp(steps), shape[dim] // shards_of).reshape((-1,) + (1,) * (len(shape) - 1 - dim))
    return level


def centred(key, shape, width, most, cuts=(), kind=jnp.bfloat16):
    values = jax.random.normal(key, shape, jnp.float32) * width
    if len(cuts) > 0:
        values = block_levels(key, shape, cuts, -0.22, 0.18) * values
    return jnp.clip(values, min=-most, max=most).astype(kind)


def setup_inputs(seed: int = 0) -> dict:
    streams_of = jax.random.split(jax.random.key(seed), 14)
    hidden_in = centred(streams_of[0], (ROWS, LENGTH, D), 1.0, 6.0, ((0, 8), (1, 4)))
    segment_ids = draw_segment_ids(jax.random.fold_in(streams_of[13], 71), 0)
    gain_attn = jnp.clip(1.0 + 0.1 * jax.random.normal(streams_of[2], (D,), jnp.float32), 0.5, 1.5).astype(jnp.bfloat16)
    w_query = centred(streams_of[3], (D, INNER), (6 * D) ** -0.5, 0.0625, ((0, 32),))
    w_key = centred(streams_of[4], (D, INNER), (6 * D) ** -0.5, 0.0625, ((0, 32),))
    w_value = centred(streams_of[5], (D, INNER), D ** -0.5, 0.15625, ((0, 32),))
    w_out = centred(streams_of[6], (INNER, D), (INNER // 16) ** -0.5, 0.875, ((1, 32),))
    rel_table = centred(streams_of[7], (BUCKETS, HEADS), 1.0, 4.0)
    gain_ff = jnp.clip(1.0 + 0.1 * jax.random.normal(streams_of[8], (D,), jnp.float32), 0.5, 1.5).astype(jnp.bfloat16)
    w_gate = centred(streams_of[9], (D, FF), D ** -0.5, 0.15625, ((0, 32),))
    w_up = centred(streams_of[10], (D, FF), D ** -0.5, 0.15625, ((0, 32),))
    w_down = centred(streams_of[11], (FF, D), FF ** -0.5, 0.09375, ((1, 32),))
    cotangent = centred(streams_of[12], (ROWS, LENGTH, D), 1.0, 6.0, ((0, 8), (1, 4)))
    return dict(hidden_in=hidden_in, segment_ids=segment_ids, gain_attn=gain_attn, w_query=w_query, w_key=w_key, w_value=w_value, w_out=w_out, rel_table=rel_table, gain_ff=gain_ff, w_gate=w_gate, w_up=w_up, w_down=w_down, cotangent=cotangent)


epsilon = 1e-06
far_bounds = (12, 16, 23, 32, 46, 64, 91)
highest = lax.Precision.HIGHEST

@jax.custom_vjp
def low(v):
    return lax.optimization_barrier(v.astype(jnp.bfloat16)).astype(jnp.float32)

@jax.custom_vjp
def low_back(v):
    return v

def low_keep(v):
    return (low(v), None)

def low_pass(kept, grad):
    return (grad,)

def back_keep(v):
    return (v, None)

def back_low(kept, grad):
    return (low(grad),)
low.defvjp(low_keep, low_pass)
low_back.defvjp(back_keep, back_low)

def bucket_table(offset):
    magnitude = jnp.abs(offset)
    distant = 8 + sum(((magnitude >= bound).astype(jnp.int32) for bound in far_bounds))
    signed_part = jnp.where(offset > 0, 16, 0).astype(jnp.int32)
    return (signed_part + jnp.where(magnitude < 8, magnitude, distant)).astype(jnp.int32)

def rms_normed(hidden, gain):
    return hidden * lax.rsqrt(lax.optimization_barrier(jnp.mean(hidden * hidden, axis=-1, keepdims=True)) + epsilon) * gain

def project(values, weight):
    return jnp.einsum('gtd,de->gte', values, weight, precision=highest)

def block_forward(hidden, segments, gain_attn, w_query, w_key, w_value, w_out, table, gain_ff, w_gate, w_up, w_down):
    place = jnp.arange(LENGTH, dtype=jnp.int32)
    buckets = bucket_table(place[None, :] - place[:, None])
    onehot = (buckets[:, :, None] == jnp.arange(BUCKETS, dtype=jnp.int32)).astype(jnp.float32)
    bias = jnp.einsum('qkb,bh->hqk', onehot, table, precision=highest)
    self_pair = place[:, None] == place[None, :]
    normed_a = low(rms_normed(hidden, gain_attn))
    queries = low_back(low(project(normed_a, w_query)))
    keys_all = low_back(low(project(normed_a, w_key)))
    values_all = low_back(low(project(normed_a, w_value)))

    def attend(item):
        query_row, key_row, value_row, seg_row = item
        query_heads = query_row.reshape(LENGTH, HEADS, KV)
        key_heads = key_row.reshape(LENGTH, HEADS, KV)
        value_heads = value_row.reshape(LENGTH, HEADS, KV)
        raw_scores = jnp.einsum('qhd,khd->hqk', query_heads, key_heads, precision=highest)
        logits = low_back(raw_scores + bias)
        allowed = (seg_row[:, None] == seg_row[None, :]) & ((seg_row[None, :] > 0) | self_pair)
        masked = jnp.where(allowed[None], logits, -1000000000.0)
        probs = jax.nn.softmax(masked, axis=-1)
        mixed_heads = jnp.einsum('hqk,khd->qhd', low(probs), value_heads, precision=highest)
        return mixed_heads.reshape(LENGTH, HEADS * KV)
    mixed = lax.map(jax.checkpoint(attend), (queries, keys_all, values_all, segments))
    mixed = low_back(low(mixed))
    middle = hidden + low_back(project(mixed, w_out))
    normed_f = low(rms_normed(middle, gain_ff))
    gate_pre = low_back(project(normed_f, w_gate))
    up_pre = low_back(project(normed_f, w_up))
    hidden_mid = low_back(low(jax.nn.gelu(gate_pre, approximate=True) * up_pre))
    return middle + low_back(project(hidden_mid, w_down))

def reference(hidden_in, segment_ids, gain_attn, w_query, w_key, w_value, w_out, rel_table, gain_ff, w_gate, w_up, w_down, cotangent):
    params = tuple((weight.astype(jnp.float32) for weight in (gain_attn, w_query, w_key, w_value, w_out, rel_table, gain_ff, w_gate, w_up, w_down)))
    groups = ROWS // 4
    inputs = hidden_in.astype(jnp.float32).reshape(groups, 4, LENGTH, D)
    segments = segment_ids.astype(jnp.int32).reshape(groups, 4, LENGTH)
    cotangents = cotangent.astype(jnp.float32).reshape(groups, 4, LENGTH, D)

    def step(totals, item):
        group_in, group_seg, group_cot = item

        def forward(values, *weights):
            return block_forward(values, group_seg, *weights)
        outputs, pull = jax.vjp(forward, group_in, *params)
        grads = pull(group_cot)
        new_totals = tuple((left + right for left, right in zip(totals, grads[1:])))
        return (new_totals, (outputs, grads[0]))
    zeros = tuple((jnp.zeros_like(weight) for weight in params))
    totals, (outputs, input_grads) = lax.scan(step, zeros, (inputs, segments, cotangents))
    block_out = outputs.reshape(ROWS, LENGTH, D)
    grad_in = input_grads.reshape(ROWS, LENGTH, D)
    return (block_out, grad_in, totals[0], totals[1], totals[2], totals[3], totals[4], totals[5], totals[6], totals[7], totals[8], totals[9])
```

```python
import jax
import jax.numpy as jnp
from jax import lax
from jax.sharding import PartitionSpec as P

epsilon = 1e-06
far_bounds = (12, 16, 23, 32, 46, 64, 91)
highest = lax.Precision.HIGHEST


def bucket_table(offset):
    magnitude = jnp.abs(offset)
    distant = 8 + sum(((magnitude >= bound).astype(jnp.int32) for bound in far_bounds))
    signed_part = jnp.where(offset > 0, 16, 0).astype(jnp.int32)
    return signed_part + jnp.where(magnitude < 8, magnitude, distant)


def norm_scale(hidden):
    return lax.rsqrt(jnp.mean(hidden * hidden, axis=-1, keepdims=True) + epsilon)


def norm_backward(grad_normed, hidden, scale, gain):
    weighted = grad_normed * gain
    grad_gain = jnp.sum(grad_normed * hidden * scale, axis=0)
    grad_hidden = scale * weighted - hidden * (scale * scale * scale) * jnp.mean(
        weighted * hidden, axis=-1, keepdims=True
    )
    return (grad_hidden, grad_gain)


def scores_of(query_heads, key_heads, bias, allowed):
    raw_scores = jnp.einsum(
        "rqhd,rkhd->rhqk", query_heads, key_heads, preferred_element_type=jnp.float32
    )
    return jnp.where(allowed, raw_scores + bias[None], -1000000000.0)


def gather_rows(shard):
    return lax.all_gather(shard, ("dp", "seq"), axis=0, tiled=True)


def scatter_sum(parts):
    data_count = lax.axis_size("dp")
    piece_count = lax.axis_size("seq")
    shard_width = parts.shape[0] // (data_count * piece_count)
    split = parts.reshape(data_count, piece_count, shard_width, parts.shape[1])
    half = lax.psum_scatter(split, "dp", scatter_dimension=0, tiled=True)
    return lax.psum_scatter(half, "seq", scatter_dimension=1, tiled=True)[0, 0]


def local(
    hidden_in,
    segment_ids,
    gain_attn,
    w_query,
    w_key,
    w_value,
    w_out,
    rel_table,
    gain_ff,
    w_gate,
    w_up,
    w_down,
    cotangent,
):
    row_count, local_len, model_width = hidden_in.shape
    row_length = segment_ids.shape[1]
    bucket_count, head_count = rel_table.shape
    token_count = row_count * local_len
    data_count = lax.axis_size("dp")
    piece_count = lax.axis_size("seq")
    shard_width = model_width // (data_count * piece_count)
    first_place = lax.axis_index("seq") * local_len
    query_place = first_place + jnp.arange(local_len, dtype=jnp.int32)
    key_place = jnp.arange(row_length, dtype=jnp.int32)
    buckets = bucket_table(key_place[None, :] - query_place[:, None])
    onehot = (buckets[:, :, None] == jnp.arange(bucket_count, dtype=jnp.int32)).astype(jnp.float32)
    bias = jnp.einsum("qkb,bh->hqk", onehot, rel_table.astype(jnp.float32), precision=highest)
    query_segs = lax.dynamic_slice_in_dim(segment_ids, first_place, local_len, 1)
    same_doc = query_segs[:, :, None] == segment_ids[:, None, :]
    visible = (segment_ids[:, None, :] > 0) | (query_place[:, None] == key_place[None, :])[None]
    allowed = (same_doc & visible)[:, None]
    inner = w_query.shape[1]
    ff_width = w_gate.shape[1]
    gains = jnp.pad(jnp.stack([gain_attn, gain_ff], axis=1), ((0, 0), (0, 126)))
    attn_full = gather_rows(jnp.concatenate([w_query, w_key, w_value, w_out.T, gains], axis=1))
    feed_full = gather_rows(jnp.concatenate([w_gate, w_up, w_down.T], axis=1))
    query_full = attn_full[:, :inner]
    key_full = attn_full[:, inner : 2 * inner]
    value_full = attn_full[:, 2 * inner : 3 * inner]
    out_full = attn_full[:, 3 * inner : 4 * inner].T
    gain_one = attn_full[:, 4 * inner]
    gain_two = attn_full[:, 4 * inner + 1]
    gate_full = feed_full[:, :ff_width]
    up_full = feed_full[:, ff_width : 2 * ff_width]
    down_full = feed_full[:, 2 * ff_width :].T
    gain_first = gain_one.astype(jnp.float32)
    residual_in = hidden_in.astype(jnp.float32).reshape(token_count, model_width)
    scale_first = norm_scale(residual_in)
    normed_first = (residual_in * scale_first * gain_first).astype(jnp.bfloat16)
    queries = jnp.dot(normed_first, query_full, preferred_element_type=jnp.float32).astype(
        jnp.bfloat16
    )
    keys_local = jnp.dot(normed_first, key_full, preferred_element_type=jnp.float32).astype(
        jnp.bfloat16
    )
    values_local = jnp.dot(normed_first, value_full, preferred_element_type=jnp.float32).astype(
        jnp.bfloat16
    )
    head_size = inner // head_count
    keys_row, values_row = (
        lax.all_gather(keys_local.reshape(row_count, local_len, inner), "seq", axis=1, tiled=True),
        lax.all_gather(
            values_local.reshape(row_count, local_len, inner), "seq", axis=1, tiled=True
        ),
    )
    query_heads = queries.reshape(row_count, local_len, head_count, head_size)
    key_heads = keys_row.reshape(row_count, row_length, head_count, head_size)
    value_heads = values_row.reshape(row_count, row_length, head_count, head_size)
    logits = scores_of(query_heads, key_heads, bias, allowed)
    row_max = jnp.max(logits, axis=-1, keepdims=True)
    exp_scores = jnp.exp(logits - row_max)
    denominator = jnp.sum(exp_scores, axis=-1, keepdims=True)
    probs_low = (exp_scores / denominator).astype(jnp.bfloat16)
    log_total = row_max + jnp.log(denominator)
    mixed = (
        jnp.einsum("rhqk,rkhd->rqhd", probs_low, value_heads, preferred_element_type=jnp.float32)
        .astype(jnp.bfloat16)
        .reshape(token_count, inner)
    )
    middle = residual_in + jnp.dot(mixed, out_full, preferred_element_type=jnp.float32)
    gain_second = gain_two.astype(jnp.float32)
    scale_second = norm_scale(middle)
    normed_second = (middle * scale_second * gain_second).astype(jnp.bfloat16)
    gate_pre = jnp.dot(normed_second, gate_full, preferred_element_type=jnp.float32)
    up_pre = jnp.dot(normed_second, up_full, preferred_element_type=jnp.float32)
    activated = jax.nn.gelu(gate_pre, approximate=True)
    hidden_mid = (activated * up_pre).astype(jnp.bfloat16)
    block_out = middle + jnp.dot(hidden_mid, down_full, preferred_element_type=jnp.float32)
    gain_second = gain_two.astype(jnp.float32)
    grad_out = cotangent.reshape(token_count, model_width)
    grad_down_parts = jnp.einsum(
        "tf,td->df", hidden_mid, grad_out, preferred_element_type=jnp.float32
    ).astype(jnp.bfloat16)
    down_sum = scatter_sum(grad_down_parts)
    grad_hidden = (
        jnp.einsum("td,fd->tf", grad_out, down_full, preferred_element_type=jnp.float32)
        .astype(jnp.bfloat16)
        .astype(jnp.float32)
    )
    gelu_value, gelu_pull = jax.vjp(lambda value: jax.nn.gelu(value, approximate=True), gate_pre)
    grad_gate = gelu_pull(grad_hidden * up_pre)[0].astype(jnp.bfloat16)
    grad_up = (grad_hidden * gelu_value).astype(jnp.bfloat16)
    grad_gate_up = jnp.concatenate([grad_gate, grad_up], axis=1)
    grad_gate_up_parts = jnp.einsum(
        "td,tf->df", normed_second, grad_gate_up, preferred_element_type=jnp.float32
    ).astype(jnp.bfloat16)
    gate_up_sum = scatter_sum(grad_gate_up_parts)
    grad_normed_second = jnp.einsum(
        "tf,df->td", grad_gate, gate_full, preferred_element_type=jnp.float32
    ) + jnp.einsum("tf,df->td", grad_up, up_full, preferred_element_type=jnp.float32)
    grad_middle_norm, grad_gain_two = norm_backward(
        grad_normed_second, middle, scale_second, gain_second
    )
    grad_middle = grad_out.astype(jnp.float32) + grad_middle_norm
    grad_gate_shard = gate_up_sum[:, :ff_width].astype(jnp.float32)
    grad_up_shard = gate_up_sum[:, ff_width:].astype(jnp.float32)
    grad_down_shard = down_sum.T.astype(jnp.float32)
    grad_attended = grad_middle.astype(jnp.bfloat16)
    grad_wout_parts = jnp.einsum(
        "ti,td->di", mixed, grad_attended, preferred_element_type=jnp.float32
    ).astype(jnp.bfloat16)
    grad_mixed = jnp.einsum(
        "td,id->ti", grad_attended, out_full, preferred_element_type=jnp.float32
    ).astype(jnp.bfloat16)
    grad_heads = grad_mixed.reshape(row_count, local_len, head_count, head_size)
    logits_again = scores_of(query_heads, key_heads, bias, allowed)
    probs_again = jnp.exp(logits_again - log_total)
    probs_again_low = probs_again.astype(jnp.bfloat16)
    grad_probs = jnp.einsum(
        "rqhd,rkhd->rhqk", grad_heads, value_heads, preferred_element_type=jnp.float32
    )
    row_dot = jnp.sum(probs_again * grad_probs, axis=-1, keepdims=True)
    grad_logits = (probs_again * (grad_probs - row_dot)).astype(jnp.bfloat16)
    grad_bias = jnp.sum(grad_logits.astype(jnp.float32), axis=0)
    grad_table = jnp.einsum("qkb,hqk->bh", onehot, grad_bias, precision=highest)
    grad_queries = (
        jnp.einsum("rhqk,rkhd->rqhd", grad_logits, key_heads, preferred_element_type=jnp.float32)
        .astype(jnp.bfloat16)
        .reshape(token_count, inner)
    )
    grad_keys_row = jnp.einsum(
        "rhqk,rqhd->rkhd", grad_logits, query_heads, preferred_element_type=jnp.float32
    )
    grad_values_row = jnp.einsum(
        "rhqk,rqhd->rkhd", probs_again_low, grad_heads, preferred_element_type=jnp.float32
    )
    grad_keys_part, grad_values_part = (
        lax.psum_scatter(
            grad_keys_row.astype(jnp.bfloat16), "seq", scatter_dimension=1, tiled=True
        ).astype(jnp.float32),
        lax.psum_scatter(
            grad_values_row.astype(jnp.bfloat16), "seq", scatter_dimension=1, tiled=True
        ).astype(jnp.float32),
    )
    grad_keys = grad_keys_part.astype(jnp.bfloat16).reshape(token_count, inner)
    grad_values = grad_values_part.astype(jnp.bfloat16).reshape(token_count, inner)
    grad_projected = jnp.concatenate([grad_queries, grad_keys, grad_values], axis=1)
    grad_projection_parts = jnp.einsum(
        "td,ti->di", normed_first, grad_projected, preferred_element_type=jnp.float32
    ).astype(jnp.bfloat16)
    grad_normed_first = jnp.einsum(
        "ti,di->td", grad_queries, query_full, preferred_element_type=jnp.float32
    )
    grad_normed_first = grad_normed_first + jnp.einsum(
        "ti,di->td", grad_keys, key_full, preferred_element_type=jnp.float32
    )
    grad_normed_first = grad_normed_first + jnp.einsum(
        "ti,di->td", grad_values, value_full, preferred_element_type=jnp.float32
    )
    grad_first, grad_gain_one = norm_backward(
        grad_normed_first, residual_in, scale_first, gain_first
    )
    grad_input = grad_middle + grad_first
    device_count = data_count * piece_count
    table_size = bucket_count * head_count
    table_rows = -(-table_size // shard_width)
    table_block = jnp.pad(grad_table.reshape(-1), (0, table_rows * shard_width - table_size))
    table_block = jnp.broadcast_to(
        table_block.reshape(1, table_rows, shard_width), (device_count, table_rows, shard_width)
    )
    gain_block = jnp.stack([grad_gain_one, grad_gain_two], axis=0)
    gain_block = gain_block.reshape(2, device_count, shard_width).transpose(1, 0, 2)
    extra = jnp.concatenate([table_block, gain_block], axis=1).transpose(0, 2, 1)
    extra = extra.reshape(model_width, table_rows + 2)
    extra = jnp.pad(extra, ((0, 0), (0, -(table_rows + 2) % 128))).astype(jnp.bfloat16)
    attn_sum = scatter_sum(
        jnp.concatenate([grad_projection_parts, grad_wout_parts, extra], axis=1)
    ).astype(jnp.float32)
    grad_query_shard = attn_sum[:, :inner]
    grad_key_shard = attn_sum[:, inner : 2 * inner]
    grad_value_shard = attn_sum[:, 2 * inner : 3 * inner]
    grad_out_shard = attn_sum[:, 3 * inner : 4 * inner].T
    table_total = attn_sum[:, 4 * inner : 4 * inner + table_rows].T.reshape(-1)[:table_size]
    table_total = table_total.reshape(bucket_count, head_count)
    grad_gain_one_shard = attn_sum[:, 4 * inner + table_rows]
    grad_gain_two_shard = attn_sum[:, 4 * inner + table_rows + 1]
    return (
        block_out.reshape(row_count, local_len, model_width),
        grad_input.reshape(row_count, local_len, model_width),
        grad_gain_one_shard,
        grad_query_shard,
        grad_key_shard,
        grad_value_shard,
        grad_out_shard,
        table_total,
        grad_gain_two_shard,
        grad_gate_shard,
        grad_up_shard,
        grad_down_shard,
    )


def solution(mesh):
    in_specs = (
        P("dp", "seq", None),
        P("dp", None),
        P(("dp", "seq")),
        P(("dp", "seq"), None),
        P(("dp", "seq"), None),
        P(("dp", "seq"), None),
        P(None, ("dp", "seq")),
        P(),
        P(("dp", "seq")),
        P(("dp", "seq"), None),
        P(("dp", "seq"), None),
        P(None, ("dp", "seq")),
        P("dp", "seq", None),
    )
    out_specs = (
        P("dp", "seq", None),
        P("dp", "seq", None),
        P(("dp", "seq")),
        P(("dp", "seq"), None),
        P(("dp", "seq"), None),
        P(("dp", "seq"), None),
        P(None, ("dp", "seq")),
        P(),
        P(("dp", "seq")),
        P(("dp", "seq"), None),
        P(("dp", "seq"), None),
        P(None, ("dp", "seq")),
    )
    return jax.shard_map(local, mesh=mesh, in_specs=in_specs, out_specs=out_specs, check_vma=False)
```

```python
import functools

import jax
import jax.numpy as jnp
from jax import lax
from jax.experimental import pallas as pl
from jax.experimental.pallas import tpu as pltpu
from jax.sharding import PartitionSpec as P

epsilon = 1e-06
far_bounds = (12, 16, 23, 32, 46, 64, 91)
highest = lax.Precision.HIGHEST
mesh_ids = pl.DeviceIdType.MESH


def bucket_table(offset):
    magnitude = jnp.abs(offset)
    distant = 8 + sum(((magnitude >= bound).astype(jnp.int32) for bound in far_bounds))
    signed_part = jnp.where(offset > 0, 16, 0).astype(jnp.int32)
    return signed_part + jnp.where(magnitude < 8, magnitude, distant)


def norm_scale(hidden):
    return lax.rsqrt(jnp.mean(hidden * hidden, axis=-1, keepdims=True) + epsilon)


def norm_backward(grad_normed, hidden, scale, gain):
    weighted = grad_normed * gain
    grad_gain = jnp.sum(grad_normed * hidden * scale, axis=0)
    grad_hidden = scale * weighted - hidden * (scale * scale * scale) * jnp.mean(
        weighted * hidden, axis=-1, keepdims=True
    )
    return (grad_hidden, grad_gain)


def scores_of(query_heads, key_heads, bias, allowed):
    raw_scores = jnp.einsum(
        "rqhd,rkhd->rhqk", query_heads, key_heads, preferred_element_type=jnp.float32
    )
    return jnp.where(allowed, raw_scores + bias[None], -1000000000.0)


def gather_rows(shard):
    return lax.all_gather(shard, ("dp", "seq"), axis=0, tiled=True)


def scatter_sum(parts):
    data_count = lax.axis_size("dp")
    piece_count = lax.axis_size("seq")
    shard_width = parts.shape[0] // (data_count * piece_count)
    split = parts.reshape(data_count, piece_count, shard_width, parts.shape[1])
    half = lax.psum_scatter(split, "dp", scatter_dimension=0, tiled=True)
    return lax.psum_scatter(half, "seq", scatter_dimension=1, tiled=True)[0, 0]


def plain_sums(pairs, extra):
    found = []
    for left, rights in pairs:
        for right in rights:
            part = jnp.einsum("td,tf->df", left, right, preferred_element_type=jnp.float32)
            found.append(scatter_sum(part.astype(jnp.bfloat16)).astype(jnp.float32))
    return found, scatter_sum(extra.astype(jnp.bfloat16)).astype(jnp.float32)


def peers_of():
    dp=lax.axis_index("dp"); z=lax.axis_index("seq")
    c=lax.rem(dp,2); x=lax.rem(dp//2,2); y=dp//4
    return dp,z,c,x,y

def remote(src,dst,ss,rs,dev):
    return pltpu.make_async_remote_copy(src_ref=src,dst_ref=dst,send_sem=ss,recv_sem=rs,device_id=dev,device_id_type=mesh_ids)

part_slots=3
def rs_kernel(chunks, lt_hbm, r_hbm, out, lt, r, p, *rest):
    n=len(chunks)
    ra1=rest[0:n]; rb1=rest[n:2*n]; ra2=rest[2*n:3*n]; rb2=rest[3*n:4*n]; rz=rest[4*n:5*n]; fin=rest[5*n]
    lts,ltr,rss,rsr,ll,rl,s1,v1,s2,v2,s3,v3,s4,v4=rest[5*n+1:]
    groups=lt_hbm.shape[0]
    dp,z,c,x,y=peers_of()
    sib=(dp+1-2*c,z); dx=(dp+2-4*x,z); dy=(lax.rem(dp+4,8),z)
    zs=[lax.rem(z+k,4) for k in (1,2,3)]
    dzs=[(dp,zz) for zz in zs]
    bar=pltpu.get_barrier_semaphore()
    for d in [sib,dx,dy]+dzs: pl.semaphore_signal(bar,inc=1,device_id=d,device_id_type=mesh_ids)
    pl.semaphore_wait(bar,6)
    order=[]
    for g,off,w in chunks:
        if g not in order: order.append(g)
    ex={}
    def exch_lt(g):
        a=remote(lt_hbm.at[g],lt.at[c,g],lts.at[g],ltr.at[g],sib); a.start()
        b=pltpu.make_async_copy(lt_hbm.at[g],lt.at[c,g],ll.at[g]); b.start()
        ex[("l",g)]=(a,b)
    def exch_r(t):
        g,off,w=chunks[t]; s=pl.ds(off,w)
        a=remote(r_hbm.at[1-c,:,s],r.at[c,:,s],rss.at[t],rsr.at[t],sib); a.start()
        b=pltpu.make_async_copy(r_hbm.at[c,:,s],r.at[c,:,s],rl.at[t]); b.start()
        ex[("r",t)]=(a,b)
    seen=set()
    for t,(g,off,w) in enumerate(chunks):
        if g not in seen: seen.add(g); exch_lt(g)
        exch_r(t)
    def wait_lt(g):
        remote(lt_hbm.at[g],lt.at[1-c,g],lts.at[g],ltr.at[g],sib).wait_recv(); ex[("l",g)][1].wait()
    def wait_r(t):
        g,off,w=chunks[t]; s=pl.ds(off,w)
        remote(r_hbm.at[1-c,:,s],r.at[1-c,:,s],rss.at[t],rsr.at[t],sib).wait_recv(); ex[("r",t)][1].wait()
    got=set(); c1={}; c2={}; c3={}; c4={}
    def stage1(t):
        g,off,w=chunks[t]; b=t%part_slots
        if g not in got: got.add(g); wait_lt(g)
        wait_r(t)
        if t>=part_slots:
            for d in c1[t-part_slots]: d.wait_send()
        def body(i,_):
            rows=pl.ds(pl.multiple_of(i*192,192),192)
            acc=jnp.dot(lt[0,g,rows,:],r[0,:,off:off+w],preferred_element_type=jnp.float32)
            acc=acc+jnp.dot(lt[1,g,rows,:],r[1,:,off:off+w],preferred_element_type=jnp.float32)
            p[b,i//4,lax.rem(i//2,2),lax.rem(i,2),:,:,0:w]=acc.astype(jnp.bfloat16).reshape(4,48,w)
            return 0
        lax.fori_loop(0,8,body,0)
        a=remote(p.at[b,:,1-x,0,:,:,pl.ds(0,w)],ra1[t],s1.at[t,0],v1.at[t,0],dx)
        e=remote(p.at[b,1-y,:,1,:,:,pl.ds(0,w)],rb1[t],s1.at[t,1],v1.at[t,1],dy)
        a.start(); e.start(); c1[t]=(a,e)
    def stage2(t):
        g,off,w=chunks[t]; b=t%part_slots
        for d in c1[t]: d.wait_recv()
        def body(i,_):
            h=i//4; zz=lax.rem(i,4)
            ra1[t][h,zz]=ra1[t][h,zz]+p[b,h,x,0,zz,:,0:w]
            rb1[t][h,zz]=rb1[t][h,zz]+p[b,y,h,1,zz,:,0:w]
            return 0
        lax.fori_loop(0,8,body,0)
        a=remote(ra1[t].at[1-y],ra2[t],s2.at[t,0],v2.at[t,0],dy)
        e=remote(rb1[t].at[1-x],rb2[t],s2.at[t,1],v2.at[t,1],dx)
        a.start(); e.start(); c2[t]=(a,e)
    def stage3(t):
        for d in c2[t]: d.wait_recv()
        def body(zz,_):
            ra2[t][zz]=ra2[t][zz]+ra1[t][y,zz]
            rb2[t][zz]=rb2[t][zz]+rb1[t][x,zz]
            return 0
        lax.fori_loop(0,4,body,0)
        cs=[]
        for k in range(3):
            cs.append(remote(ra2[t].at[zs[k]],rz[t].at[k,0],s3.at[t,k,0],v3.at[t,k,0],dzs[k]))
            cs.append(remote(rb2[t].at[zs[k]],rz[t].at[k,1],s3.at[t,k,1],v3.at[t,k,1],dzs[k]))
        for d in cs: d.start()
        c3[t]=cs
    def stage4(t):
        g,off,w=chunks[t]
        for d in c3[t]: d.wait_recv()
        f0=ra2[t][z].astype(jnp.float32); f1=rb2[t][z].astype(jnp.float32)
        for k in range(3):
            f0=f0+rz[t][k,0].astype(jnp.float32); f1=f1+rz[t][k,1].astype(jnp.float32)
        fin[0,:,off:off+w]=f0; fin[1,:,off:off+w]=f1
        out[c,:,off:off+w]=fin[c,:,off:off+w]
        a=remote(fin.at[1-c,:,pl.ds(off,w)],out.at[c,:,pl.ds(off,w)],s4.at[t],v4.at[t],sib)
        a.start(); c4[t]=a
    for t in range(n+3):
        if t<n: stage1(t)
        if 0<=t-1<n: stage2(t-1)
        if 0<=t-2<n: stage3(t-2)
        if 0<=t-3<n: stage4(t-3)
    for t in range(n):
        g,off,w=chunks[t]
        remote(fin.at[1-c,:,pl.ds(off,w)],out.at[1-c,:,pl.ds(off,w)],s4.at[t],v4.at[t],sib).wait_recv()
        c4[t].wait_send()
        if t>=n-part_slots:
            for d in c1[t]: d.wait_send()
        for d in c2[t]: d.wait_send()
        for d in c3[t]: d.wait_send()
        ex[("r",t)][0].wait_send()
    for g in order: ex[("l",g)][0].wait_send()

def reduce_scatter(lt, r, chunks, cid=1):
    n=len(chunks); G=lt.shape[0]; C=r.shape[2]; wm=max(w for _,_,w in chunks)
    D=pltpu.SemaphoreType.DMA; bf=jnp.bfloat16
    V=pltpu.VMEM
    scratch=[V((2,)+lt.shape,bf),V(r.shape,bf),V((part_slots,2,2,2,4,48,wm),bf)]
    scratch+=[V((2,4,48,w),bf) for _,_,w in chunks]*1
    scratch+=[V((2,4,48,w),bf) for _,_,w in chunks]
    scratch+=[V((4,48,w),bf) for _,_,w in chunks]
    scratch+=[V((4,48,w),bf) for _,_,w in chunks]
    scratch+=[V((3,2,48,w),bf) for _,_,w in chunks]
    scratch+=[V((2,48,C),jnp.float32)]
    scratch+=[D((G,)),D((G,)),D((n,)),D((n,)),D((G,)),D((n,)),D((n,2)),D((n,2)),D((n,2)),D((n,2)),D((n,3,2)),D((n,3,2)),D((n,)),D((n,))]
    return pl.pallas_call(functools.partial(rs_kernel,chunks),
        out_shape=jax.ShapeDtypeStruct((2,48,C),jnp.float32),
        in_specs=[pl.BlockSpec(memory_space=pltpu.HBM)]*2,
        out_specs=pl.BlockSpec(memory_space=pltpu.VMEM),
        scratch_shapes=scratch,
        compiler_params=pltpu.CompilerParams(collective_id=cid,has_side_effects=True,vmem_limit_bytes=60*2**20))(lt,r)


def halves(values, width):
    spare = 2 * width - values.shape[1]
    padded = jnp.pad(values, ((0, 0), (0, spare)))
    return padded.reshape(values.shape[0], 2, width).transpose(1, 0, 2)


def join_halves(summed, start, width, total):
    piece = summed[:, :, start : start + width]
    return piece.transpose(1, 0, 2).reshape(piece.shape[1], 2 * width)[:, :total]


def kernel_sums(pairs, extra):
    low = jnp.bfloat16
    chunks = []
    pieces = []
    places = []
    start = 0
    for group, (left, rights) in enumerate(pairs):
        for right in rights:
            width = -(-right.shape[1] // 256) * 128
            step = 512 if width % 512 == 0 else 384
            assert width % step == 0
            for offset in range(0, width, step):
                chunks.append((group, start + offset, step))
            pieces.append(halves(right.astype(low), width))
            places.append((start, width, right.shape[1]))
            start += width
    upper = extra.astype(low)
    lower = (extra - upper.astype(jnp.float32)).astype(low)
    chunks.append((len(pairs), start, 128))
    token_count = pairs[0][0].shape[0]
    pieces.append(jnp.eye(token_count, dtype=low).reshape(2, 128, token_count).transpose(0, 2, 1))
    lefts = [left.astype(low).T for left, rights in pairs]
    lefts.append(jnp.concatenate([upper, lower], axis=1))
    summed = reduce_scatter(jnp.stack(lefts), jnp.concatenate(pieces, axis=2), chunks)
    found = [join_halves(summed, *place) for place in places]
    return found, summed[0, :, start:] + summed[1, :, start:]


def local(
    hidden_in,
    segment_ids,
    gain_attn,
    w_query,
    w_key,
    w_value,
    w_out,
    rel_table,
    gain_ff,
    w_gate,
    w_up,
    w_down,
    cotangent,
):
    row_count, local_len, model_width = hidden_in.shape
    row_length = segment_ids.shape[1]
    bucket_count, head_count = rel_table.shape
    token_count = row_count * local_len
    data_count = lax.axis_size("dp")
    piece_count = lax.axis_size("seq")
    shard_width = model_width // (data_count * piece_count)
    first_place = lax.axis_index("seq") * local_len
    query_place = first_place + jnp.arange(local_len, dtype=jnp.int32)
    key_place = jnp.arange(row_length, dtype=jnp.int32)
    buckets = bucket_table(key_place[None, :] - query_place[:, None])
    onehot = (buckets[:, :, None] == jnp.arange(bucket_count, dtype=jnp.int32)).astype(jnp.float32)
    bias = jnp.einsum("qkb,bh->hqk", onehot, rel_table.astype(jnp.float32), precision=highest)
    query_segs = lax.dynamic_slice_in_dim(segment_ids, first_place, local_len, 1)
    same_doc = query_segs[:, :, None] == segment_ids[:, None, :]
    visible = (segment_ids[:, None, :] > 0) | (query_place[:, None] == key_place[None, :])[None]
    allowed = (same_doc & visible)[:, None]
    inner = w_query.shape[1]
    ff_width = w_gate.shape[1]
    gains = jnp.pad(jnp.stack([gain_attn, gain_ff], axis=1), ((0, 0), (0, 126)))
    attn_full = gather_rows(jnp.concatenate([w_query, w_key, w_value, w_out.T, gains], axis=1))
    feed_full = gather_rows(jnp.concatenate([w_gate, w_up, w_down.T], axis=1))
    query_full = attn_full[:, :inner]
    key_full = attn_full[:, inner : 2 * inner]
    value_full = attn_full[:, 2 * inner : 3 * inner]
    out_full = attn_full[:, 3 * inner : 4 * inner].T
    gain_one = attn_full[:, 4 * inner]
    gain_two = attn_full[:, 4 * inner + 1]
    gate_full = feed_full[:, :ff_width]
    up_full = feed_full[:, ff_width : 2 * ff_width]
    down_full = feed_full[:, 2 * ff_width :].T
    gain_first = gain_one.astype(jnp.float32)
    residual_in = hidden_in.astype(jnp.float32).reshape(token_count, model_width)
    scale_first = norm_scale(residual_in)
    normed_first = (residual_in * scale_first * gain_first).astype(jnp.bfloat16)
    queries = jnp.dot(normed_first, query_full, preferred_element_type=jnp.float32).astype(
        jnp.bfloat16
    )
    keys_local = jnp.dot(normed_first, key_full, preferred_element_type=jnp.float32).astype(
        jnp.bfloat16
    )
    values_local = jnp.dot(normed_first, value_full, preferred_element_type=jnp.float32).astype(
        jnp.bfloat16
    )
    head_size = inner // head_count
    keys_row, values_row = (
        lax.all_gather(keys_local.reshape(row_count, local_len, inner), "seq", axis=1, tiled=True),
        lax.all_gather(
            values_local.reshape(row_count, local_len, inner), "seq", axis=1, tiled=True
        ),
    )
    query_heads = queries.reshape(row_count, local_len, head_count, head_size)
    key_heads = keys_row.reshape(row_count, row_length, head_count, head_size)
    value_heads = values_row.reshape(row_count, row_length, head_count, head_size)
    logits = scores_of(query_heads, key_heads, bias, allowed)
    row_max = jnp.max(logits, axis=-1, keepdims=True)
    exp_scores = jnp.exp(logits - row_max)
    denominator = jnp.sum(exp_scores, axis=-1, keepdims=True)
    probs_low = (exp_scores / denominator).astype(jnp.bfloat16)
    log_total = row_max + jnp.log(denominator)
    mixed = (
        jnp.einsum("rhqk,rkhd->rqhd", probs_low, value_heads, preferred_element_type=jnp.float32)
        .astype(jnp.bfloat16)
        .reshape(token_count, inner)
    )
    middle = residual_in + jnp.dot(mixed, out_full, preferred_element_type=jnp.float32)
    gain_second = gain_two.astype(jnp.float32)
    scale_second = norm_scale(middle)
    normed_second = (middle * scale_second * gain_second).astype(jnp.bfloat16)
    gate_pre = jnp.dot(normed_second, gate_full, preferred_element_type=jnp.float32)
    up_pre = jnp.dot(normed_second, up_full, preferred_element_type=jnp.float32)
    activated = jax.nn.gelu(gate_pre, approximate=True)
    hidden_mid = (activated * up_pre).astype(jnp.bfloat16)
    block_out = middle + jnp.dot(hidden_mid, down_full, preferred_element_type=jnp.float32)
    gain_second = gain_two.astype(jnp.float32)
    grad_out = cotangent.reshape(token_count, model_width)
    grad_hidden = (
        jnp.einsum("td,fd->tf", grad_out, down_full, preferred_element_type=jnp.float32)
        .astype(jnp.bfloat16)
        .astype(jnp.float32)
    )
    gelu_value, gelu_pull = jax.vjp(lambda value: jax.nn.gelu(value, approximate=True), gate_pre)
    grad_gate = gelu_pull(grad_hidden * up_pre)[0].astype(jnp.bfloat16)
    grad_up = (grad_hidden * gelu_value).astype(jnp.bfloat16)
    grad_normed_second = jnp.einsum(
        "tf,df->td", grad_gate, gate_full, preferred_element_type=jnp.float32
    ) + jnp.einsum("tf,df->td", grad_up, up_full, preferred_element_type=jnp.float32)
    grad_middle_norm, grad_gain_two = norm_backward(
        grad_normed_second, middle, scale_second, gain_second
    )
    grad_middle = grad_out.astype(jnp.float32) + grad_middle_norm
    grad_attended = grad_middle.astype(jnp.bfloat16)
    grad_mixed = jnp.einsum(
        "td,id->ti", grad_attended, out_full, preferred_element_type=jnp.float32
    ).astype(jnp.bfloat16)
    grad_heads = grad_mixed.reshape(row_count, local_len, head_count, head_size)
    logits_again = scores_of(query_heads, key_heads, bias, allowed)
    probs_again = jnp.exp(logits_again - log_total)
    probs_again_low = probs_again.astype(jnp.bfloat16)
    grad_probs = jnp.einsum(
        "rqhd,rkhd->rhqk", grad_heads, value_heads, preferred_element_type=jnp.float32
    )
    row_dot = jnp.sum(probs_again * grad_probs, axis=-1, keepdims=True)
    grad_logits = (probs_again * (grad_probs - row_dot)).astype(jnp.bfloat16)
    grad_bias = jnp.sum(grad_logits.astype(jnp.float32), axis=0)
    grad_table = jnp.einsum("qkb,hqk->bh", onehot, grad_bias, precision=highest)
    grad_queries = (
        jnp.einsum("rhqk,rkhd->rqhd", grad_logits, key_heads, preferred_element_type=jnp.float32)
        .astype(jnp.bfloat16)
        .reshape(token_count, inner)
    )
    grad_keys_row = jnp.einsum(
        "rhqk,rqhd->rkhd", grad_logits, query_heads, preferred_element_type=jnp.float32
    )
    grad_values_row = jnp.einsum(
        "rhqk,rqhd->rkhd", probs_again_low, grad_heads, preferred_element_type=jnp.float32
    )
    grad_keys_part, grad_values_part = (
        lax.psum_scatter(
            grad_keys_row.astype(jnp.bfloat16), "seq", scatter_dimension=1, tiled=True
        ).astype(jnp.float32),
        lax.psum_scatter(
            grad_values_row.astype(jnp.bfloat16), "seq", scatter_dimension=1, tiled=True
        ).astype(jnp.float32),
    )
    grad_keys = grad_keys_part.astype(jnp.bfloat16).reshape(token_count, inner)
    grad_values = grad_values_part.astype(jnp.bfloat16).reshape(token_count, inner)
    grad_normed_first = jnp.einsum(
        "ti,di->td", grad_queries, query_full, preferred_element_type=jnp.float32
    )
    grad_normed_first = grad_normed_first + jnp.einsum(
        "ti,di->td", grad_keys, key_full, preferred_element_type=jnp.float32
    )
    grad_normed_first = grad_normed_first + jnp.einsum(
        "ti,di->td", grad_values, value_full, preferred_element_type=jnp.float32
    )
    grad_first, grad_gain_one = norm_backward(
        grad_normed_first, residual_in, scale_first, gain_first
    )
    grad_input = grad_middle + grad_first
    device_count = data_count * piece_count
    table_size = bucket_count * head_count
    table_rows = -(-table_size // shard_width)
    table_block = jnp.pad(grad_table.reshape(-1), (0, table_rows * shard_width - table_size))
    table_block = jnp.broadcast_to(
        table_block.reshape(1, table_rows, shard_width), (device_count, table_rows, shard_width)
    )
    gain_block = jnp.stack([grad_gain_one, grad_gain_two], axis=0)
    gain_block = gain_block.reshape(2, device_count, shard_width).transpose(1, 0, 2)
    extra = jnp.concatenate([table_block, gain_block], axis=1).transpose(0, 2, 1)
    extra = extra.reshape(model_width, table_rows + 2)
    extra = jnp.pad(extra, ((0, 0), (0, -(table_rows + 2) % 128)))
    pairs = (
        (normed_second, (grad_gate, grad_up)),
        (grad_out, (hidden_mid,)),
        (grad_attended, (mixed,)),
        (normed_first, (grad_queries, grad_keys, grad_values)),
    )
    sums = kernel_sums if data_count == 8 and piece_count == 4 else plain_sums
    (gate_sum, up_sum, down_sum, out_sum, query_sum, key_sum, value_sum), extra_sum = sums(
        pairs, extra
    )
    table_total = extra_sum[:, :table_rows].T.reshape(-1)[:table_size]
    table_total = table_total.reshape(bucket_count, head_count)
    grad_gain_one_shard = extra_sum[:, table_rows]
    grad_gain_two_shard = extra_sum[:, table_rows + 1]
    return (
        block_out.reshape(row_count, local_len, model_width),
        grad_input.reshape(row_count, local_len, model_width),
        grad_gain_one_shard,
        query_sum,
        key_sum,
        value_sum,
        out_sum.T,
        table_total,
        grad_gain_two_shard,
        gate_sum,
        up_sum,
        down_sum.T,
    )


def solution(mesh):
    in_specs = (
        P("dp", "seq", None),
        P("dp", None),
        P(("dp", "seq")),
        P(("dp", "seq"), None),
        P(("dp", "seq"), None),
        P(("dp", "seq"), None),
        P(None, ("dp", "seq")),
        P(),
        P(("dp", "seq")),
        P(("dp", "seq"), None),
        P(("dp", "seq"), None),
        P(None, ("dp", "seq")),
        P("dp", "seq", None),
    )
    out_specs = (
        P("dp", "seq", None),
        P("dp", "seq", None),
        P(("dp", "seq")),
        P(("dp", "seq"), None),
        P(("dp", "seq"), None),
        P(("dp", "seq"), None),
        P(None, ("dp", "seq")),
        P(),
        P(("dp", "seq")),
        P(("dp", "seq"), None),
        P(("dp", "seq"), None),
        P(None, ("dp", "seq")),
    )
    return jax.shard_map(local, mesh=mesh, in_specs=in_specs, out_specs=out_specs, check_vma=False)
```

```python
import functools

import jax
import jax.numpy as jnp
from jax import lax
from jax.experimental import pallas as pl
from jax.experimental.pallas import tpu as pltpu
from jax.sharding import PartitionSpec as P

epsilon = 1e-06
far_bounds = (12, 16, 23, 32, 46, 64, 91)
highest = lax.Precision.HIGHEST
mesh_ids = pl.DeviceIdType.MESH


def bucket_table(offset):
    magnitude = jnp.abs(offset)
    distant = 8 + sum(((magnitude >= bound).astype(jnp.int32) for bound in far_bounds))
    signed_part = jnp.where(offset > 0, 16, 0).astype(jnp.int32)
    return signed_part + jnp.where(magnitude < 8, magnitude, distant)


def norm_scale(hidden):
    return lax.rsqrt(jnp.mean(hidden * hidden, axis=-1, keepdims=True) + epsilon)


def norm_backward(grad_normed, hidden, scale, gain):
    weighted = grad_normed * gain
    grad_gain = jnp.sum(grad_normed * hidden * scale, axis=0)
    grad_hidden = scale * weighted - hidden * (scale * scale * scale) * jnp.mean(
        weighted * hidden, axis=-1, keepdims=True
    )
    return (grad_hidden, grad_gain)


def scores_of(query_heads, key_heads, bias, allowed):
    raw_scores = jnp.einsum(
        "rqhd,rkhd->rhqk", query_heads, key_heads, preferred_element_type=jnp.float32
    )
    return jnp.where(allowed, raw_scores + bias[None], -1000000000.0)


def gather_rows(shard):
    return lax.all_gather(shard, ("dp", "seq"), axis=0, tiled=True)


def scatter_sum(parts):
    data_count = lax.axis_size("dp")
    piece_count = lax.axis_size("seq")
    shard_width = parts.shape[0] // (data_count * piece_count)
    split = parts.reshape(data_count, piece_count, shard_width, parts.shape[1])
    half = lax.psum_scatter(split, "dp", scatter_dimension=0, tiled=True)
    return lax.psum_scatter(half, "seq", scatter_dimension=1, tiled=True)[0, 0]


def plain_sums(pairs, extra):
    found = []
    for left, rights in pairs:
        for right in rights:
            part = jnp.einsum("td,tf->df", left, right, preferred_element_type=jnp.float32)
            found.append(scatter_sum(part.astype(jnp.bfloat16)).astype(jnp.float32))
    return found, scatter_sum(extra.astype(jnp.bfloat16)).astype(jnp.float32)


def plain_local(
    hidden_in,
    segment_ids,
    gain_attn,
    w_query,
    w_key,
    w_value,
    w_out,
    rel_table,
    gain_ff,
    w_gate,
    w_up,
    w_down,
    cotangent,
):
    row_count, local_len, model_width = hidden_in.shape
    row_length = segment_ids.shape[1]
    bucket_count, head_count = rel_table.shape
    token_count = row_count * local_len
    data_count = lax.axis_size("dp")
    piece_count = lax.axis_size("seq")
    shard_width = model_width // (data_count * piece_count)
    first_place = lax.axis_index("seq") * local_len
    query_place = first_place + jnp.arange(local_len, dtype=jnp.int32)
    key_place = jnp.arange(row_length, dtype=jnp.int32)
    buckets = bucket_table(key_place[None, :] - query_place[:, None])
    onehot = (buckets[:, :, None] == jnp.arange(bucket_count, dtype=jnp.int32)).astype(jnp.float32)
    bias = jnp.einsum("qkb,bh->hqk", onehot, rel_table.astype(jnp.float32), precision=highest)
    query_segs = lax.dynamic_slice_in_dim(segment_ids, first_place, local_len, 1)
    same_doc = query_segs[:, :, None] == segment_ids[:, None, :]
    visible = (segment_ids[:, None, :] > 0) | (query_place[:, None] == key_place[None, :])[None]
    allowed = (same_doc & visible)[:, None]
    inner = w_query.shape[1]
    ff_width = w_gate.shape[1]
    gains = jnp.pad(jnp.stack([gain_attn, gain_ff], axis=1), ((0, 0), (0, 126)))
    attn_full = gather_rows(jnp.concatenate([w_query, w_key, w_value, w_out.T, gains], axis=1))
    feed_full = gather_rows(jnp.concatenate([w_gate, w_up, w_down.T], axis=1))
    query_full = attn_full[:, :inner]
    key_full = attn_full[:, inner : 2 * inner]
    value_full = attn_full[:, 2 * inner : 3 * inner]
    out_full = attn_full[:, 3 * inner : 4 * inner].T
    gain_one = attn_full[:, 4 * inner]
    gain_two = attn_full[:, 4 * inner + 1]
    gate_full = feed_full[:, :ff_width]
    up_full = feed_full[:, ff_width : 2 * ff_width]
    down_full = feed_full[:, 2 * ff_width :].T
    gain_first = gain_one.astype(jnp.float32)
    residual_in = hidden_in.astype(jnp.float32).reshape(token_count, model_width)
    scale_first = norm_scale(residual_in)
    normed_first = (residual_in * scale_first * gain_first).astype(jnp.bfloat16)
    queries = jnp.dot(normed_first, query_full, preferred_element_type=jnp.float32).astype(
        jnp.bfloat16
    )
    keys_local = jnp.dot(normed_first, key_full, preferred_element_type=jnp.float32).astype(
        jnp.bfloat16
    )
    values_local = jnp.dot(normed_first, value_full, preferred_element_type=jnp.float32).astype(
        jnp.bfloat16
    )
    head_size = inner // head_count
    keys_row, values_row = (
        lax.all_gather(keys_local.reshape(row_count, local_len, inner), "seq", axis=1, tiled=True),
        lax.all_gather(
            values_local.reshape(row_count, local_len, inner), "seq", axis=1, tiled=True
        ),
    )
    query_heads = queries.reshape(row_count, local_len, head_count, head_size)
    key_heads = keys_row.reshape(row_count, row_length, head_count, head_size)
    value_heads = values_row.reshape(row_count, row_length, head_count, head_size)
    logits = scores_of(query_heads, key_heads, bias, allowed)
    row_max = jnp.max(logits, axis=-1, keepdims=True)
    exp_scores = jnp.exp(logits - row_max)
    denominator = jnp.sum(exp_scores, axis=-1, keepdims=True)
    probs_low = (exp_scores / denominator).astype(jnp.bfloat16)
    log_total = row_max + jnp.log(denominator)
    mixed = (
        jnp.einsum("rhqk,rkhd->rqhd", probs_low, value_heads, preferred_element_type=jnp.float32)
        .astype(jnp.bfloat16)
        .reshape(token_count, inner)
    )
    middle = residual_in + jnp.dot(mixed, out_full, preferred_element_type=jnp.float32)
    gain_second = gain_two.astype(jnp.float32)
    scale_second = norm_scale(middle)
    normed_second = (middle * scale_second * gain_second).astype(jnp.bfloat16)
    gate_pre = jnp.dot(normed_second, gate_full, preferred_element_type=jnp.float32)
    up_pre = jnp.dot(normed_second, up_full, preferred_element_type=jnp.float32)
    activated = jax.nn.gelu(gate_pre, approximate=True)
    hidden_mid = (activated * up_pre).astype(jnp.bfloat16)
    block_out = middle + jnp.dot(hidden_mid, down_full, preferred_element_type=jnp.float32)
    gain_second = gain_two.astype(jnp.float32)
    grad_out = cotangent.reshape(token_count, model_width)
    grad_hidden = (
        jnp.einsum("td,fd->tf", grad_out, down_full, preferred_element_type=jnp.float32)
        .astype(jnp.bfloat16)
        .astype(jnp.float32)
    )
    gelu_value, gelu_pull = jax.vjp(lambda value: jax.nn.gelu(value, approximate=True), gate_pre)
    grad_gate = gelu_pull(grad_hidden * up_pre)[0].astype(jnp.bfloat16)
    grad_up = (grad_hidden * gelu_value).astype(jnp.bfloat16)
    grad_normed_second = jnp.einsum(
        "tf,df->td", grad_gate, gate_full, preferred_element_type=jnp.float32
    ) + jnp.einsum("tf,df->td", grad_up, up_full, preferred_element_type=jnp.float32)
    grad_middle_norm, grad_gain_two = norm_backward(
        grad_normed_second, middle, scale_second, gain_second
    )
    grad_middle = grad_out.astype(jnp.float32) + grad_middle_norm
    grad_attended = grad_middle.astype(jnp.bfloat16)
    grad_mixed = jnp.einsum(
        "td,id->ti", grad_attended, out_full, preferred_element_type=jnp.float32
    ).astype(jnp.bfloat16)
    grad_heads = grad_mixed.reshape(row_count, local_len, head_count, head_size)
    logits_again = scores_of(query_heads, key_heads, bias, allowed)
    probs_again = jnp.exp(logits_again - log_total)
    probs_again_low = probs_again.astype(jnp.bfloat16)
    grad_probs = jnp.einsum(
        "rqhd,rkhd->rhqk", grad_heads, value_heads, preferred_element_type=jnp.float32
    )
    row_dot = jnp.sum(probs_again * grad_probs, axis=-1, keepdims=True)
    grad_logits = (probs_again * (grad_probs - row_dot)).astype(jnp.bfloat16)
    grad_bias = jnp.sum(grad_logits.astype(jnp.float32), axis=0)
    grad_table = jnp.einsum("qkb,hqk->bh", onehot, grad_bias, precision=highest)
    grad_queries = (
        jnp.einsum("rhqk,rkhd->rqhd", grad_logits, key_heads, preferred_element_type=jnp.float32)
        .astype(jnp.bfloat16)
        .reshape(token_count, inner)
    )
    grad_keys_row = jnp.einsum(
        "rhqk,rqhd->rkhd", grad_logits, query_heads, preferred_element_type=jnp.float32
    )
    grad_values_row = jnp.einsum(
        "rhqk,rqhd->rkhd", probs_again_low, grad_heads, preferred_element_type=jnp.float32
    )
    grad_keys_part, grad_values_part = (
        lax.psum_scatter(
            grad_keys_row.astype(jnp.bfloat16), "seq", scatter_dimension=1, tiled=True
        ).astype(jnp.float32),
        lax.psum_scatter(
            grad_values_row.astype(jnp.bfloat16), "seq", scatter_dimension=1, tiled=True
        ).astype(jnp.float32),
    )
    grad_keys = grad_keys_part.astype(jnp.bfloat16).reshape(token_count, inner)
    grad_values = grad_values_part.astype(jnp.bfloat16).reshape(token_count, inner)
    grad_normed_first = jnp.einsum(
        "ti,di->td", grad_queries, query_full, preferred_element_type=jnp.float32
    )
    grad_normed_first = grad_normed_first + jnp.einsum(
        "ti,di->td", grad_keys, key_full, preferred_element_type=jnp.float32
    )
    grad_normed_first = grad_normed_first + jnp.einsum(
        "ti,di->td", grad_values, value_full, preferred_element_type=jnp.float32
    )
    grad_first, grad_gain_one = norm_backward(
        grad_normed_first, residual_in, scale_first, gain_first
    )
    grad_input = grad_middle + grad_first
    device_count = data_count * piece_count
    table_size = bucket_count * head_count
    table_rows = -(-table_size // shard_width)
    table_block = jnp.pad(grad_table.reshape(-1), (0, table_rows * shard_width - table_size))
    table_block = jnp.broadcast_to(
        table_block.reshape(1, table_rows, shard_width), (device_count, table_rows, shard_width)
    )
    gain_block = jnp.stack([grad_gain_one, grad_gain_two], axis=0)
    gain_block = gain_block.reshape(2, device_count, shard_width).transpose(1, 0, 2)
    extra = jnp.concatenate([table_block, gain_block], axis=1).transpose(0, 2, 1)
    extra = extra.reshape(model_width, table_rows + 2)
    extra = jnp.pad(extra, ((0, 0), (0, -(table_rows + 2) % 128)))
    pairs = (
        (normed_second, (grad_gate, grad_up)),
        (grad_out, (hidden_mid,)),
        (grad_attended, (mixed,)),
        (normed_first, (grad_queries, grad_keys, grad_values)),
    )
    (gate_sum, up_sum, down_sum, out_sum, query_sum, key_sum, value_sum), extra_sum = plain_sums(
        pairs, extra
    )
    table_total = extra_sum[:, :table_rows].T.reshape(-1)[:table_size]
    table_total = table_total.reshape(bucket_count, head_count)
    grad_gain_one_shard = extra_sum[:, table_rows]
    grad_gain_two_shard = extra_sum[:, table_rows + 1]
    return (
        block_out.reshape(row_count, local_len, model_width),
        grad_input.reshape(row_count, local_len, model_width),
        grad_gain_one_shard,
        query_sum,
        key_sum,
        value_sum,
        out_sum.T,
        table_total,
        grad_gain_two_shard,
        gate_sum,
        up_sum,
        down_sum.T,
    )


gelu_c=0.7978845608028654

def peers_of():
    dp=lax.axis_index("dp"); z=lax.axis_index("seq")
    c=lax.rem(dp,2); x=lax.rem(dp//2,2); y=dp//4
    return dp,z,c,x,y

def remote(src,dst,ss,rs,dev):
    return pltpu.make_async_remote_copy(src_ref=src,dst_ref=dst,send_sem=ss,recv_sem=rs,device_id=dev,device_id_type=mesh_ids)

def dot(a,b):
    return jnp.dot(a,b,preferred_element_type=jnp.float32)

def dot_nt(a,b):
    return lax.dot_general(a,b,(((1,),(1,)),((),())),preferred_element_type=jnp.float32)

def lanes(shape):
    return lax.broadcasted_iota(jnp.int32,shape,len(shape)-1)

def greet(devices):
    bar=pltpu.get_barrier_semaphore()
    for d in devices: pl.semaphore_signal(bar,inc=1,device_id=d,device_id_type=mesh_ids)
    pl.semaphore_wait(bar,len(devices))

low=jnp.bfloat16
f32=jnp.float32

def forward_kernel(ff_steps, wp, hid, cot, segr, segc, base,
                   w, lt_o, hdg_o, q_o, kk_o, vv_o, mx_o, lse_o, gmid_o, bo_o, ggf_o, segr_o, segc_o,
                   hrow, cotv, sr, sc, wa, wf, qq, kk, vv, mx, lse, bias, part, mid, n2, hd, yy, lt, gs, r1, r2, r3,
                   s0s, s0r, l0, s1s, s1r, s2s, s2r, s3s, s3r, hs, hr, xs, xr, ll, lo):
    width=wp.shape[2]
    cols=[(0,768),(768,896)]+[(1664+512*i,512) for i in range(3*ff_steps)]
    n=len(cols)
    dp,z,c,x,y=peers_of()
    q=dp//2; qx=2*y+1-x; qy=lax.rem(q+2,4); qd=3-q
    sib=(dp+1-2*c,z); dx=(2*qx+c,z); dy=(2*qy+c,z); dxy=(dx,dy)
    zs=[lax.rem(z+k,4) for k in (1,2,3)]; zf=[lax.rem(z+4-k,4) for k in (1,2,3)]
    dz=[(dp,zz) for zz in zs]
    greet([sib,dx,dy]+dz)
    def cs(t): return pl.ds(cols[t][0],cols[t][1])
    def s0(t,recv=False):
        return remote(wp.at[1-c,:,cs(t)], w.at[(dp+1-2*c) if recv else dp,z,:,cs(t)], s0s.at[t], s0r.at[t], sib)
    def keep(t): return pltpu.make_async_copy(wp.at[c,:,cs(t)], w.at[dp,z,:,cs(t)], l0.at[t])
    def s1(t,k,recv=False):
        r=w.at[pl.ds(2*q,2), zf[k] if recv else z, :, cs(t)]
        return remote(r,r,s1s.at[t,k],s1r.at[t,k],dz[k])
    def s2(t,a,recv=False):
        r=w.at[pl.ds(2*((qx,qy)[a] if recv else q),2),:,:,cs(t)]
        return remote(r,r,s2s.at[t,a],s2r.at[t,a],dxy[a])
    def s3(t,a,recv=False):
        r=w.at[2*(qd if recv else (qy,qx)[a])+a,:,:,cs(t)]
        return remote(r,r,s3s.at[t,a],s3r.at[t,a],dxy[a])
    def hz(k,recv=False): return remote(hid,hrow.at[c,zf[k] if recv else z],hs.at[k],hr.at[k],dz[k])
    done=set()
    def once(*k):
        if k in done: return False
        done.add(k); return True
    def start1(t):
        if t<n and once(1,t):
            keep(t).wait(); s0(t,True).wait_recv()
            for k in range(3): s1(t,k).start()
    def start2(t):
        if t<n and once(2,t):
            for k in range(3): s1(t,k,True).wait_recv()
            for a in range(2): s2(t,a).start()
    def start3(t):
        if 0<=t<n and once(3,t):
            for a in range(2): s2(t,a,True).wait_recv()
            for a in range(2): s3(t,a).start()
    def finish(t):
        if 0<=t<n and once(4,t):
            for a in range(2): s3(t,a,True).wait_recv()
    def advance(t):
        start1(t+2); start2(t); start3(t-1); finish(t-2)
    keep_h=pltpu.make_async_copy(hid,hrow.at[c,z],ll.at[0]); keep_h.start()
    keep_c=pltpu.make_async_copy(cot,cotv.at[c],ll.at[1]); keep_c.start()
    keep_r=pltpu.make_async_copy(segr,sr.at[c],ll.at[2]); keep_r.start()
    keep_s=pltpu.make_async_copy(segc,sc.at[c],ll.at[3]); keep_s.start()
    for t in range(2): s0(t).start(); keep(t).start()
    give_c=remote(cot,cotv.at[c],xs.at[0],xr.at[0],sib); give_c.start()
    give_r=remote(segr,sr.at[c],xs.at[1],xr.at[1],sib); give_r.start()
    give_s=remote(segc,sc.at[c],xs.at[2],xr.at[2],sib); give_s.start()
    for t in range(2,n): s0(t).start(); keep(t).start()
    start1(0); start1(1)
    for k in range(3): hz(k).start()
    advance(0); advance(1)
    start3(1); finish(0); finish(1)
    load_a=pltpu.make_async_copy(w.at[:,:,:,pl.ds(0,1664)],wa,ll.at[4]); load_a.start()
    keep_h.wait(); keep_c.wait(); keep_r.wait(); keep_s.wait()
    remote(segr,sr.at[1-c],xs.at[1],xr.at[1],sib).wait_recv()
    remote(segc,sc.at[1-c],xs.at[2],xr.at[2],sib).wait_recv()
    remote(cot,cotv.at[1-c],xs.at[0],xr.at[0],sib).wait_recv()
    load_a.wait()
    def wcol(a,b): return wa[:,:,:,a:b].reshape(1536,b-a)
    pick=(lanes((8,128))==lax.broadcasted_iota(jnp.int32,(8,128),0)).astype(low)
    gs[...]=dot_nt(pick,wcol(1536,1664))
    def transpose_cot(i,_):
        lt[2,:,pl.ds(pl.multiple_of(i*128,128),128)]=cotv[i//2,pl.ds(pl.multiple_of(lax.rem(i,2)*128,128),128),:].astype(f32).T.astype(low)
        return 0
    lax.fori_loop(0,4,transpose_cot,0)
    for k in range(3): hz(k,True).wait_recv()
    give_h=remote(hrow.at[c],hrow.at[c],xs.at[3],xr.at[3],sib); give_h.start()
    def normed(v,row):
        s=lax.rsqrt(jnp.mean(v*v,axis=-1,keepdims=True)+epsilon)
        return v*s*gs[row:row+1,:]
    def keys_of(r):
        def body(i,_):
            a=pl.ds(pl.multiple_of(lax.rem(i,2)*128,128),128)
            v=normed(hrow[r,i//2,a,:].astype(f32),0).astype(low)
            d=pl.ds(pl.multiple_of(i*128,128),128)
            kk[r,d,:]=dot(v,wcol(384,768)).astype(low)
            vv[r,d,:]=dot(v,wcol(768,1152)).astype(low)
            return 0
        lax.fori_loop(0,8,body,0)
    keys_of(c)
    remote(hrow.at[1-c],hrow.at[1-c],xs.at[3],xr.at[3],sib).wait_recv()
    advance(2)
    keys_of(1-c)
    def queries(i,_):
        a=pl.ds(pl.multiple_of(lax.rem(i,2)*128,128),128)
        v=normed(hrow[i//2,z,a,:].astype(f32),0)
        d=pl.ds(pl.multiple_of(i*128,128),128)
        qq[d,:]=dot(v.astype(low),wcol(0,384)).astype(low)
        lt[0,:,d]=v.T.astype(low)
        return 0
    lax.fori_loop(0,4,queries,0)
    advance(3)
    for h in range(6):
        pair=pl.ds(128*(h//2),128); odd=h%2
        bias[...]=pltpu.roll(jnp.broadcast_to(base[h:h+1,:],(256,1280)),1024,1,stride=1,stride_axis=0)
        def attend(i,_):
            r=i//2; d=pl.ds(pl.multiple_of(i*128,128),128)
            a=pl.ds(pl.multiple_of(lax.rem(i,2)*128,128),128)
            mine=(lanes((128,128))>=64) if odd else (lanes((128,128))<64)
            qh=jnp.where(mine,qq[d,pair].astype(f32),0.0).astype(low)
            s=dot_nt(qh,kk[r,:,pair])+bias[a,0:1024]
            s=jnp.where(sc[r,a,0:1]==sr[r,0:1,:],s,-1000000000.0)
            m=jnp.max(s,axis=-1,keepdims=True)
            e=jnp.exp(s-m)
            l=jnp.sum(e,axis=-1,keepdims=True)
            p=(e*(1.0/l)).astype(low)
            o=dot(p,vv[r,:,pair])
            if odd: o=jnp.where(mine,o,mx[d,pair].astype(f32))
            mx[d,pair]=o.astype(low)
            lse[r,a,:]=jnp.where(lanes((128,128))==h,m+jnp.log(l),lse[r,a,:]) if h else jnp.broadcast_to(m+jnp.log(l),(128,128))
            return 0
        lax.fori_loop(0,4,attend,0)
        if h in (1,3): advance(4+h//2)
    def project(i,_):
        part[i//2,pl.ds(pl.multiple_of(lax.rem(i,2)*128,128),128),:]=dot_nt(mx[pl.ds(pl.multiple_of(i*128,128),128),:],wcol(1152,1536))
        return 0
    lax.fori_loop(0,4,project,0)
    give_p=remote(part,r1,xs.at[4],xr.at[4],sib); give_p.start()
    outs=[pltpu.make_async_copy(a,b,lo.at[i]) for i,(a,b) in enumerate(((qq,q_o),(kk,kk_o),(vv,vv_o),(mx,mx_o),(lse,lse_o),(sr,segr_o),(sc,segc_o)))]
    for o in outs: o.start()
    give_p.wait_recv()
    def middle(i,_):
        a=pl.ds(pl.multiple_of(lax.rem(i,2)*128,128),128); r=i//2
        d=pl.ds(pl.multiple_of(i*128,128),128)
        v=hrow[r,z,a,:].astype(f32)+(part[r,a,:]+r1[r,a,:])
        mid[r,a,:]=v
        v=normed(v,1)
        n2[d,:]=v.astype(low)
        lt[1,:,d]=v.T.astype(low)
        return 0
    lax.fori_loop(0,4,middle,0)
    give_p.wait_send()
    give_lt=pltpu.make_async_copy(lt,lt_o,ll.at[5]); give_lt.start()
    advance(6)
    hout=[]
    for j in range(ff_steps):
        if j:
            for t in range(4+3*j,7+3*j): advance(t)
        loads=[pltpu.make_async_copy(w.at[:,:,:,cs(2+3*j+i)],wf.at[i],ll.at[6+i]) for i in range(3)]
        for l in loads: l.start()
        b=j%2
        if j>=2: hout[j-2].wait()
        for l in loads: l.wait()
        def feed(i,_):
            d=pl.ds(pl.multiple_of(i*256,256),256)
            v=n2[d,:]
            wg=wf[0].reshape(1536,512); wu=wf[1].reshape(1536,512); wd=wf[2].reshape(1536,512)
            gate=dot(v,wg); up=dot(v,wu)
            gh=dot(cotv[i],wd).astype(low).astype(f32)
            u2=gate*gate
            th=jnp.tanh(gelu_c*(gate+0.044715*(gate*u2)))
            act=0.5*gate*(1.0+th)
            slope=0.5*(1.0+th)+0.5*gate*(1.0-th*th)*(gelu_c*(1.0+3*0.044715*u2))
            hm=(act*up).astype(low); dg=(gh*up*slope).astype(low); du=(gh*act).astype(low)
            hd[b,0,d,:]=hm; hd[b,1,d,:]=dg; hd[b,2,d,:]=du
            yp=dot_nt(hm,wd); gp=dot_nt(dg,wg)+dot_nt(du,wu)
            if j: yp=yp+yy[i]; gp=gp+part[i]
            yy[i]=yp; part[i]=gp
            return 0
        lax.fori_loop(0,2,feed,0)
        o=pltpu.make_async_copy(hd.at[b],hdg_o.at[:,:,pl.ds(512*j,512)],lo.at[7+b]); o.start(); hout.append(o)
    give_g=remote(part,r2,xs.at[5],xr.at[5],sib); give_g.start()
    give_y=remote(yy.at[1-c],r3,xs.at[6],xr.at[6],sib); give_y.start()
    give_g.wait_recv()
    give_g.wait_send()
    def gradient(i,acc):
        a=pl.ds(pl.multiple_of(lax.rem(i,2)*128,128),128); r=i//2
        v=mid[r,a,:]; gn=part[r,a,:]+r2[r,a,:]
        s=lax.rsqrt(jnp.mean(v*v,axis=-1,keepdims=True)+epsilon)
        wg=gn*gs[1:2,:]
        part[r,a,:]=cotv[r,a,:].astype(f32)+(s*wg-v*(s*s*s)*jnp.mean(wg*v,axis=-1,keepdims=True))
        return acc+jnp.where(r==c,1.0,0.0)*jnp.sum(gn*v*s,axis=0,keepdims=True)
    acc=lax.fori_loop(0,4,gradient,jnp.zeros((1,1536),f32))
    ggf_o[0:8,:]=jnp.broadcast_to(acc,(8,1536))
    ggf_o[8:16,:]=gs[...]
    give_m=pltpu.make_async_copy(part,gmid_o,ll.at[9]); give_m.start()
    give_y.wait_recv(); give_y.wait_send()
    def final(i,_):
        a=pl.ds(pl.multiple_of(i*128,128),128)
        yy[c,a,:]=mid[c,a,:]+(yy[c,a,:]+r3[a,:])
        return 0
    lax.fori_loop(0,2,final,0)
    give_b=pltpu.make_async_copy(yy.at[c],bo_o,ll.at[10]); give_b.start()
    for o in outs+hout[-2:]: o.wait()
    give_lt.wait(); give_m.wait(); give_b.wait()
    give_c.wait_send(); give_r.wait_send(); give_s.wait_send(); give_h.wait_send()
    for k in range(3): hz(k).wait_send()
    for t in range(n):
        s0(t).wait_send()
        for k in range(3): s1(t,k).wait_send()
        for a in range(2): s2(t,a).wait_send(); s3(t,a).wait_send()

def forward_call(wp, hid, cot, segr, segc, base, ff_steps, cid=0):
    n=2+3*ff_steps
    S=jax.ShapeDtypeStruct; V=pltpu.VMEM; D=pltpu.SemaphoreType.DMA
    fw=512*ff_steps
    hbm=pl.BlockSpec(memory_space=pltpu.HBM); vm=pl.BlockSpec(memory_space=pltpu.VMEM)
    outs=(S((8,4,48,wp.shape[2]),low),S((3,1536,512),low),S((3,512,fw),low),S((512,384),low),S((2,1024,384),low),S((2,1024,384),low),
          S((512,384),low),S((2,256,128),f32),S((2,256,1536),f32),S((256,1536),f32),S((16,1536),f32),S((2,8,1024),f32),S((2,256,128),f32))
    ospec=[hbm]*13; ospec[10]=vm
    scratch=[V((2,4,256,1536),low),V((2,256,1536),low),V((2,8,1024),f32),V((2,256,128),f32),V((8,4,48,1664),low),V((3,8,4,48,512),low),
             V((512,384),low),V((2,1024,384),low),V((2,1024,384),low),V((512,384),low),V((2,256,128),f32),V((256,1280),f32),
             V((2,256,1536),f32),V((2,256,1536),f32),V((512,1536),low),V((2,3,512,512),low),V((2,256,1536),f32),V((3,1536,512),low),V((8,1536),f32),
             V((2,256,1536),f32),V((2,256,1536),f32),V((256,1536),f32),
             D((n,)),D((n,)),D((n,)),D((n,3)),D((n,3)),D((n,2)),D((n,2)),D((n,2)),D((n,2)),D((3,)),D((3,)),D((7,)),D((7,)),D((11,)),D((9,))]
    return pl.pallas_call(functools.partial(forward_kernel,ff_steps),out_shape=outs,
        in_specs=[hbm]*5+[vm],out_specs=tuple(ospec),scratch_shapes=scratch,
        compiler_params=pltpu.CompilerParams(collective_id=cid,has_side_effects=True,vmem_limit_bytes=62*2**20))(wp,hid,cot,segr,segc,base)

def dot_tn(a,b):
    return lax.dot_general(a,b,(((0,),(0,)),((),())),preferred_element_type=jnp.float32)

part_slots=2
sum_slots=3
def backward_kernel(chunks, ff_steps, w, lt_h, hdg, q_h, kk_h, vv_h, mx_h, lse_h, gmid, segr_h, segc_h, hid_h, base, rows, spots, tile,
                    out, gin_o, *rest):
    n=len(chunks)
    ra1=rest[0:n]; rb1=rest[n:2*n]; ra2=rest[2*n:3*n]; rb2=rest[3*n:4*n]; rz=rest[4*n:5*n]
    (fin,p,lt,gat,rbuf,wa,qq,kk,vv,mx,gm,lse,sr,sc,bias,dbias,dq,acc,dkv,rkv,dk,dv,part,r3,gin,hid,dtab,ext,
     ll,lr,lo,s1,v1,s2,v2,s3,v3,s4,v4,ks,kr,xs,xr)=rest[5*n:]
    dp,z,c,x,y=peers_of()
    sib=(dp+1-2*c,z); dx=(dp+2-4*x,z); dy=(lax.rem(dp+4,8),z)
    zs=[lax.rem(z+k,4) for k in (1,2,3)]; dz=[(dp,zz) for zz in zs]
    loads=[pltpu.make_async_copy(a,b,ll.at[i]) for i,(a,b) in enumerate((
        (lt_h.at[pl.ds(1,2)],lt),(gmid,part),(w.at[:,:,:,pl.ds(1152,384)],wa.at[:,:,:,pl.ds(0,384)]),(q_h,qq),(kk_h,kk),(vv_h,vv),(mx_h,mx),(lse_h,lse),(segr_h,sr),(segc_h,sc),(hid_h,hid),(gmid.at[c],gin)))]
    for l in loads: l.start()
    slots=rbuf.shape[0]
    def fetch(t):
        kind,i,j=chunks[t][3]
        return pltpu.make_async_copy(hdg.at[i,:,pl.ds(512*j,512)],rbuf.at[t%slots],lr.at[t])
    feeds=[t for t in range(n) if chunks[t][3][0]=="feed"]
    for t in feeds[:slots]: fetch(t).start()
    greet([sib,dx,dy]+dz)
    load_n=pltpu.make_async_copy(lt_h.at[0],lt.at[1],ll.at[14])
    c1={}; c2={}; c3={}; c4={}; done=set()
    def once(*k):
        if k in done: return False
        done.add(k); return True
    def stage1(t):
        left,off,wd,src=chunks[t]; b=t%part_slots
        if t>=part_slots:
            for d in c1[t-part_slots]: d.wait_send()
        if src[0]=="feed":
            fetch(t).wait()
            right=lambda: rbuf[t%slots]
        else:
            right=(lambda: mx[...],lambda: dq[...],lambda: dk[...],lambda: dv[...],None)[src[1]]
        if src==("ref",1,0): load_n.wait()
        if right is None:
            p[b,:,:,:,:,:,0:wd]=ext[...].T.astype(low).reshape(2,2,2,4,48,wd)
        else:
            def body(i,_):
                rs=pl.ds(pl.multiple_of(i*192,192),192)
                lhs=gat[rs,:] if left==3 else lt[left,rs,:]
                p[b,i//4,lax.rem(i//2,2),lax.rem(i,2),:,:,0:wd]=dot(lhs,right()).astype(low).reshape(4,48,wd)
                return 0
            lax.fori_loop(0,8,body,0)
        if t==feeds[-1]:
            load_n.start()
        if src[0]=="feed" and t+slots<n and chunks[t+slots][3][0]=="feed": fetch(t+slots).start()
        a=remote(p.at[b,:,1-x,0,:,:,pl.ds(0,wd)],ra1[t],s1.at[t,0],v1.at[t,0],dx)
        e=remote(p.at[b,1-y,:,1,:,:,pl.ds(0,wd)],rb1[t],s1.at[t,1],v1.at[t,1],dy)
        a.start(); e.start(); c1[t]=(a,e)
    def stage2(t):
        wd=chunks[t][2]; b=t%part_slots
        for d in c1[t]: d.wait_recv()
        def body(i,_):
            h=i//4; zz=lax.rem(i,4)
            ra1[t][h,zz]=ra1[t][h,zz]+p[b,h,x,0,zz,:,0:wd]
            rb1[t][h,zz]=rb1[t][h,zz]+p[b,y,h,1,zz,:,0:wd]
            return 0
        lax.fori_loop(0,8,body,0)
        a=remote(ra1[t].at[1-y],ra2[t],s2.at[t,0],v2.at[t,0],dy)
        e=remote(rb1[t].at[1-x],rb2[t],s2.at[t,1],v2.at[t,1],dx)
        a.start(); e.start(); c2[t]=(a,e)
    def stage3(t):
        for d in c2[t]: d.wait_recv()
        def body(zz,_):
            ra2[t][zz]=ra2[t][zz]+ra1[t][y,zz]
            rb2[t][zz]=rb2[t][zz]+rb1[t][x,zz]
            return 0
        lax.fori_loop(0,4,body,0)
        cs=[]
        for k in range(3):
            cs.append(remote(ra2[t].at[zs[k]],rz[t].at[k,0],s3.at[t,k,0],v3.at[t,k,0],dz[k]))
            cs.append(remote(rb2[t].at[zs[k]],rz[t].at[k,1],s3.at[t,k,1],v3.at[t,k,1],dz[k]))
        for d in cs: d.start()
        c3[t]=cs
    def stage4(t):
        off,wd=chunks[t][1:3]
        for d in c3[t]: d.wait_recv()
        f0=ra2[t][z].astype(f32); f1=rb2[t][z].astype(f32)
        for k in range(3):
            f0=f0+rz[t][k,0].astype(f32); f1=f1+rz[t][k,1].astype(f32)
        b=t%sum_slots
        if t>=sum_slots:
            c4[t-sum_slots][0].wait_send(); c4[t-sum_slots][1].wait()
        fin[b,0,:,0:wd]=f0; fin[b,1,:,0:wd]=f1
        cols=pl.ds(off,wd)
        a=remote(fin.at[b,1-c,:,pl.ds(0,wd)],out.at[c,:,cols],s4.at[t],v4.at[t],sib)
        e=pltpu.make_async_copy(fin.at[b,c,:,pl.ds(0,wd)],out.at[c,:,cols],lo.at[t])
        a.start(); e.start(); c4[t]=(a,e)
    def step(t):
        for k,f in ((0,stage1),(1,stage2),(2,stage3),(3,stage4)):
            if 0<=t-k<n and once(k,t-k): f(t-k)
    loads[0].wait()
    step(0)
    for l in loads[1:]: l.wait()
    def wcol(a,b): return wa[:,:,:,a:b].reshape(1536,b-a)
    def mixed_grad(i,_):
        a=pl.ds(pl.multiple_of(lax.rem(i,2)*128,128),128); d=pl.ds(pl.multiple_of(i*128,128),128)
        v=part[i//2,a,:]
        gat[:,d]=v.T.astype(low)
        gm[d,:]=dot(v.astype(low),wcol(0,384)).astype(low)
        return 0
    lax.fori_loop(0,4,mixed_grad,0)
    load_w=pltpu.make_async_copy(w.at[:,:,:,pl.ds(0,1152)],wa,ll.at[13]); load_w.start()
    step(1)
    dbias[...]=jnp.zeros((256,1280),f32)
    ext[...]=jnp.zeros((128,1536),f32)
    dtab[...]=jnp.zeros((8,1280),f32)
    gives=[]
    at=2
    for h in range(6):
        odd=h%2; pair=pl.ds(128*(h//2),128); pp=h//2
        bias[...]=pltpu.roll(jnp.broadcast_to(base[h:h+1,:],(256,1280)),1024,1,stride=1,stride_axis=0)
        if not odd: acc[...]=jnp.zeros((2,2,1024,128),f32)
        def attend(i,_):
            r=i//2; d=pl.ds(pl.multiple_of(i*128,128),128)
            a=pl.ds(pl.multiple_of(lax.rem(i,2)*128,128),128)
            mine=(lanes((128,128))>=64) if odd else (lanes((128,128))<64)
            qh=jnp.where(mine,qq[d,pair].astype(f32),0.0).astype(low)
            gh=jnp.where(mine,gm[d,pair].astype(f32),0.0).astype(low)
            s=dot_nt(qh,kk[r,:,pair])+bias[a,0:1024]
            s=jnp.where(sc[r,a,0:1]==sr[r,0:1,:],s,-1000000000.0)
            pr=jnp.exp(s-lse[r,a,h:h+1])
            gp=dot_nt(gh,vv[r,:,pair])
            gl=(pr*(gp-jnp.sum(pr*gp,axis=-1,keepdims=True))).astype(low)
            wide=gl.astype(f32)
            dbias[a,0:1024]=wide+jnp.where(r==0,0.0,1.0)*dbias[a,0:1024]
            g=jnp.where(mine,dot(gl,kk[r,:,pair]),0.0)
            if odd: g=g+dq[d,pair].astype(f32)
            dq[d,pair]=g.astype(low)
            acc[0,r]=acc[0,r]+dot_tn(gl,qh)
            acc[1,r]=acc[1,r]+dot_tn(pr.astype(low),gh)
            return 0
        lax.fori_loop(0,4,attend,0)
        m=128
        v=dbias[0:128,:]+pltpu.roll(dbias[128:256,:],1280-128,1)
        while m>1:
            m//=2
            v=v[0:m]+pltpu.roll(v[m:2*m],1280-m,1)
        dtab[h:h+1,:]=pltpu.roll(v,256,1)
        if odd:
            for j in range(2):
                for r in range(2):
                    for zz in range(4):
                        dkv[zz,pp,j,r]=acc[j,r,256*zz:256*zz+256,:].astype(low)
            for k in range(3):
                g=remote(dkv.at[zs[k],pp],rkv.at[k,pp],ks.at[pp,k],kr.at[pp,k],dz[k]); g.start(); gives.append(g)
            step(at); at+=1
    tab=dtab[...]
    high=tab.astype(low); rest1=tab-high.astype(f32); mid1=rest1.astype(low); last=(rest1-mid1.astype(f32)).astype(low)
    found=dot(high,spots[...])+dot(mid1,spots[...])+dot(last,spots[...])
    def spread(v,row):
        upper=v.astype(low)
        ext[row:row+8,:]=upper.astype(f32)
        ext[row+8:row+16,:]=v-upper.astype(f32)
    upper=found.astype(low)
    ext[0:8,:]=dot(upper,tile[...])
    ext[8:16,:]=dot((found-upper.astype(f32)).astype(low),tile[...])
    spread(rows[0:8,:],32)
    step(at); at+=1
    step(at); at+=1
    step(at); at+=1
    for g in gives: g.wait_recv()
    for pp in range(3):
        for j,o in enumerate((dk,dv)):
            for r in range(2):
                v=dkv[z,pp,j,r].astype(f32)
                for k in range(3): v=v+rkv[k,pp,j,r].astype(f32)
                o[256*r:256*r+256,128*pp:128*pp+128]=v.astype(low)
    step(at); at+=1
    load_w.wait()
    def input_grad(i,_):
        d=pl.ds(pl.multiple_of(i*128,128),128); a=pl.ds(pl.multiple_of(lax.rem(i,2)*128,128),128)
        part[i//2,a,:]=dot_nt(dq[d,:],wcol(0,384))+dot_nt(dk[d,:],wcol(384,768))+dot_nt(dv[d,:],wcol(768,1152))
        return 0
    lax.fori_loop(0,4,input_grad,0)
    give=remote(part.at[1-c],r3,xs.at[0],xr.at[0],sib); give.start()
    step(at); at+=1
    give.wait_recv()
    def last_grad(i,total):
        a=pl.ds(pl.multiple_of(i*128,128),128)
        v=hid[a,:].astype(f32); gn=part[c,a,:]+r3[a,:]
        s=lax.rsqrt(jnp.mean(v*v,axis=-1,keepdims=True)+epsilon)
        wg=gn*rows[8:9,:]
        gin[a,:]=gin[a,:]+(s*wg-v*(s*s*s)*jnp.mean(wg*v,axis=-1,keepdims=True))
        return total+jnp.sum(gn*v*s,axis=0,keepdims=True)
    total=lax.fori_loop(0,2,last_grad,jnp.zeros((1,1536),f32))
    spread(jnp.broadcast_to(total,(8,1536)),16)
    give_i=pltpu.make_async_copy(gin,gin_o,ll.at[12]); give_i.start()
    while at<n+3:
        step(at); at+=1
    for t in range(n):
        off,wd=chunks[t][1:3]; cols=pl.ds(off,wd)
        remote(fin.at[t%sum_slots,1-c,:,pl.ds(0,wd)],out.at[1-c,:,cols],s4.at[t],v4.at[t],sib).wait_recv()
        if t>=n-sum_slots:
            c4[t][0].wait_send(); c4[t][1].wait()
        if t>=n-part_slots:
            for d in c1[t]: d.wait_send()
        for d in c2[t]: d.wait_send()
        for d in c3[t]: d.wait_send()
    for g in gives: g.wait_send()
    give.wait_send(); give_i.wait()

def backward_chunks(ff_steps):
    fw=512*ff_steps
    chunks=[]
    for j in range(ff_steps):
        chunks+=[(0,512*j,512,("feed",1,j)),(0,fw+512*j,512,("feed",2,j)),(1,2*fw+512*j,512,("feed",0,j))]
    o=3*fw
    chunks+=[(3,o,384,("ref",0,0)),(1,o+384,384,("ref",1,0)),(1,o+768,384,("ref",2,0)),(1,o+1152,384,("ref",3,0)),(1,o+1536,128,("ref",4,0))]
    return chunks

def backward_call(w,lt,hdg,q,kk,vv,mx,lse,gmid,segr,segc,hid,base,rows,spots,tile,ff_steps,cid=1):
    chunks=backward_chunks(ff_steps); n=len(chunks)
    C=3*512*ff_steps+1664
    S=jax.ShapeDtypeStruct; V=pltpu.VMEM; D=pltpu.SemaphoreType.DMA
    hbm=pl.BlockSpec(memory_space=pltpu.HBM); vm=pl.BlockSpec(memory_space=pltpu.VMEM)
    ws=[k[2] for k in chunks]
    scratch=[V((2,4,48,k),low) for k in ws]*1+[V((2,4,48,k),low) for k in ws]+[V((4,48,k),low) for k in ws]+[V((4,48,k),low) for k in ws]+[V((3,2,48,k),low) for k in ws]
    scratch+=[V((sum_slots,2,48,512),f32),V((part_slots,2,2,2,4,48,512),low),V((2,1536,512),low),V((1536,512),low),V((2,512,512),low),V((8,4,48,1152),low),
      V((512,384),low),V((2,1024,384),low),V((2,1024,384),low),V((512,384),low),V((512,384),low),V((2,256,128),f32),V((2,8,1024),f32),V((2,256,128),f32),
      V((256,1280),f32),V((256,1280),f32),V((512,384),low),V((2,2,1024,128),f32),V((4,3,2,2,256,128),low),V((3,3,2,2,256,128),low),V((512,384),low),V((512,384),low),
      V((2,256,1536),f32),V((256,1536),f32),V((256,1536),f32),V((256,1536),low),V((8,1280),f32),V((128,1536),f32)]
    scratch+=[D((15,)),D((n,)),D((n,)),D((n,2)),D((n,2)),D((n,2)),D((n,2)),D((n,3,2)),D((n,3,2)),D((n,)),D((n,)),D((3,3)),D((3,3)),D((1,)),D((1,))]
    return pl.pallas_call(functools.partial(backward_kernel,chunks,ff_steps),out_shape=(S((2,48,C),f32),S((256,1536),f32)),
        in_specs=[hbm]*12+[vm]*4,out_specs=(hbm,hbm),scratch_shapes=scratch,
        compiler_params=pltpu.CompilerParams(collective_id=cid,has_side_effects=True,vmem_limit_bytes=62*2**20))(w,lt,hdg,q,kk,vv,mx,lse,gmid,segr,segc,hid,base,rows,spots,tile)

def cut(v,h,w):
    n=v.shape[1]
    a=min(h*w,n); b=min((h+1)*w,n)
    p=v[:,a:b]
    return jnp.pad(p,((0,0),(0,w-(b-a)))) if b-a<w else p
def pack(wq,wk,wv,wo,ga,gf,wg,wu,wd,steps):
    gains=jnp.pad(jnp.stack([ga,gf],axis=1),((0,0),(0,126)))
    fw=512*steps
    rows=[]
    for h in (0,1):
        m=[cut(v,h,384) for v in (wq,wk,wv,wo.T)]+[gains]
        f=[cut(v,h,fw) for v in (wg,wu,wd.T)]
        for j in range(steps):
            m+=[v[:,512*j:512*j+512] for v in f]
        rows.append(jnp.concatenate(m,axis=1))
    return jnp.stack(rows)
def seg_ids(seg):
    n=seg.shape[1]
    place=jnp.arange(n,dtype=jnp.int32)
    ids=jnp.where(seg[0]>0,seg[0],-1-place).astype(jnp.float32)
    r=jnp.broadcast_to(ids[None],(8,n))
    mine=lax.dynamic_slice_in_dim(ids,lax.axis_index("seq")*256,256,0)
    return r, jnp.broadcast_to(mine[:,None],(256,128))
def base_of(table):
    off=jnp.arange(1280,dtype=jnp.int32)-256-256*lax.axis_index("seq")
    oh=(bucket_table(off)[:,None]==jnp.arange(32,dtype=jnp.int32)).astype(jnp.float32)
    c=lax.rem(lax.axis_index("dp"),2)
    tab=table.astype(jnp.float32)
    mine=jnp.where(c==0,tab[:,:6],tab[:,6:])
    b=jnp.einsum("ub,bh->hu",oh,mine,precision=lax.Precision.HIGHEST)
    return jnp.pad(b,((0,2),(0,0))), oh

def joined(o,start,width,total):
    return jnp.concatenate([o[0,:,start:start+width],o[1,:,start:start+width]],axis=1)[:,:total]
def kernel_local(hid,seg,ga,wq,wk,wv,wo,tab,gf,wg,wu,wd,cot):
    steps=4; fw=512*steps; ff=wg.shape[1]
    wp=pack(wq,wk,wv,wo,ga,gf,wg,wu,wd,steps)
    r,s=seg_ids(seg); b,oh=base_of(tab)
    w,lt,hdg,q,kk,vv,mx,lse,gmid,bo,rows,segr,segc=forward_call(wp,hid[0],cot[0],r,s,b,steps)
    spots=jnp.pad(oh,((0,0),(0,96))).astype(jnp.bfloat16)
    tile=(jnp.arange(1536)[None,:]%48==jnp.arange(128)[:,None]).astype(jnp.bfloat16)
    o,gin=backward_call(w,lt,hdg,q,kk,vv,mx,lse,gmid,segr,segc,hid[0],b,rows,spots,tile,steps)
    e=3*fw+1536
    i=3*fw
    ext=o[:,:,e:]
    t=ext[:,:32,0:8]+ext[:,:32,8:16]
    table=jnp.concatenate([t[0,:,:6],t[1,:,:6]],axis=1)
    g=ext[0]+ext[1]
    gg=lambda a: g[:,a]+g[:,a+8]
    return (bo[None],gin[None],gg(16),joined(o,i+384,384,768),joined(o,i+768,384,768),joined(o,i+1152,384,768),joined(o,i,384,768).T,table,gg(32),
            joined(o,0,fw,ff),joined(o,fw,fw,ff),joined(o,2*fw,fw,ff).T)


def solution(mesh):
    in_specs = (
        P("dp", "seq", None),
        P("dp", None),
        P(("dp", "seq")),
        P(("dp", "seq"), None),
        P(("dp", "seq"), None),
        P(("dp", "seq"), None),
        P(None, ("dp", "seq")),
        P(),
        P(("dp", "seq")),
        P(("dp", "seq"), None),
        P(("dp", "seq"), None),
        P(None, ("dp", "seq")),
        P("dp", "seq", None),
    )
    out_specs = (
        P("dp", "seq", None),
        P("dp", "seq", None),
        P(("dp", "seq")),
        P(("dp", "seq"), None),
        P(("dp", "seq"), None),
        P(("dp", "seq"), None),
        P(None, ("dp", "seq")),
        P(),
        P(("dp", "seq")),
        P(("dp", "seq"), None),
        P(("dp", "seq"), None),
        P(None, ("dp", "seq")),
    )
    small = mesh.shape["dp"] == 8 and mesh.shape["seq"] == 4
    local = kernel_local if small else plain_local
    return jax.shard_map(local, mesh=mesh, in_specs=in_specs, out_specs=out_specs, check_vma=False)
```

```python
import functools

import jax
import jax.numpy as jnp
from jax import lax
from jax.experimental import pallas as pl
from jax.experimental.pallas import tpu as pltpu
from jax.sharding import PartitionSpec as P

epsilon = 1e-06
far_bounds = (12, 16, 23, 32, 46, 64, 91)
highest = lax.Precision.HIGHEST
mesh_ids = pl.DeviceIdType.MESH


def bucket_table(offset):
    magnitude = jnp.abs(offset)
    distant = 8 + sum(((magnitude >= bound).astype(jnp.int32) for bound in far_bounds))
    signed_part = jnp.where(offset > 0, 16, 0).astype(jnp.int32)
    return signed_part + jnp.where(magnitude < 8, magnitude, distant)


def norm_scale(hidden):
    return lax.rsqrt(jnp.mean(hidden * hidden, axis=-1, keepdims=True) + epsilon)


def norm_backward(grad_normed, hidden, scale, gain):
    weighted = grad_normed * gain
    grad_gain = jnp.sum(grad_normed * hidden * scale, axis=0)
    grad_hidden = scale * weighted - hidden * (scale * scale * scale) * jnp.mean(
        weighted * hidden, axis=-1, keepdims=True
    )
    return (grad_hidden, grad_gain)


def scores_of(query_heads, key_heads, bias, allowed):
    raw_scores = jnp.einsum(
        "rqhd,rkhd->rhqk", query_heads, key_heads, preferred_element_type=jnp.float32
    )
    return jnp.where(allowed, raw_scores + bias[None], -1000000000.0)


def gather_rows(shard):
    return lax.all_gather(shard, ("dp", "seq"), axis=0, tiled=True)


def scatter_sum(parts):
    data_count = lax.axis_size("dp")
    piece_count = lax.axis_size("seq")
    shard_width = parts.shape[0] // (data_count * piece_count)
    split = parts.reshape(data_count, piece_count, shard_width, parts.shape[1])
    half = lax.psum_scatter(split, "dp", scatter_dimension=0, tiled=True)
    return lax.psum_scatter(half, "seq", scatter_dimension=1, tiled=True)[0, 0]


def plain_sums(pairs, extra):
    found = []
    for left, rights in pairs:
        for right in rights:
            part = jnp.einsum("td,tf->df", left, right, preferred_element_type=jnp.float32)
            found.append(scatter_sum(part.astype(jnp.bfloat16)).astype(jnp.float32))
    return found, scatter_sum(extra.astype(jnp.bfloat16)).astype(jnp.float32)


def plain_local(
    hidden_in,
    segment_ids,
    gain_attn,
    w_query,
    w_key,
    w_value,
    w_out,
    rel_table,
    gain_ff,
    w_gate,
    w_up,
    w_down,
    cotangent,
):
    row_count, local_len, model_width = hidden_in.shape
    row_length = segment_ids.shape[1]
    bucket_count, head_count = rel_table.shape
    token_count = row_count * local_len
    data_count = lax.axis_size("dp")
    piece_count = lax.axis_size("seq")
    shard_width = model_width // (data_count * piece_count)
    first_place = lax.axis_index("seq") * local_len
    query_place = first_place + jnp.arange(local_len, dtype=jnp.int32)
    key_place = jnp.arange(row_length, dtype=jnp.int32)
    buckets = bucket_table(key_place[None, :] - query_place[:, None])
    onehot = (buckets[:, :, None] == jnp.arange(bucket_count, dtype=jnp.int32)).astype(jnp.float32)
    bias = jnp.einsum("qkb,bh->hqk", onehot, rel_table.astype(jnp.float32), precision=highest)
    query_segs = lax.dynamic_slice_in_dim(segment_ids, first_place, local_len, 1)
    same_doc = query_segs[:, :, None] == segment_ids[:, None, :]
    visible = (segment_ids[:, None, :] > 0) | (query_place[:, None] == key_place[None, :])[None]
    allowed = (same_doc & visible)[:, None]
    inner = w_query.shape[1]
    ff_width = w_gate.shape[1]
    gains = jnp.pad(jnp.stack([gain_attn, gain_ff], axis=1), ((0, 0), (0, 126)))
    attn_full = gather_rows(jnp.concatenate([w_query, w_key, w_value, w_out.T, gains], axis=1))
    feed_full = gather_rows(jnp.concatenate([w_gate, w_up, w_down.T], axis=1))
    query_full = attn_full[:, :inner]
    key_full = attn_full[:, inner : 2 * inner]
    value_full = attn_full[:, 2 * inner : 3 * inner]
    out_full = attn_full[:, 3 * inner : 4 * inner].T
    gain_one = attn_full[:, 4 * inner]
    gain_two = attn_full[:, 4 * inner + 1]
    gate_full = feed_full[:, :ff_width]
    up_full = feed_full[:, ff_width : 2 * ff_width]
    down_full = feed_full[:, 2 * ff_width :].T
    gain_first = gain_one.astype(jnp.float32)
    residual_in = hidden_in.astype(jnp.float32).reshape(token_count, model_width)
    scale_first = norm_scale(residual_in)
    normed_first = (residual_in * scale_first * gain_first).astype(jnp.bfloat16)
    queries = jnp.dot(normed_first, query_full, preferred_element_type=jnp.float32).astype(
        jnp.bfloat16
    )
    keys_local = jnp.dot(normed_first, key_full, preferred_element_type=jnp.float32).astype(
        jnp.bfloat16
    )
    values_local = jnp.dot(normed_first, value_full, preferred_element_type=jnp.float32).astype(
        jnp.bfloat16
    )
    head_size = inner // head_count
    keys_row, values_row = (
        lax.all_gather(keys_local.reshape(row_count, local_len, inner), "seq", axis=1, tiled=True),
        lax.all_gather(
            values_local.reshape(row_count, local_len, inner), "seq", axis=1, tiled=True
        ),
    )
    query_heads = queries.reshape(row_count, local_len, head_count, head_size)
    key_heads = keys_row.reshape(row_count, row_length, head_count, head_size)
    value_heads = values_row.reshape(row_count, row_length, head_count, head_size)
    logits = scores_of(query_heads, key_heads, bias, allowed)
    row_max = jnp.max(logits, axis=-1, keepdims=True)
    exp_scores = jnp.exp(logits - row_max)
    denominator = jnp.sum(exp_scores, axis=-1, keepdims=True)
    probs_low = (exp_scores / denominator).astype(jnp.bfloat16)
    log_total = row_max + jnp.log(denominator)
    mixed = (
        jnp.einsum("rhqk,rkhd->rqhd", probs_low, value_heads, preferred_element_type=jnp.float32)
        .astype(jnp.bfloat16)
        .reshape(token_count, inner)
    )
    middle = residual_in + jnp.dot(mixed, out_full, preferred_element_type=jnp.float32)
    gain_second = gain_two.astype(jnp.float32)
    scale_second = norm_scale(middle)
    normed_second = (middle * scale_second * gain_second).astype(jnp.bfloat16)
    gate_pre = jnp.dot(normed_second, gate_full, preferred_element_type=jnp.float32)
    up_pre = jnp.dot(normed_second, up_full, preferred_element_type=jnp.float32)
    activated = jax.nn.gelu(gate_pre, approximate=True)
    hidden_mid = (activated * up_pre).astype(jnp.bfloat16)
    block_out = middle + jnp.dot(hidden_mid, down_full, preferred_element_type=jnp.float32)
    gain_second = gain_two.astype(jnp.float32)
    grad_out = cotangent.reshape(token_count, model_width)
    grad_hidden = (
        jnp.einsum("td,fd->tf", grad_out, down_full, preferred_element_type=jnp.float32)
        .astype(jnp.bfloat16)
        .astype(jnp.float32)
    )
    gelu_value, gelu_pull = jax.vjp(lambda value: jax.nn.gelu(value, approximate=True), gate_pre)
    grad_gate = gelu_pull(grad_hidden * up_pre)[0].astype(jnp.bfloat16)
    grad_up = (grad_hidden * gelu_value).astype(jnp.bfloat16)
    grad_normed_second = jnp.einsum(
        "tf,df->td", grad_gate, gate_full, preferred_element_type=jnp.float32
    ) + jnp.einsum("tf,df->td", grad_up, up_full, preferred_element_type=jnp.float32)
    grad_middle_norm, grad_gain_two = norm_backward(
        grad_normed_second, middle, scale_second, gain_second
    )
    grad_middle = grad_out.astype(jnp.float32) + grad_middle_norm
    grad_attended = grad_middle.astype(jnp.bfloat16)
    grad_mixed = jnp.einsum(
        "td,id->ti", grad_attended, out_full, preferred_element_type=jnp.float32
    ).astype(jnp.bfloat16)
    grad_heads = grad_mixed.reshape(row_count, local_len, head_count, head_size)
    logits_again = scores_of(query_heads, key_heads, bias, allowed)
    probs_again = jnp.exp(logits_again - log_total)
    probs_again_low = probs_again.astype(jnp.bfloat16)
    grad_probs = jnp.einsum(
        "rqhd,rkhd->rhqk", grad_heads, value_heads, preferred_element_type=jnp.float32
    )
    row_dot = jnp.sum(probs_again * grad_probs, axis=-1, keepdims=True)
    grad_logits = (probs_again * (grad_probs - row_dot)).astype(jnp.bfloat16)
    grad_bias = jnp.sum(grad_logits.astype(jnp.float32), axis=0)
    grad_table = jnp.einsum("qkb,hqk->bh", onehot, grad_bias, precision=highest)
    grad_queries = (
        jnp.einsum("rhqk,rkhd->rqhd", grad_logits, key_heads, preferred_element_type=jnp.float32)
        .astype(jnp.bfloat16)
        .reshape(token_count, inner)
    )
    grad_keys_row = jnp.einsum(
        "rhqk,rqhd->rkhd", grad_logits, query_heads, preferred_element_type=jnp.float32
    )
    grad_values_row = jnp.einsum(
        "rhqk,rqhd->rkhd", probs_again_low, grad_heads, preferred_element_type=jnp.float32
    )
    grad_keys_part, grad_values_part = (
        lax.psum_scatter(
            grad_keys_row.astype(jnp.bfloat16), "seq", scatter_dimension=1, tiled=True
        ).astype(jnp.float32),
        lax.psum_scatter(
            grad_values_row.astype(jnp.bfloat16), "seq", scatter_dimension=1, tiled=True
        ).astype(jnp.float32),
    )
    grad_keys = grad_keys_part.astype(jnp.bfloat16).reshape(token_count, inner)
    grad_values = grad_values_part.astype(jnp.bfloat16).reshape(token_count, inner)
    grad_normed_first = jnp.einsum(
        "ti,di->td", grad_queries, query_full, preferred_element_type=jnp.float32
    )
    grad_normed_first = grad_normed_first + jnp.einsum(
        "ti,di->td", grad_keys, key_full, preferred_element_type=jnp.float32
    )
    grad_normed_first = grad_normed_first + jnp.einsum(
        "ti,di->td", grad_values, value_full, preferred_element_type=jnp.float32
    )
    grad_first, grad_gain_one = norm_backward(
        grad_normed_first, residual_in, scale_first, gain_first
    )
    grad_input = grad_middle + grad_first
    device_count = data_count * piece_count
    table_size = bucket_count * head_count
    table_rows = -(-table_size // shard_width)
    table_block = jnp.pad(grad_table.reshape(-1), (0, table_rows * shard_width - table_size))
    table_block = jnp.broadcast_to(
        table_block.reshape(1, table_rows, shard_width), (device_count, table_rows, shard_width)
    )
    gain_block = jnp.stack([grad_gain_one, grad_gain_two], axis=0)
    gain_block = gain_block.reshape(2, device_count, shard_width).transpose(1, 0, 2)
    extra = jnp.concatenate([table_block, gain_block], axis=1).transpose(0, 2, 1)
    extra = extra.reshape(model_width, table_rows + 2)
    extra = jnp.pad(extra, ((0, 0), (0, -(table_rows + 2) % 128)))
    pairs = (
        (normed_second, (grad_gate, grad_up)),
        (grad_out, (hidden_mid,)),
        (grad_attended, (mixed,)),
        (normed_first, (grad_queries, grad_keys, grad_values)),
    )
    (gate_sum, up_sum, down_sum, out_sum, query_sum, key_sum, value_sum), extra_sum = plain_sums(
        pairs, extra
    )
    table_total = extra_sum[:, :table_rows].T.reshape(-1)[:table_size]
    table_total = table_total.reshape(bucket_count, head_count)
    grad_gain_one_shard = extra_sum[:, table_rows]
    grad_gain_two_shard = extra_sum[:, table_rows + 1]
    return (
        block_out.reshape(row_count, local_len, model_width),
        grad_input.reshape(row_count, local_len, model_width),
        grad_gain_one_shard,
        query_sum,
        key_sum,
        value_sum,
        out_sum.T,
        table_total,
        grad_gain_two_shard,
        gate_sum,
        up_sum,
        down_sum.T,
    )


gelu_c=0.7978845608028654

def peers_of():
    dp=lax.axis_index("dp"); z=lax.axis_index("seq")
    c=lax.rem(dp,2); x=lax.rem(dp//2,2); y=dp//4
    return dp,z,c,x,y

def remote(src,dst,ss,rs,dev):
    return pltpu.make_async_remote_copy(src_ref=src,dst_ref=dst,send_sem=ss,recv_sem=rs,device_id=dev,device_id_type=mesh_ids)

def dot(a,b):
    return jnp.dot(a,b,preferred_element_type=jnp.float32)

def dot_nt(a,b):
    return lax.dot_general(a,b,(((1,),(1,)),((),())),preferred_element_type=jnp.float32)

def lanes(shape):
    return lax.broadcasted_iota(jnp.int32,shape,len(shape)-1)

def greet(devices):
    bar=pltpu.get_barrier_semaphore()
    for d in devices: pl.semaphore_signal(bar,inc=1,device_id=d,device_id_type=mesh_ids)
    pl.semaphore_wait(bar,len(devices))

low=jnp.bfloat16
f32=jnp.float32

h_parts=4
def forward_kernel(ff_steps, wp, hid, cot, segr, segc, base,
                   w1, w2, w, lt_o, hdg_o, q_o, kk_o, vv_o, mx_o, lse_o, gnf_o, yy_o, gs_o, segr_o, segc_o, mid_o, cot_o,
                   hrow, cotv, sr, sc, wa, wf, qq, kk, vv, mx, lse, bias, part, mid, n2, hd, yy, lt, gs, r1,
                   s0s, s0r, l0, s1s, s1r, s2s, s2r, s3s, s3r, hs, hr, xs, xr, ll, lo):
    cols=[(0,768),(768,896)]+[(1664+512*i,512) for i in range(3*ff_steps)]
    n=len(cols)
    dp,z,c,x,y=peers_of()
    q=dp//2; qx=2*y+1-x; qy=lax.rem(q+2,4); qd=3-q
    sib=(dp+1-2*c,z); dx=(2*qx+c,z); dy=(2*qy+c,z); dxy=(dx,dy)
    zb=lax.rem(z,2); pe=z+1-2*zb; mo=2-z//2; zo=2-2*(z//2)
    inner=(z==1)|(z==2); outer=(z==0)|(z==3)
    dpe=(dp,pe); dmo=(dp,mo)
    greet([sib,dx,dy]+[(dp,lax.rem(z+k,4)) for k in (1,2,3)])
    def cs(t): return pl.ds(cols[t][0],cols[t][1])
    def wr(t): return (w1,w2)[t] if t<2 else w.at[t-2]
    def s0(t,recv=False):
        return remote(wp.at[1-c,:,cs(t)], wr(t).at[(dp+1-2*c) if recv else dp,z], s0s.at[t], s0r.at[t], sib)
    def keep(t): return pltpu.make_async_copy(wp.at[c,:,cs(t)], wr(t).at[dp,z], l0.at[t])
    def s1a(t,recv=False):
        r=wr(t).at[pl.ds(2*q,2), pe if recv else z]
        return remote(r,r,s1s.at[t,0],s1r.at[t,0],dpe)
    def s1b(t):
        r=wr(t).at[pl.ds(2*q,2), z]
        return remote(r,r,s1s.at[t,1],s1r.at[t,1+zb],dmo)
    def s1bw(t,k):
        r=wr(t).at[pl.ds(2*q,2), zo+k]
        return remote(r,r,s1s.at[t,1],s1r.at[t,1+k],dmo)
    def s1c(t):
        r=wr(t).at[pl.ds(2*q,2), pl.ds(zo,2)]
        return remote(r,r,s1s.at[t,2],s1r.at[t,3],dpe)
    def s2(t,a,recv=False):
        r=wr(t).at[pl.ds(2*((qx,qy)[a] if recv else q),2)]
        return remote(r,r,s2s.at[t,a],s2r.at[t,a],dxy[a])
    def s3(t,a,recv=False):
        r=wr(t).at[2*(qd if recv else (qy,qx)[a])+a]
        return remote(r,r,s3s.at[t,a],s3r.at[t,a],dxy[a])
    hp=hrow.shape[2]//h_parts
    def ht(p): return pl.ds(p*hp,hp)
    def ha(p,recv=False): return remote(hid.at[ht(p)],hrow.at[c,pe if recv else z,ht(p)],hs.at[p,0],hr.at[p,0],dpe)
    def hb(p): return remote(hid.at[ht(p)],hrow.at[c,z,ht(p)],hs.at[p,1],hr.at[p,1+zb],dmo)
    def hbw(p,k): return remote(hid.at[ht(p)],hrow.at[c,zo+k,ht(p)],hs.at[p,1],hr.at[p,1+k],dmo)
    def hc(p):
        r=hrow.at[c,pl.ds(zo,2),ht(p)]
        return remote(r,r,hs.at[p,2],hr.at[p,3],dpe)
    done=set()
    def once(*k):
        if k in done: return False
        done.add(k); return True
    def start1(t):
        if t<n and once(1,t):
            keep(t).wait(); s0(t,True).wait_recv()
            s1a(t).start(); s1b(t).start()
    def forward(t):
        if t<n and once(5,t):
            @pl.when(inner)
            def _():
                s1bw(t,0).wait_recv(); s1bw(t,1).wait_recv(); s1c(t).start()
    def start2(t):
        forward(t)
        if t<n and once(2,t):
            s1a(t,True).wait_recv()
            @pl.when(outer)
            def _(): s1c(t).wait_recv()
            for a in range(2): s2(t,a).start()
    def start3(t):
        if 0<=t<n and once(3,t):
            for a in range(2): s2(t,a,True).wait_recv()
            for a in range(2): s3(t,a).start()
    def finish(t):
        if 0<=t<n and once(4,t):
            for a in range(2): s3(t,a,True).wait_recv()
    def advance(t):
        for u in range(t+4): start1(u)
        for f,u in ((forward,t+1),(start2,t),(start3,t-1),(finish,t-2)):
            for v in range(u+1): f(v)
    def h_go(p): ha(p).start(); hb(p).start()
    def h_on(p):
        @pl.when(inner)
        def _():
            hbw(p,0).wait_recv(); hbw(p,1).wait_recv(); hc(p).start()
    keep_h=pltpu.make_async_copy(hid,hrow.at[c,z],ll.at[0]); keep_h.start()
    keep_c=pltpu.make_async_copy(cot,cotv.at[c],ll.at[1]); keep_c.start()
    keep_r=pltpu.make_async_copy(segr,sr.at[c],ll.at[2]); keep_r.start()
    keep_s=pltpu.make_async_copy(segc,sc.at[c],ll.at[3]); keep_s.start()
    for t in range(3): s0(t).start(); keep(t).start()
    give_h=[remote(hid,hrow.at[c,z],xs.at[3],xr.at[3],sib)]; give_h[0].start()
    give_c=remote(cot,cotv.at[c],xs.at[0],xr.at[0],sib); give_c.start()
    give_r=remote(segr,sr.at[c],xs.at[1],xr.at[1],sib); give_r.start()
    give_s=remote(segc,sc.at[c],xs.at[2],xr.at[2],sib); give_s.start()
    for t in range(3,n): s0(t).start(); keep(t).start()
    start1(0); start1(1); start1(2); h_go(0)
    forward(0); start2(0); forward(1); start2(1); forward(2)
    h_on(0); start1(3); h_go(1)
    start3(0); start2(2)
    keep_h.wait(); keep_c.wait(); keep_r.wait(); keep_s.wait()
    remote(segr,sr.at[1-c],xs.at[1],xr.at[1],sib).wait_recv()
    remote(segc,sc.at[1-c],xs.at[2],xr.at[2],sib).wait_recv()
    remote(cot,cotv.at[1-c],xs.at[0],xr.at[0],sib).wait_recv()
    remote(hid,hrow.at[1-c,z],xs.at[3],xr.at[3],sib).wait_recv()
    start3(1); forward(3); h_on(1); start1(4); h_go(2)
    finish(0); finish(1)
    load_a=[pltpu.make_async_copy(w1,wa.at[:,:,:,pl.ds(0,768)],ll.at[4]),pltpu.make_async_copy(w2,wa.at[:,:,:,pl.ds(768,896)],ll.at[11])]
    for l in load_a: l.start()
    start3(2); start2(3); forward(4); h_on(2); start1(5); h_go(3)
    for l in load_a: l.wait()
    def wcol(a,b): return wa[:,:,:,a:b].reshape(1536,b-a)
    pick=(lanes((8,128))==lax.broadcasted_iota(jnp.int32,(8,128),0)).astype(low)
    gs[...]=dot_nt(pick,wcol(1536,1664))
    def transpose_cot(i,_):
        lt[2,:,pl.ds(pl.multiple_of(i*128,128),128)]=cotv[i//2,pl.ds(pl.multiple_of(lax.rem(i,2)*128,128),128),:].astype(f32).T.astype(low)
        return 0
    lax.fori_loop(0,4,transpose_cot,0)
    def normed(v,row):
        s=lax.rsqrt(jnp.mean(v*v,axis=-1,keepdims=True)+epsilon)
        return v*s*gs[row:row+1,:]
    def queries(i,_):
        a=pl.ds(pl.multiple_of(lax.rem(i,2)*128,128),128)
        v=normed(hrow[i//2,z,a,:].astype(f32),0)
        d=pl.ds(pl.multiple_of(i*128,128),128)
        qq[d,:]=dot(v.astype(low),wcol(0,384)).astype(low)
        lt[0,:,d]=v.T.astype(low)
        return 0
    lax.fori_loop(0,4,queries,0)
    start2(4); start3(3); finish(2); forward(5); h_on(3)
    for p in range(h_parts):
        ha(p,True).wait_recv()
        @pl.when(outer)
        def _(): hc(p).wait_recv()
    for k in (1,2,3):
        r=hrow.at[c,lax.rem(z+k,4)]
        g=remote(r,r,xs.at[6+k],xr.at[6+k],sib); g.start(); give_h.append(g)
    def keys_of(r):
        def body(i,_):
            a=pl.ds(pl.multiple_of(lax.rem(i,2)*128,128),128)
            v=normed(hrow[r,i//2,a,:].astype(f32),0).astype(low)
            d=pl.ds(pl.multiple_of(i*128,128),128)
            kk[r,d,:]=dot(v,wcol(384,768)).astype(low)
            vv[r,d,:]=dot(v,wcol(768,1152)).astype(low)
            return 0
        lax.fori_loop(0,8,body,0)
    keys_of(c)
    for k in (1,2,3):
        r=hrow.at[1-c,lax.rem(z+k,4)]
        remote(r,r,xs.at[6+k],xr.at[6+k],sib).wait_recv()
    advance(5)
    keys_of(1-c)
    advance(6)
    for h in range(6):
        pair=pl.ds(128*(h//2),128); odd=h%2
        bias[...]=pltpu.roll(jnp.broadcast_to(base[h:h+1,:],(256,1280)),1024,1,stride=1,stride_axis=0)
        def attend(i,_):
            r=i//2; d=pl.ds(pl.multiple_of(i*128,128),128)
            a=pl.ds(pl.multiple_of(lax.rem(i,2)*128,128),128)
            mine=(lanes((128,128))>=64) if odd else (lanes((128,128))<64)
            qh=jnp.where(mine,qq[d,pair].astype(f32),0.0).astype(low)
            s=dot_nt(qh,kk[r,:,pair])+bias[a,0:1024]
            s=jnp.where(sc[r,a,0:1]==sr[r,0:1,:],s,-1000000000.0)
            m=jnp.max(s,axis=-1,keepdims=True)
            e=jnp.exp(s-m)
            l=jnp.sum(e,axis=-1,keepdims=True)
            p=(e*(1.0/l)).astype(low)
            o=dot(p,vv[r,:,pair])
            if odd: o=jnp.where(mine,o,mx[d,pair].astype(f32))
            mx[d,pair]=o.astype(low)
            lse[r,a,:]=jnp.where(lanes((128,128))==h,m+jnp.log(l),lse[r,a,:]) if h else jnp.broadcast_to(m+jnp.log(l),(128,128))
            return 0
        lax.fori_loop(0,4,attend,0)
        if h in (1,3): advance(7+h//2)
    def project(i,_):
        part[i//2,pl.ds(pl.multiple_of(lax.rem(i,2)*128,128),128),:]=dot_nt(mx[pl.ds(pl.multiple_of(i*128,128),128),:],wcol(1152,1536))
        return 0
    lax.fori_loop(0,4,project,0)
    give_p=remote(part,r1,xs.at[4],xr.at[4],sib); give_p.start()
    outs=[pltpu.make_async_copy(a,b,lo.at[i]) for i,(a,b) in enumerate(((qq,q_o),(kk,kk_o),(vv,vv_o),(mx,mx_o),(lse,lse_o),(sr,segr_o),(sc,segc_o),(cotv,cot_o)))]
    for o in outs: o.start()
    give_p.wait_recv()
    def middle(i,_):
        a=pl.ds(pl.multiple_of(lax.rem(i,2)*128,128),128); r=i//2
        d=pl.ds(pl.multiple_of(i*128,128),128)
        v=hrow[r,z,a,:].astype(f32)+(part[r,a,:]+r1[r,a,:])
        mid[r,a,:]=v
        v=normed(v,1)
        n2[d,:]=v.astype(low)
        lt[1,:,d]=v.T.astype(low)
        return 0
    lax.fori_loop(0,4,middle,0)
    give_p.wait_send()
    give_lt=pltpu.make_async_copy(lt,lt_o,ll.at[5]); give_lt.start()
    give_mid=pltpu.make_async_copy(mid,mid_o,ll.at[12]); give_mid.start()
    gs_o[...]=gs[...]
    advance(9)
    hout=[]
    for j in range(ff_steps):
        if j:
            for t in range(4+3*j,7+3*j): advance(t)
        loads=[pltpu.make_async_copy(w.at[3*j+i],wf.at[i],ll.at[6+i]) for i in range(3)]
        for l in loads: l.start()
        b=j%2
        if j>=2: hout[j-2].wait()
        for l in loads: l.wait()
        def feed(i,_):
            d=pl.ds(pl.multiple_of(i*256,256),256)
            v=n2[d,:]
            wg=wf[0].reshape(1536,512); wu=wf[1].reshape(1536,512); wd=wf[2].reshape(1536,512)
            gate=dot(v,wg); up=dot(v,wu)
            gh=dot(cotv[i],wd).astype(low).astype(f32)
            u2=gate*gate
            th=jnp.tanh(gelu_c*(gate+0.044715*(gate*u2)))
            act=0.5*gate*(1.0+th)
            slope=0.5*(1.0+th)+0.5*gate*(1.0-th*th)*(gelu_c*(1.0+3*0.044715*u2))
            hm=(act*up).astype(low); dg=(gh*up*slope).astype(low); du=(gh*act).astype(low)
            hd[b,0,d,:]=hm; hd[b,1,d,:]=dg; hd[b,2,d,:]=du
            yp=dot_nt(hm,wd); gp=dot_nt(dg,wg)+dot_nt(du,wu)
            if j: yp=yp+yy[i]; gp=gp+part[i]
            yy[i]=yp; part[i]=gp
            return 0
        lax.fori_loop(0,2,feed,0)
        o=pltpu.make_async_copy(hd.at[b],hdg_o.at[:,:,pl.ds(512*j,512)],lo.at[8+b]); o.start(); hout.append(o)
    give_m=[pltpu.make_async_copy(part,gnf_o,ll.at[9]),pltpu.make_async_copy(yy,yy_o,ll.at[10])]
    for g in give_m: g.start()
    for o in outs+hout[-2:]: o.wait()
    give_lt.wait(); give_mid.wait()
    for g in give_m: g.wait()
    give_c.wait_send(); give_r.wait_send(); give_s.wait_send()
    for g in give_h: g.wait_send()
    for p in range(h_parts):
        ha(p).wait_send(); hb(p).wait_send()
        @pl.when(inner)
        def _(): hc(p).wait_send()
    for t in range(n):
        s0(t).wait_send()
        s1a(t).wait_send(); s1b(t).wait_send()
        @pl.when(inner)
        def _(): s1c(t).wait_send()
        for a in range(2): s2(t,a).wait_send(); s3(t,a).wait_send()

def forward_call(wp, hid, cot, segr, segc, base, ff_steps, cid=0):
    n=2+3*ff_steps
    S=jax.ShapeDtypeStruct; V=pltpu.VMEM; D=pltpu.SemaphoreType.DMA
    fw=512*ff_steps
    hbm=pl.BlockSpec(memory_space=pltpu.HBM); vm=pl.BlockSpec(memory_space=pltpu.VMEM)
    outs=(S((8,4,48,768),low),S((8,4,48,896),low),S((3*ff_steps,8,4,48,512),low),S((3,1536,512),low),S((3,512,fw),low),S((512,384),low),S((2,1024,384),low),S((2,1024,384),low),
          S((512,384),low),S((2,256,128),f32),S((2,256,1536),f32),S((2,256,1536),f32),S((8,1536),f32),S((2,8,1024),f32),S((2,256,128),f32),S((2,256,1536),f32),S((2,256,1536),low))
    ospec=[hbm]*17; ospec[12]=vm
    scratch=[V((2,4,256,1536),low),V((2,256,1536),low),V((2,8,1024),f32),V((2,256,128),f32),V((8,4,48,1664),low),V((3,8,4,48,512),low),
             V((512,384),low),V((2,1024,384),low),V((2,1024,384),low),V((512,384),low),V((2,256,128),f32),V((256,1280),f32),
             V((2,256,1536),f32),V((2,256,1536),f32),V((512,1536),low),V((2,3,512,512),low),V((2,256,1536),f32),V((3,1536,512),low),V((8,1536),f32),
             V((2,256,1536),f32),
             D((n,)),D((n,)),D((n,)),D((n,3)),D((n,4)),D((n,2)),D((n,2)),D((n,2)),D((n,2)),D((h_parts,3)),D((h_parts,4)),D((10,)),D((10,)),D((13,)),D((10,))]
    return pl.pallas_call(functools.partial(forward_kernel,ff_steps),out_shape=outs,
        in_specs=[vm]+[hbm]*4+[vm],out_specs=tuple(ospec),scratch_shapes=scratch,
        compiler_params=pltpu.CompilerParams(collective_id=cid,has_side_effects=True,vmem_limit_bytes=62*2**20))(wp,hid,cot,segr,segc,base)

def dot_tn(a,b):
    return lax.dot_general(a,b,(((0,),(0,)),((),())),preferred_element_type=jnp.float32)

part_slots=2
sum_slots=3
lag=6
def backward_kernel(chunks, ff_steps, w1, w2, lt_h, hdg, q_h, kk_h, vv_h, mx_h, lse_h, gnf_h, yy_h, mid_h, cot_h, segr_h, segc_h, hid_h, base, gains, spots, tile,
                    out, gin_o, bo_o, xg, xy, *rest):
    n=len(chunks)
    ra1=rest[0:n]; rb1=rest[n:2*n]; ra2=rest[2*n:3*n]; rb2=rest[3*n:4*n]; rz=rest[4*n:5*n]
    (fin,p,lt,gat,rbuf,wa,qq,kk,vv,mx,gm,lse,sr,sc,bias,dbias,dq,acc,dkv,rka,rkb,rkc,dk,dv,part,r3,hid,dtab,ext,cb,
     ll,lr,lo,s1,v1,s2,v2,s3,v3,s4,v4,ks,kr,xs,xr,lb)=rest[5*n:]
    dp,z,c,x,y=peers_of()
    sib=(dp+1-2*c,z); dx=(dp+2-4*x,z); dy=(lax.rem(dp+4,8),z)
    zs=[lax.rem(z+k,4) for k in (1,2,3)]; dz=[(dp,zz) for zz in zs]
    zb=lax.rem(z,2); pe=z+1-2*zb; mo=2-z//2; zo=2-2*(z//2)
    inner=(z==1)|(z==2); outer=(z==0)|(z==3)
    def ka(pp,recv=False): return remote(dkv.at[pp,pe],rka.at[pp],ks.at[pp,0],kr.at[pp,0],(dp,pe))
    def kc(pp): return remote(dkv.at[pp,pl.ds(zo,2)],rkc.at[pp],ks.at[pp,1],kr.at[pp,1],(dp,pe))
    def kb(pp,k): return remote(dkv.at[pp,zo+k],rkb.at[pp],ks.at[pp,2+k],kr.at[pp,2],(dp,zo+k))
    def relay(pp):
        @pl.when(inner)
        def _():
            kc(pp).wait_recv()
            for k in range(2):
                for j in range(2):
                    for r in range(2):
                        dkv[pp,zo+k,j,r]=(dkv[pp,zo+k,j,r].astype(f32)+rkc[pp,k,j,r].astype(f32)).astype(low)
                kb(pp,k).start()
    loads=[pltpu.make_async_copy(a,b,ll.at[i]) for i,(a,b) in enumerate((
        (lt_h.at[pl.ds(1,2)],lt),(w2.at[:,:,:,pl.ds(384,384)],wa.at[:,:,:,pl.ds(0,384)]),(q_h,qq),(kk_h,kk),(vv_h,vv),(mx_h,mx),(lse_h,lse),(segr_h,sr),(segc_h,sc),(hid_h,hid)))]
    for l in loads: l.start()
    slots=rbuf.shape[0]
    def fetch(t):
        kind,i,j=chunks[t][3]
        return pltpu.make_async_copy(hdg.at[i,:,pl.ds(512*j,512)],rbuf.at[t%slots],lr.at[t])
    feeds=[t for t in range(n) if chunks[t][3][0]=="feed"]
    for t in feeds[:slots]: fetch(t).start()
    greet([sib,dx,dy]+dz)
    load_n=pltpu.make_async_copy(lt_h.at[0],lt.at[1],ll.at[14])
    c1={}; c2={}; c3={}; c4={}; done=set()
    def once(*k):
        if k in done: return False
        done.add(k); return True
    def stage1(t):
        left,off,wd,src=chunks[t]; b=t%part_slots
        if t>=part_slots:
            for d in c1[t-part_slots]: d.wait_send()
        if src[0]=="feed":
            fetch(t).wait()
            right=lambda: rbuf[t%slots]
        else:
            right=(lambda: mx[...],lambda: dq[...],lambda: dk[...],lambda: dv[...],None)[src[1]]
        if src==("ref",1,0): load_n.wait()
        if right is None:
            p[b,:,:,:,:,:,0:wd]=ext[...].T.astype(low).reshape(2,2,2,4,48,wd)
        else:
            def body(i,_):
                rs=pl.ds(pl.multiple_of(i*192,192),192)
                lhs=gat[rs,:] if left==3 else lt[left,rs,:]
                p[b,i//4,lax.rem(i//2,2),lax.rem(i,2),:,:,0:wd]=dot(lhs,right()).astype(low).reshape(4,48,wd)
                return 0
            lax.fori_loop(0,8,body,0)
        if t==feeds[-1]:
            load_n.start()
        if src[0]=="feed" and t+slots<n and chunks[t+slots][3][0]=="feed": fetch(t+slots).start()
        a=remote(p.at[b,:,1-x,0,:,:,pl.ds(0,wd)],ra1[t],s1.at[t,0],v1.at[t,0],dx)
        e=remote(p.at[b,1-y,:,1,:,:,pl.ds(0,wd)],rb1[t],s1.at[t,1],v1.at[t,1],dy)
        a.start(); e.start(); c1[t]=(a,e)
    def stage2(t):
        wd=chunks[t][2]; b=t%part_slots
        for d in c1[t]: d.wait_recv()
        def body(i,_):
            h=i//4; zz=lax.rem(i,4)
            ra1[t][h,zz]=ra1[t][h,zz]+p[b,h,x,0,zz,:,0:wd]
            rb1[t][h,zz]=rb1[t][h,zz]+p[b,y,h,1,zz,:,0:wd]
            return 0
        lax.fori_loop(0,8,body,0)
        a=remote(ra1[t].at[1-y],ra2[t],s2.at[t,0],v2.at[t,0],dy)
        e=remote(rb1[t].at[1-x],rb2[t],s2.at[t,1],v2.at[t,1],dx)
        a.start(); e.start(); c2[t]=(a,e)
    def stage3(t):
        for d in c2[t]: d.wait_recv()
        def body(zz,_):
            ra2[t][zz]=ra2[t][zz]+ra1[t][y,zz]
            rb2[t][zz]=rb2[t][zz]+rb1[t][x,zz]
            return 0
        lax.fori_loop(0,4,body,0)
        cs=[]
        for k in range(3):
            cs.append(remote(ra2[t].at[zs[k]],rz[t].at[k,0],s3.at[t,k,0],v3.at[t,k,0],dz[k]))
            cs.append(remote(rb2[t].at[zs[k]],rz[t].at[k,1],s3.at[t,k,1],v3.at[t,k,1],dz[k]))
        for d in cs: d.start()
        c3[t]=cs
    def stage4(t):
        off,wd=chunks[t][1:3]
        for d in c3[t]: d.wait_recv()
        f0=ra2[t][z].astype(f32); f1=rb2[t][z].astype(f32)
        for k in range(3):
            f0=f0+rz[t][k,0].astype(f32); f1=f1+rz[t][k,1].astype(f32)
        b=t%sum_slots
        if t>=sum_slots:
            c4[t-sum_slots][0].wait_send(); c4[t-sum_slots][1].wait()
        fin[b,0,:,0:wd]=f0; fin[b,1,:,0:wd]=f1
        cols=pl.ds(off,wd)
        a=remote(fin.at[b,1-c,:,pl.ds(0,wd)],out.at[c,:,cols],s4.at[t],v4.at[t],sib)
        e=pltpu.make_async_copy(fin.at[b,c,:,pl.ds(0,wd)],out.at[c,:,cols],lo.at[t])
        a.start(); e.start(); c4[t]=(a,e)
    def step(s):
        for f,t in ((stage2,s),(stage1,s+2),(stage3,s-1),(stage4,s-lag)):
            if 0<=t<n and once(f.__name__,t): f(t)
    give_g=remote(gnf_h,xg,xs.at[1],xr.at[1],sib); give_g.start()
    give_y=remote(yy_h.at[1-c],xy,xs.at[2],xr.at[2],sib); give_y.start()
    loads[0].wait()
    stage1(0); stage1(1); once("stage1",0); once("stage1",1)
    for l in loads[1:]: l.wait()
    def wcol(a,b): return wa[:,:,:,a:b].reshape(1536,b-a)
    give_g.wait_recv()
    total=jnp.zeros((1,1536),f32)
    for i in range(4):
        r=i//2; a=pl.ds(128*(i%2),128); d=pl.ds(128*i,128)
        first=part.at[0,pl.ds(0,128)]; second=part.at[0,pl.ds(128,128)]; third=part.at[1,pl.ds(0,128)]
        moves=[pltpu.make_async_copy(f,g,lb.at[k]) for k,(f,g) in enumerate(((mid_h.at[r,a],first),(gnf_h.at[r,a],second),(xg.at[r,a],third),(cot_h.at[r,a],cb)))]
        for m in moves: m.start()
        for m in moves: m.wait()
        v=part[0,0:128,:]; gn=part[0,128:256,:]+part[1,0:128,:]
        s=lax.rsqrt(jnp.mean(v*v,axis=-1,keepdims=True)+epsilon)
        wg=gn*gains[1:2,:]
        g=cb[...].astype(f32)+(s*wg-v*(s*s*s)*jnp.mean(wg*v,axis=-1,keepdims=True))
        total=total+jnp.where(c==r,1.0,0.0)*jnp.sum(gn*v*s,axis=0,keepdims=True)
        part[1,128:256,:]=g
        @pl.when(c==r)
        def _():
            back=pltpu.make_async_copy(part.at[1,pl.ds(128,128)],gin_o.at[a],lb.at[4]); back.start(); back.wait()
        gat[:,d]=g.T.astype(low)
        gm[d,:]=dot(g.astype(low),wcol(0,384)).astype(low)
    ext[...]=jnp.zeros((128,1536),f32)
    def spread(v,row):
        upper=v.astype(low)
        ext[row:row+8,:]=upper.astype(f32)
        ext[row+8:row+16,:]=v-upper.astype(f32)
    spread(jnp.broadcast_to(total,(8,1536)),32)
    load_w=[pltpu.make_async_copy(w1,wa.at[:,:,:,pl.ds(0,768)],ll.at[13]),pltpu.make_async_copy(w2.at[:,:,:,pl.ds(0,384)],wa.at[:,:,:,pl.ds(768,384)],ll.at[15])]
    for l in load_w: l.start()
    step(0)
    dbias[...]=jnp.zeros((256,1280),f32)
    dtab[...]=jnp.zeros((8,1280),f32)
    at=1
    for h in range(6):
        odd=h%2; pair=pl.ds(128*(h//2),128); pp=h//2
        bias[...]=pltpu.roll(jnp.broadcast_to(base[h:h+1,:],(256,1280)),1024,1,stride=1,stride_axis=0)
        if not odd: acc[...]=jnp.zeros((2,2,1024,128),f32)
        def attend(i,_):
            r=i//2; d=pl.ds(pl.multiple_of(i*128,128),128)
            a=pl.ds(pl.multiple_of(lax.rem(i,2)*128,128),128)
            mine=(lanes((128,128))>=64) if odd else (lanes((128,128))<64)
            qh=jnp.where(mine,qq[d,pair].astype(f32),0.0).astype(low)
            gh=jnp.where(mine,gm[d,pair].astype(f32),0.0).astype(low)
            s=dot_nt(qh,kk[r,:,pair])+bias[a,0:1024]
            s=jnp.where(sc[r,a,0:1]==sr[r,0:1,:],s,-1000000000.0)
            pr=jnp.exp(s-lse[r,a,h:h+1])
            gp=dot_nt(gh,vv[r,:,pair])
            gl=(pr*(gp-jnp.sum(pr*gp,axis=-1,keepdims=True))).astype(low)
            wide=gl.astype(f32)
            dbias[a,0:1024]=wide+jnp.where(r==0,0.0,1.0)*dbias[a,0:1024]
            g=jnp.where(mine,dot(gl,kk[r,:,pair]),0.0)
            if odd: g=g+dq[d,pair].astype(f32)
            dq[d,pair]=g.astype(low)
            acc[0,r]=acc[0,r]+dot_tn(gl,qh)
            acc[1,r]=acc[1,r]+dot_tn(pr.astype(low),gh)
            return 0
        lax.fori_loop(0,4,attend,0)
        m=128
        v=dbias[0:128,:]+pltpu.roll(dbias[128:256,:],1280-128,1)
        while m>1:
            m//=2
            v=v[0:m]+pltpu.roll(v[m:2*m],1280-m,1)
        dtab[h:h+1,:]=pltpu.roll(v,256,1)
        if odd:
            for j in range(2):
                for r in range(2):
                    for zz in range(4):
                        dkv[pp,zz,j,r]=acc[j,r,256*zz:256*zz+256,:].astype(low)
            ka(pp).start()
            @pl.when(outer)
            def _(): kc(pp).start()
            step(at); at+=1
            if pp: relay(pp-1)
    tab=dtab[...]
    high=tab.astype(low); rest1=tab-high.astype(f32); mid1=rest1.astype(low); last=(rest1-mid1.astype(f32)).astype(low)
    found=dot(high,spots[...])+dot(mid1,spots[...])+dot(last,spots[...])
    upper=found.astype(low)
    ext[0:8,:]=dot(upper,tile[...])
    ext[8:16,:]=dot((found-upper.astype(f32)).astype(low),tile[...])
    give_y.wait_recv()
    for i in range(2):
        a=pl.ds(128*i,128)
        first=part.at[0,pl.ds(0,128)]; second=part.at[0,pl.ds(128,128)]; third=part.at[1,pl.ds(0,128)]
        moves=[pltpu.make_async_copy(f,g,lb.at[k]) for k,(f,g) in enumerate(((mid_h.at[c,a],first),(yy_h.at[c,a],second),(xy.at[a],third)))]
        for m in moves: m.start()
        for m in moves: m.wait()
        part[1,128:256,:]=part[0,0:128,:]+(part[0,128:256,:]+part[1,0:128,:])
        back=pltpu.make_async_copy(part.at[1,pl.ds(128,128)],bo_o.at[a],lb.at[4]); back.start(); back.wait()
    step(at); at+=1
    relay(2)
    while at<9:
        step(at); at+=1
    for pp in range(3):
        ka(pp).wait_recv(); kb(pp,0).wait_recv()
        for j,o in enumerate((dk,dv)):
            for r in range(2):
                v=dkv[pp,z,j,r].astype(f32)+rka[pp,j,r].astype(f32)+rkb[pp,j,r].astype(f32)
                o[256*r:256*r+256,128*pp:128*pp+128]=v.astype(low)
    step(at); at+=1
    for l in load_w: l.wait()
    def input_grad(i,_):
        d=pl.ds(pl.multiple_of(i*128,128),128); a=pl.ds(pl.multiple_of(lax.rem(i,2)*128,128),128)
        part[i//2,a,:]=dot_nt(dq[d,:],wcol(0,384))+dot_nt(dk[d,:],wcol(384,768))+dot_nt(dv[d,:],wcol(768,1152))
        return 0
    lax.fori_loop(0,4,input_grad,0)
    give=remote(part.at[1-c],r3,xs.at[0],xr.at[0],sib); give.start()
    step(at); at+=1
    give.wait_send()
    load_i=pltpu.make_async_copy(gin_o,part.at[1-c],lb.at[0]); load_i.start()
    give.wait_recv(); load_i.wait()
    def last_grad(i,total):
        a=pl.ds(pl.multiple_of(i*128,128),128)
        v=hid[a,:].astype(f32); gn=part[c,a,:]+r3[a,:]
        s=lax.rsqrt(jnp.mean(v*v,axis=-1,keepdims=True)+epsilon)
        wg=gn*gains[0:1,:]
        part[1-c,a,:]=part[1-c,a,:]+(s*wg-v*(s*s*s)*jnp.mean(wg*v,axis=-1,keepdims=True))
        return total+jnp.sum(gn*v*s,axis=0,keepdims=True)
    total=lax.fori_loop(0,2,last_grad,jnp.zeros((1,1536),f32))
    spread(jnp.broadcast_to(total,(8,1536)),16)
    give_i=pltpu.make_async_copy(part.at[1-c],gin_o,ll.at[12]); give_i.start()
    while at<n+lag:
        step(at); at+=1
    for t in range(n):
        off,wd=chunks[t][1:3]; cols=pl.ds(off,wd)
        remote(fin.at[t%sum_slots,1-c,:,pl.ds(0,wd)],out.at[1-c,:,cols],s4.at[t],v4.at[t],sib).wait_recv()
        if t>=n-sum_slots:
            c4[t][0].wait_send(); c4[t][1].wait()
        if t>=n-part_slots:
            for d in c1[t]: d.wait_send()
        for d in c2[t]: d.wait_send()
        for d in c3[t]: d.wait_send()
    for pp in range(3):
        ka(pp).wait_send()
        @pl.when(outer)
        def _(): kc(pp).wait_send()
        @pl.when(inner)
        def _(): kb(pp,0).wait_send(); kb(pp,1).wait_send()
    give_i.wait(); give_g.wait_send(); give_y.wait_send()

def backward_chunks(ff_steps):
    fw=512*ff_steps
    chunks=[]
    for j in range(ff_steps):
        chunks+=[(0,512*j,512,("feed",1,j)),(0,fw+512*j,512,("feed",2,j)),(1,2*fw+512*j,512,("feed",0,j))]
    o=3*fw
    chunks+=[(3,o,384,("ref",0,0)),(1,o+384,384,("ref",1,0)),(1,o+768,384,("ref",2,0)),(1,o+1152,384,("ref",3,0)),(1,o+1536,128,("ref",4,0))]
    return chunks

def backward_call(w1,w2,lt,hdg,q,kk,vv,mx,lse,gnf,yy,mid,cot,segr,segc,hid,base,gains,spots,tile,ff_steps,cid=1):
    chunks=backward_chunks(ff_steps); n=len(chunks)
    C=3*512*ff_steps+1664
    S=jax.ShapeDtypeStruct; V=pltpu.VMEM; D=pltpu.SemaphoreType.DMA
    hbm=pl.BlockSpec(memory_space=pltpu.HBM); vm=pl.BlockSpec(memory_space=pltpu.VMEM)
    ws=[k[2] for k in chunks]
    scratch=[V((2,4,48,k),low) for k in ws]*1+[V((2,4,48,k),low) for k in ws]+[V((4,48,k),low) for k in ws]+[V((4,48,k),low) for k in ws]+[V((3,2,48,k),low) for k in ws]
    scratch+=[V((sum_slots,2,48,512),f32),V((part_slots,2,2,2,4,48,512),low),V((2,1536,512),low),V((1536,512),low),V((2,512,512),low),V((8,4,48,1152),low),
      V((512,384),low),V((2,1024,384),low),V((2,1024,384),low),V((512,384),low),V((512,384),low),V((2,256,128),f32),V((2,8,1024),f32),V((2,256,128),f32),
      V((256,1280),f32),V((256,1280),f32),V((512,384),low),V((2,2,1024,128),f32),V((3,4,2,2,256,128),low),V((3,2,2,256,128),low),V((3,2,2,256,128),low),V((3,2,2,2,256,128),low),V((512,384),low),V((512,384),low),
      V((2,256,1536),f32),V((256,1536),f32),V((256,1536),low),V((8,1280),f32),V((128,1536),f32),V((128,1536),low)]
    scratch+=[D((16,)),D((n,)),D((n,)),D((n,2)),D((n,2)),D((n,2)),D((n,2)),D((n,3,2)),D((n,3,2)),D((n,)),D((n,)),D((3,4)),D((3,3)),D((3,)),D((3,)),D((5,))]
    return pl.pallas_call(functools.partial(backward_kernel,chunks,ff_steps),out_shape=(S((2,48,C),f32),S((256,1536),f32),S((256,1536),f32),S((2,256,1536),f32),S((256,1536),f32)),
        in_specs=[hbm]*16+[vm]*4,out_specs=(hbm,)*5,scratch_shapes=scratch,
        compiler_params=pltpu.CompilerParams(collective_id=cid,has_side_effects=True,vmem_limit_bytes=62*2**20))(w1,w2,lt,hdg,q,kk,vv,mx,lse,gnf,yy,mid,cot,segr,segc,hid,base,gains,spots,tile)

def cut(v,h,w):
    n=v.shape[1]
    a=min(h*w,n); b=min((h+1)*w,n)
    p=v[:,a:b]
    return jnp.pad(p,((0,0),(0,w-(b-a)))) if b-a<w else p
def pack(wq,wk,wv,wo,ga,gf,wg,wu,wd,steps):
    gains=jnp.pad(jnp.stack([ga,gf],axis=1),((0,0),(0,126)))
    fw=512*steps
    rows=[]
    for h in (0,1):
        m=[cut(v,h,384) for v in (wq,wk,wv,wo.T)]+[gains]
        f=[cut(v,h,fw) for v in (wg,wu,wd.T)]
        for j in range(steps):
            m+=[v[:,512*j:512*j+512] for v in f]
        rows.append(jnp.concatenate(m,axis=1))
    return jnp.stack(rows)
def seg_ids(seg):
    n=seg.shape[1]
    place=jnp.arange(n,dtype=jnp.int32)
    ids=jnp.where(seg[0]>0,seg[0],-1-place).astype(jnp.float32)
    r=jnp.broadcast_to(ids[None],(8,n))
    mine=lax.dynamic_slice_in_dim(ids,lax.axis_index("seq")*256,256,0)
    return r, jnp.broadcast_to(mine[:,None],(256,128))
def base_of(table):
    off=jnp.arange(1280,dtype=jnp.int32)-256-256*lax.axis_index("seq")
    oh=(bucket_table(off)[:,None]==jnp.arange(32,dtype=jnp.int32)).astype(jnp.float32)
    c=lax.rem(lax.axis_index("dp"),2)
    tab=table.astype(jnp.float32)
    mine=jnp.where(c==0,tab[:,:6],tab[:,6:])
    b=jnp.einsum("ub,bh->hu",oh,mine,precision=lax.Precision.HIGHEST)
    return jnp.pad(b,((0,2),(0,0))), oh

def joined(o,start,width,total):
    return jnp.concatenate([o[0,:,start:start+width],o[1,:,start:start+width]],axis=1)[:,:total]
def kernel_local(hid,seg,ga,wq,wk,wv,wo,tab,gf,wg,wu,wd,cot):
    steps=4; fw=512*steps; ff=wg.shape[1]
    wp=pack(wq,wk,wv,wo,ga,gf,wg,wu,wd,steps)
    r,s=seg_ids(seg); b,oh=base_of(tab)
    w1,w2,w,lt,hdg,q,kk,vv,mx,lse,gnf,yy,gains,segr,segc,mid,cot2=forward_call(wp,hid[0],cot[0],r,s,b,steps)
    spots=jnp.pad(oh,((0,0),(0,96))).astype(jnp.bfloat16)
    tile=(jnp.arange(1536)[None,:]%48==jnp.arange(128)[:,None]).astype(jnp.bfloat16)
    o,gin,bo,_,_=backward_call(w1,w2,lt,hdg,q,kk,vv,mx,lse,gnf,yy,mid,cot2,segr,segc,hid[0],b,gains,spots,tile,steps)
    e=3*fw+1536
    i=3*fw
    ext=o[:,:,e:]
    t=ext[:,:32,0:8]+ext[:,:32,8:16]
    table=jnp.concatenate([t[0,:,:6],t[1,:,:6]],axis=1)
    g=ext[0]+ext[1]
    gg=lambda a: g[:,a]+g[:,a+8]
    return (bo[None],gin[None],gg(16),joined(o,i+384,384,768),joined(o,i+768,384,768),joined(o,i+1152,384,768),joined(o,i,384,768).T,table,gg(32),
            joined(o,0,fw,ff),joined(o,fw,fw,ff),joined(o,2*fw,fw,ff).T)


def solution(mesh):
    in_specs = (
        P("dp", "seq", None),
        P("dp", None),
        P(("dp", "seq")),
        P(("dp", "seq"), None),
        P(("dp", "seq"), None),
        P(("dp", "seq"), None),
        P(None, ("dp", "seq")),
        P(),
        P(("dp", "seq")),
        P(("dp", "seq"), None),
        P(("dp", "seq"), None),
        P(None, ("dp", "seq")),
        P("dp", "seq", None),
    )
    out_specs = (
        P("dp", "seq", None),
        P("dp", "seq", None),
        P(("dp", "seq")),
        P(("dp", "seq"), None),
        P(("dp", "seq"), None),
        P(("dp", "seq"), None),
        P(None, ("dp", "seq")),
        P(),
        P(("dp", "seq")),
        P(("dp", "seq"), None),
        P(("dp", "seq"), None),
        P(None, ("dp", "seq")),
    )
    small = mesh.shape["dp"] == 8 and mesh.shape["seq"] == 4
    local = kernel_local if small else plain_local
    return jax.shard_map(local, mesh=mesh, in_specs=in_specs, out_specs=out_specs, check_vma=False)
```

```python
import functools

import jax
import jax.numpy as jnp
from jax import lax
from jax.experimental import pallas as pl
from jax.experimental.pallas import tpu as pltpu
from jax.sharding import PartitionSpec as P

epsilon = 1e-06
far_bounds = (12, 16, 23, 32, 46, 64, 91)
highest = lax.Precision.HIGHEST
mesh_ids = pl.DeviceIdType.MESH


def bucket_table(offset):
    magnitude = jnp.abs(offset)
    distant = 8 + sum(((magnitude >= bound).astype(jnp.int32) for bound in far_bounds))
    signed_part = jnp.where(offset > 0, 16, 0).astype(jnp.int32)
    return signed_part + jnp.where(magnitude < 8, magnitude, distant)


def norm_scale(hidden):
    return lax.rsqrt(jnp.mean(hidden * hidden, axis=-1, keepdims=True) + epsilon)


def norm_backward(grad_normed, hidden, scale, gain):
    weighted = grad_normed * gain
    grad_gain = jnp.sum(grad_normed * hidden * scale, axis=0)
    grad_hidden = scale * weighted - hidden * (scale * scale * scale) * jnp.mean(
        weighted * hidden, axis=-1, keepdims=True
    )
    return (grad_hidden, grad_gain)


def scores_of(query_heads, key_heads, bias, allowed):
    raw_scores = jnp.einsum(
        "rqhd,rkhd->rhqk", query_heads, key_heads, preferred_element_type=jnp.float32
    )
    return jnp.where(allowed, raw_scores + bias[None], -1000000000.0)


def gather_rows(shard):
    return lax.all_gather(shard, ("dp", "seq"), axis=0, tiled=True)


def scatter_sum(parts):
    data_count = lax.axis_size("dp")
    piece_count = lax.axis_size("seq")
    shard_width = parts.shape[0] // (data_count * piece_count)
    split = parts.reshape(data_count, piece_count, shard_width, parts.shape[1])
    half = lax.psum_scatter(split, "dp", scatter_dimension=0, tiled=True)
    return lax.psum_scatter(half, "seq", scatter_dimension=1, tiled=True)[0, 0]


def plain_sums(pairs, extra):
    found = []
    for left, rights in pairs:
        for right in rights:
            part = jnp.einsum("td,tf->df", left, right, preferred_element_type=jnp.float32)
            found.append(scatter_sum(part.astype(jnp.bfloat16)).astype(jnp.float32))
    return found, scatter_sum(extra.astype(jnp.bfloat16)).astype(jnp.float32)


def plain_local(
    hidden_in,
    segment_ids,
    gain_attn,
    w_query,
    w_key,
    w_value,
    w_out,
    rel_table,
    gain_ff,
    w_gate,
    w_up,
    w_down,
    cotangent,
):
    row_count, local_len, model_width = hidden_in.shape
    row_length = segment_ids.shape[1]
    bucket_count, head_count = rel_table.shape
    token_count = row_count * local_len
    data_count = lax.axis_size("dp")
    piece_count = lax.axis_size("seq")
    shard_width = model_width // (data_count * piece_count)
    first_place = lax.axis_index("seq") * local_len
    query_place = first_place + jnp.arange(local_len, dtype=jnp.int32)
    key_place = jnp.arange(row_length, dtype=jnp.int32)
    buckets = bucket_table(key_place[None, :] - query_place[:, None])
    onehot = (buckets[:, :, None] == jnp.arange(bucket_count, dtype=jnp.int32)).astype(jnp.float32)
    bias = jnp.einsum("qkb,bh->hqk", onehot, rel_table.astype(jnp.float32), precision=highest)
    query_segs = lax.dynamic_slice_in_dim(segment_ids, first_place, local_len, 1)
    same_doc = query_segs[:, :, None] == segment_ids[:, None, :]
    visible = (segment_ids[:, None, :] > 0) | (query_place[:, None] == key_place[None, :])[None]
    allowed = (same_doc & visible)[:, None]
    inner = w_query.shape[1]
    ff_width = w_gate.shape[1]
    gains = jnp.pad(jnp.stack([gain_attn, gain_ff], axis=1), ((0, 0), (0, 126)))
    attn_full = gather_rows(jnp.concatenate([w_query, w_key, w_value, w_out.T, gains], axis=1))
    feed_full = gather_rows(jnp.concatenate([w_gate, w_up, w_down.T], axis=1))
    query_full = attn_full[:, :inner]
    key_full = attn_full[:, inner : 2 * inner]
    value_full = attn_full[:, 2 * inner : 3 * inner]
    out_full = attn_full[:, 3 * inner : 4 * inner].T
    gain_one = attn_full[:, 4 * inner]
    gain_two = attn_full[:, 4 * inner + 1]
    gate_full = feed_full[:, :ff_width]
    up_full = feed_full[:, ff_width : 2 * ff_width]
    down_full = feed_full[:, 2 * ff_width :].T
    gain_first = gain_one.astype(jnp.float32)
    residual_in = hidden_in.astype(jnp.float32).reshape(token_count, model_width)
    scale_first = norm_scale(residual_in)
    normed_first = (residual_in * scale_first * gain_first).astype(jnp.bfloat16)
    queries = jnp.dot(normed_first, query_full, preferred_element_type=jnp.float32).astype(
        jnp.bfloat16
    )
    keys_local = jnp.dot(normed_first, key_full, preferred_element_type=jnp.float32).astype(
        jnp.bfloat16
    )
    values_local = jnp.dot(normed_first, value_full, preferred_element_type=jnp.float32).astype(
        jnp.bfloat16
    )
    head_size = inner // head_count
    keys_row, values_row = (
        lax.all_gather(keys_local.reshape(row_count, local_len, inner), "seq", axis=1, tiled=True),
        lax.all_gather(
            values_local.reshape(row_count, local_len, inner), "seq", axis=1, tiled=True
        ),
    )
    query_heads = queries.reshape(row_count, local_len, head_count, head_size)
    key_heads = keys_row.reshape(row_count, row_length, head_count, head_size)
    value_heads = values_row.reshape(row_count, row_length, head_count, head_size)
    logits = scores_of(query_heads, key_heads, bias, allowed)
    row_max = jnp.max(logits, axis=-1, keepdims=True)
    exp_scores = jnp.exp(logits - row_max)
    denominator = jnp.sum(exp_scores, axis=-1, keepdims=True)
    probs_low = (exp_scores / denominator).astype(jnp.bfloat16)
    log_total = row_max + jnp.log(denominator)
    mixed = (
        jnp.einsum("rhqk,rkhd->rqhd", probs_low, value_heads, preferred_element_type=jnp.float32)
        .astype(jnp.bfloat16)
        .reshape(token_count, inner)
    )
    middle = residual_in + jnp.dot(mixed, out_full, preferred_element_type=jnp.float32)
    gain_second = gain_two.astype(jnp.float32)
    scale_second = norm_scale(middle)
    normed_second = (middle * scale_second * gain_second).astype(jnp.bfloat16)
    gate_pre = jnp.dot(normed_second, gate_full, preferred_element_type=jnp.float32)
    up_pre = jnp.dot(normed_second, up_full, preferred_element_type=jnp.float32)
    activated = jax.nn.gelu(gate_pre, approximate=True)
    hidden_mid = (activated * up_pre).astype(jnp.bfloat16)
    block_out = middle + jnp.dot(hidden_mid, down_full, preferred_element_type=jnp.float32)
    gain_second = gain_two.astype(jnp.float32)
    grad_out = cotangent.reshape(token_count, model_width)
    grad_hidden = (
        jnp.einsum("td,fd->tf", grad_out, down_full, preferred_element_type=jnp.float32)
        .astype(jnp.bfloat16)
        .astype(jnp.float32)
    )
    gelu_value, gelu_pull = jax.vjp(lambda value: jax.nn.gelu(value, approximate=True), gate_pre)
    grad_gate = gelu_pull(grad_hidden * up_pre)[0].astype(jnp.bfloat16)
    grad_up = (grad_hidden * gelu_value).astype(jnp.bfloat16)
    grad_normed_second = jnp.einsum(
        "tf,df->td", grad_gate, gate_full, preferred_element_type=jnp.float32
    ) + jnp.einsum("tf,df->td", grad_up, up_full, preferred_element_type=jnp.float32)
    grad_middle_norm, grad_gain_two = norm_backward(
        grad_normed_second, middle, scale_second, gain_second
    )
    grad_middle = grad_out.astype(jnp.float32) + grad_middle_norm
    grad_attended = grad_middle.astype(jnp.bfloat16)
    grad_mixed = jnp.einsum(
        "td,id->ti", grad_attended, out_full, preferred_element_type=jnp.float32
    ).astype(jnp.bfloat16)
    grad_heads = grad_mixed.reshape(row_count, local_len, head_count, head_size)
    logits_again = scores_of(query_heads, key_heads, bias, allowed)
    probs_again = jnp.exp(logits_again - log_total)
    probs_again_low = probs_again.astype(jnp.bfloat16)
    grad_probs = jnp.einsum(
        "rqhd,rkhd->rhqk", grad_heads, value_heads, preferred_element_type=jnp.float32
    )
    row_dot = jnp.sum(probs_again * grad_probs, axis=-1, keepdims=True)
    grad_logits = (probs_again * (grad_probs - row_dot)).astype(jnp.bfloat16)
    grad_bias = jnp.sum(grad_logits.astype(jnp.float32), axis=0)
    grad_table = jnp.einsum("qkb,hqk->bh", onehot, grad_bias, precision=highest)
    grad_queries = (
        jnp.einsum("rhqk,rkhd->rqhd", grad_logits, key_heads, preferred_element_type=jnp.float32)
        .astype(jnp.bfloat16)
        .reshape(token_count, inner)
    )
    grad_keys_row = jnp.einsum(
        "rhqk,rqhd->rkhd", grad_logits, query_heads, preferred_element_type=jnp.float32
    )
    grad_values_row = jnp.einsum(
        "rhqk,rqhd->rkhd", probs_again_low, grad_heads, preferred_element_type=jnp.float32
    )
    grad_keys_part, grad_values_part = (
        lax.psum_scatter(
            grad_keys_row.astype(jnp.bfloat16), "seq", scatter_dimension=1, tiled=True
        ).astype(jnp.float32),
        lax.psum_scatter(
            grad_values_row.astype(jnp.bfloat16), "seq", scatter_dimension=1, tiled=True
        ).astype(jnp.float32),
    )
    grad_keys = grad_keys_part.astype(jnp.bfloat16).reshape(token_count, inner)
    grad_values = grad_values_part.astype(jnp.bfloat16).reshape(token_count, inner)
    grad_normed_first = jnp.einsum(
        "ti,di->td", grad_queries, query_full, preferred_element_type=jnp.float32
    )
    grad_normed_first = grad_normed_first + jnp.einsum(
        "ti,di->td", grad_keys, key_full, preferred_element_type=jnp.float32
    )
    grad_normed_first = grad_normed_first + jnp.einsum(
        "ti,di->td", grad_values, value_full, preferred_element_type=jnp.float32
    )
    grad_first, grad_gain_one = norm_backward(
        grad_normed_first, residual_in, scale_first, gain_first
    )
    grad_input = grad_middle + grad_first
    device_count = data_count * piece_count
    table_size = bucket_count * head_count
    table_rows = -(-table_size // shard_width)
    table_block = jnp.pad(grad_table.reshape(-1), (0, table_rows * shard_width - table_size))
    table_block = jnp.broadcast_to(
        table_block.reshape(1, table_rows, shard_width), (device_count, table_rows, shard_width)
    )
    gain_block = jnp.stack([grad_gain_one, grad_gain_two], axis=0)
    gain_block = gain_block.reshape(2, device_count, shard_width).transpose(1, 0, 2)
    extra = jnp.concatenate([table_block, gain_block], axis=1).transpose(0, 2, 1)
    extra = extra.reshape(model_width, table_rows + 2)
    extra = jnp.pad(extra, ((0, 0), (0, -(table_rows + 2) % 128)))
    pairs = (
        (normed_second, (grad_gate, grad_up)),
        (grad_out, (hidden_mid,)),
        (grad_attended, (mixed,)),
        (normed_first, (grad_queries, grad_keys, grad_values)),
    )
    (gate_sum, up_sum, down_sum, out_sum, query_sum, key_sum, value_sum), extra_sum = plain_sums(
        pairs, extra
    )
    table_total = extra_sum[:, :table_rows].T.reshape(-1)[:table_size]
    table_total = table_total.reshape(bucket_count, head_count)
    grad_gain_one_shard = extra_sum[:, table_rows]
    grad_gain_two_shard = extra_sum[:, table_rows + 1]
    return (
        block_out.reshape(row_count, local_len, model_width),
        grad_input.reshape(row_count, local_len, model_width),
        grad_gain_one_shard,
        query_sum,
        key_sum,
        value_sum,
        out_sum.T,
        table_total,
        grad_gain_two_shard,
        gate_sum,
        up_sum,
        down_sum.T,
    )


gelu_c=0.7978845608028654

def peers_of():
    dp=lax.axis_index("dp"); z=lax.axis_index("seq")
    c=lax.rem(dp,2); x=lax.rem(dp//2,2); y=dp//4
    return dp,z,c,x,y

def remote(src,dst,ss,rs,dev):
    return pltpu.make_async_remote_copy(src_ref=src,dst_ref=dst,send_sem=ss,recv_sem=rs,device_id=dev,device_id_type=mesh_ids)

def dot(a,b):
    return jnp.dot(a,b,preferred_element_type=jnp.float32)

def dot_nt(a,b):
    return lax.dot_general(a,b,(((1,),(1,)),((),())),preferred_element_type=jnp.float32)

def lanes(shape):
    return lax.broadcasted_iota(jnp.int32,shape,len(shape)-1)

def greet(devices):
    bar=pltpu.get_barrier_semaphore()
    for d in devices: pl.semaphore_signal(bar,inc=1,device_id=d,device_id_type=mesh_ids)
    pl.semaphore_wait(bar,len(devices))

low=jnp.bfloat16
f32=jnp.float32

h_parts=4
across_first=2
def forward_kernel(ff_steps, w_q, w_k, w_v, w_o, w_g, w_u, w_d, gains, hid, cot, segr, segc, base,
                   w1, w2, w, lt_o, hdg_o, q_o, kk_o, vv_o, mx_o, lse_o, gnf_o, yy_o, gs_o, segr_o, segc_o, mid_o, cot_o,
                   hrow, cotv, sr, sc, wa, wf, qq, kk, vv, mx, lse, bias, part, mid, n2, hd, yy, lt, gs, r1, wp,
                   s0s, s0r, l0, s1s, s1r, s2s, s2r, s3s, s3r, hs, hr, xs, xr, ll, lo):
    cols=[(0,768),(768,896)]+[(1664+512*i,512) for i in range(3*ff_steps)]
    n=len(cols)
    dp,z,c,x,y=peers_of()
    q=dp//2; qx=2*y+1-x; qy=lax.rem(q+2,4); qd=3-q
    sib=(dp+1-2*c,z); dx=(2*qx+c,z); dy=(2*qy+c,z); dxy=(dx,dy)
    zb=lax.rem(z,2); pe=z+1-2*zb; mo=2-z//2; zo=2-2*(z//2)
    inner=(z==1)|(z==2); outer=(z==0)|(z==3)
    dpe=(dp,pe); dmo=(dp,mo)
    greet([sib,dx,dy]+[(dp,lax.rem(z+k,4)) for k in (1,2,3)])
    def cs(t): return pl.ds(cols[t][0],cols[t][1])
    def wr(t): return (w1,w2)[t] if t<2 else w.at[t-2]
    def s0(t,recv=False):
        return remote(wp.at[1-c,:,cs(t)], wr(t).at[(dp+1-2*c) if recv else dp,z], s0s.at[t], s0r.at[t], sib)
    def keep(t): return pltpu.make_async_copy(wp.at[c,:,cs(t)], wr(t).at[dp,z], l0.at[t])
    across=set(range(n-across_first,n))
    def group(t): return pl.ds(0,8) if t in across else pl.ds(2*q,2)
    def span(t): return z if t in across else pl.ds(0,4)
    def s1a(t,recv=False):
        r=wr(t).at[group(t), pe if recv else z]
        return remote(r,r,s1s.at[t,0],s1r.at[t,0],dpe)
    def s1b(t):
        r=wr(t).at[group(t), z]
        return remote(r,r,s1s.at[t,1],s1r.at[t,1+zb],dmo)
    def s1bw(t,k):
        r=wr(t).at[group(t), zo+k]
        return remote(r,r,s1s.at[t,1],s1r.at[t,1+k],dmo)
    def s1c(t):
        r=wr(t).at[group(t), pl.ds(zo,2)]
        return remote(r,r,s1s.at[t,2],s1r.at[t,3],dpe)
    def s2(t,a,recv=False):
        r=wr(t).at[pl.ds(2*((qx,qy)[a] if recv else q),2), span(t)]
        return remote(r,r,s2s.at[t,a],s2r.at[t,a],dxy[a])
    def s3(t,a,recv=False):
        r=wr(t).at[2*(qd if recv else (qy,qx)[a])+a, span(t)]
        return remote(r,r,s3s.at[t,a],s3r.at[t,a],dxy[a])
    hp=hrow.shape[2]//h_parts
    def ht(p): return pl.ds(p*hp,hp)
    def ha(p,recv=False): return remote(hid.at[ht(p)],hrow.at[c,pe if recv else z,ht(p)],hs.at[p,0],hr.at[p,0],dpe)
    def hb(p): return remote(hid.at[ht(p)],hrow.at[c,z,ht(p)],hs.at[p,1],hr.at[p,1+zb],dmo)
    def hbw(p,k): return remote(hid.at[ht(p)],hrow.at[c,zo+k,ht(p)],hs.at[p,1],hr.at[p,1+k],dmo)
    def hc(p):
        r=hrow.at[c,pl.ds(zo,2),ht(p)]
        return remote(r,r,hs.at[p,2],hr.at[p,3],dpe)
    done=set()
    def once(*k):
        if k in done: return False
        done.add(k); return True
    def start1(t):
        if t<n and t not in across and once(1,t):
            keep(t).wait(); s0(t,True).wait_recv()
            s1a(t).start(); s1b(t).start()
    def across1(t):
        keep(t).wait(); s0(t,True).wait_recv()
        for a in range(2): s2(t,a).start()
    def across2(t):
        for a in range(2): s2(t,a,True).wait_recv()
        for a in range(2): s3(t,a).start()
    def across3(t):
        for a in range(2): s3(t,a,True).wait_recv()
        s1a(t).start(); s1b(t).start()
    def across4(t):
        @pl.when(inner)
        def _():
            s1bw(t,0).wait_recv(); s1bw(t,1).wait_recv(); s1c(t).start()
    def across5(t):
        s1a(t,True).wait_recv()
        @pl.when(outer)
        def _(): s1c(t).wait_recv()
    def forward(t):
        if t<n and t not in across and once(5,t):
            @pl.when(inner)
            def _():
                s1bw(t,0).wait_recv(); s1bw(t,1).wait_recv(); s1c(t).start()
    def start2(t):
        forward(t)
        if t<n and t not in across and once(2,t):
            s1a(t,True).wait_recv()
            @pl.when(outer)
            def _(): s1c(t).wait_recv()
            for a in range(2): s2(t,a).start()
    def start3(t):
        if 0<=t<n and t not in across and once(3,t):
            for a in range(2): s2(t,a,True).wait_recv()
            for a in range(2): s3(t,a).start()
    def finish(t):
        if 0<=t<n and t not in across and once(4,t):
            for a in range(2): s3(t,a,True).wait_recv()
    def advance(t):
        for u in range(t+4): start1(u)
        for f,u in ((forward,t+1),(start2,t),(start3,t-1),(finish,t-2)):
            for v in range(u+1): f(v)
    def h_go(p): ha(p).start(); hb(p).start()
    def h_on(p):
        @pl.when(inner)
        def _():
            hbw(p,0).wait_recv(); hbw(p,1).wait_recv(); hc(p).start()
    for h in range(2):
        for i,v in enumerate((w_q,w_k,w_v,w_o)): wp[h,:,384*i:384*i+384]=v[:,384*h:384*h+384]
        wp[h,:,1536:1664]=gains[...]
        for j in range(ff_steps):
            for i,v in enumerate((w_g,w_u,w_d)):
                a=1664+1536*j+512*i; f=512*(ff_steps*h+j); g=min(512,v.shape[1]-f)
                if g>0: wp[h,:,a:a+g]=v[:,f:f+g]
                if g<512: wp[h,:,a+max(g,0):a+512]=jnp.zeros((48,512-max(g,0)),low)
    keep_h=pltpu.make_async_copy(hid,hrow.at[c,z],ll.at[0]); keep_h.start()
    keep_c=pltpu.make_async_copy(cot,cotv.at[c],ll.at[1]); keep_c.start()
    keep_r=pltpu.make_async_copy(segr,sr.at[c],ll.at[2]); keep_r.start()
    keep_s=pltpu.make_async_copy(segc,sc.at[c],ll.at[3]); keep_s.start()
    for t in [*range(3),*sorted(across)]: s0(t).start(); keep(t).start()
    give_h=[remote(hid,hrow.at[c,z],xs.at[3],xr.at[3],sib)]; give_h[0].start()
    give_c=remote(cot,cotv.at[c],xs.at[0],xr.at[0],sib); give_c.start()
    give_r=remote(segr,sr.at[c],xs.at[1],xr.at[1],sib); give_r.start()
    give_s=remote(segc,sc.at[c],xs.at[2],xr.at[2],sib); give_s.start()
    for t in range(3,n-across_first): s0(t).start(); keep(t).start()
    start1(0); start1(1); start1(2); h_go(0)
    for t in sorted(across): across1(t)
    forward(0); start2(0); forward(1); start2(1); forward(2)
    h_on(0); start1(3); h_go(1)
    for t in sorted(across): across2(t)
    start3(0); start2(2)
    keep_h.wait(); keep_c.wait(); keep_r.wait(); keep_s.wait()
    remote(segr,sr.at[1-c],xs.at[1],xr.at[1],sib).wait_recv()
    remote(segc,sc.at[1-c],xs.at[2],xr.at[2],sib).wait_recv()
    remote(cot,cotv.at[1-c],xs.at[0],xr.at[0],sib).wait_recv()
    remote(hid,hrow.at[1-c,z],xs.at[3],xr.at[3],sib).wait_recv()
    start3(1); forward(3); h_on(1); start1(4); h_go(2)
    finish(0); finish(1)
    load_a=[pltpu.make_async_copy(w1,wa.at[:,:,:,pl.ds(0,768)],ll.at[4]),pltpu.make_async_copy(w2,wa.at[:,:,:,pl.ds(768,896)],ll.at[11])]
    for l in load_a: l.start()
    start3(2); start2(3); forward(4); h_on(2); start1(5); h_go(3)
    for l in load_a: l.wait()
    def wcol(a,b): return wa[:,:,:,a:b].reshape(1536,b-a)
    pick=(lanes((8,128))==lax.broadcasted_iota(jnp.int32,(8,128),0)).astype(low)
    gs[...]=dot_nt(pick,wcol(1536,1664))
    def transpose_cot(i,_):
        lt[2,:,pl.ds(pl.multiple_of(i*128,128),128)]=cotv[i//2,pl.ds(pl.multiple_of(lax.rem(i,2)*128,128),128),:].astype(f32).T.astype(low)
        return 0
    lax.fori_loop(0,4,transpose_cot,0)
    def normed(v,row):
        s=lax.rsqrt(jnp.mean(v*v,axis=-1,keepdims=True)+epsilon)
        return v*s*gs[row:row+1,:]
    def queries(i,_):
        a=pl.ds(pl.multiple_of(lax.rem(i,2)*128,128),128)
        v=normed(hrow[i//2,z,a,:].astype(f32),0)
        d=pl.ds(pl.multiple_of(i*128,128),128)
        qq[d,:]=dot(v.astype(low),wcol(0,384)).astype(low)
        lt[0,:,d]=v.T.astype(low)
        return 0
    lax.fori_loop(0,4,queries,0)
    start2(4); start3(3); finish(2); forward(5); h_on(3); start2(5); start3(4)
    for p in range(h_parts):
        ha(p,True).wait_recv()
        @pl.when(outer)
        def _(): hc(p).wait_recv()
    for k in (1,2,3):
        r=hrow.at[c,lax.rem(z+k,4)]
        g=remote(r,r,xs.at[6+k],xr.at[6+k],sib); g.start(); give_h.append(g)
    def keys_of(r):
        def body(i,_):
            a=pl.ds(pl.multiple_of(lax.rem(i,2)*128,128),128)
            v=normed(hrow[r,i//2,a,:].astype(f32),0).astype(low)
            d=pl.ds(pl.multiple_of(i*128,128),128)
            kk[r,d,:]=dot(v,wcol(384,768)).astype(low)
            vv[r,d,:]=dot(v,wcol(768,1152)).astype(low)
            return 0
        lax.fori_loop(0,8,body,0)
    keys_of(c)
    for k in (1,2,3):
        r=hrow.at[1-c,lax.rem(z+k,4)]
        remote(r,r,xs.at[6+k],xr.at[6+k],sib).wait_recv()
    advance(5)
    keys_of(1-c)
    advance(6)
    for t in sorted(across)[:1]: across3(t)
    for h in range(6):
        pair=pl.ds(128*(h//2),128); odd=h%2
        bias[...]=pltpu.roll(jnp.broadcast_to(base[h:h+1,:],(256,1280)),1024,1,stride=1,stride_axis=0)
        def attend(i,_):
            r=i//2; d=pl.ds(pl.multiple_of(i*128,128),128)
            a=pl.ds(pl.multiple_of(lax.rem(i,2)*128,128),128)
            mine=(lanes((128,128))>=64) if odd else (lanes((128,128))<64)
            qh=jnp.where(mine,qq[d,pair].astype(f32),0.0).astype(low)
            s=dot_nt(qh,kk[r,:,pair])+bias[a,0:1024]
            s=jnp.where(sc[r,a,0:1]==sr[r,0:1,:],s,-1000000000.0)
            m=jnp.max(s,axis=-1,keepdims=True)
            e=jnp.exp(s-m)
            l=jnp.sum(e,axis=-1,keepdims=True)
            p=(e*(1.0/l)).astype(low)
            o=dot(p,vv[r,:,pair])
            if odd: o=jnp.where(mine,o,mx[d,pair].astype(f32))
            mx[d,pair]=o.astype(low)
            lse[r,a,:]=jnp.where(lanes((128,128))==h,m+jnp.log(l),lse[r,a,:]) if h else jnp.broadcast_to(m+jnp.log(l),(128,128))
            return 0
        lax.fori_loop(0,4,attend,0)
        if h in (1,3): advance(7+h//2)
        if h==3:
            for t in sorted(across)[:1]: across4(t)
            for t in sorted(across)[1:]: across3(t)
    def project(i,_):
        part[i//2,pl.ds(pl.multiple_of(lax.rem(i,2)*128,128),128),:]=dot_nt(mx[pl.ds(pl.multiple_of(i*128,128),128),:],wcol(1152,1536))
        return 0
    lax.fori_loop(0,4,project,0)
    give_p=remote(part,r1,xs.at[4],xr.at[4],sib); give_p.start()
    advance(9)
    outs=[pltpu.make_async_copy(a,b,lo.at[i]) for i,(a,b) in enumerate(((qq,q_o),(kk,kk_o),(vv,vv_o),(mx,mx_o),(lse,lse_o),(sr,segr_o),(sc,segc_o),(cotv,cot_o)))]
    for o in outs: o.start()
    give_p.wait_recv()
    def middle(i,_):
        a=pl.ds(pl.multiple_of(lax.rem(i,2)*128,128),128); r=i//2
        d=pl.ds(pl.multiple_of(i*128,128),128)
        v=hrow[r,z,a,:].astype(f32)+(part[r,a,:]+r1[r,a,:])
        mid[r,a,:]=v
        v=normed(v,1)
        n2[d,:]=v.astype(low)
        lt[1,:,d]=v.T.astype(low)
        return 0
    lax.fori_loop(0,4,middle,0)
    give_p.wait_send()
    give_lt=pltpu.make_async_copy(lt,lt_o,ll.at[5]); give_lt.start()
    give_mid=pltpu.make_async_copy(mid,mid_o,ll.at[12]); give_mid.start()
    gs_o[...]=gs[...]
    advance(10)
    for t in sorted(across)[1:]: across4(t)
    hout=[]
    for j in range(ff_steps):
        if j:
            for t in range(4+3*j,7+3*j) if j==ff_steps-1 else [10+j]: advance(t)
            if j==ff_steps-1:
                for t in sorted(across): across5(t)
        loads=[pltpu.make_async_copy(w.at[3*j+i],wf.at[i],ll.at[6+i]) for i in range(3)]
        for l in loads: l.start()
        b=j%2
        if j>=2: hout[j-2].wait()
        for l in loads: l.wait()
        def feed(i,_):
            d=pl.ds(pl.multiple_of(i*256,256),256)
            v=n2[d,:]
            wg=wf[0].reshape(1536,512); wu=wf[1].reshape(1536,512); wd=wf[2].reshape(1536,512)
            gate=dot(v,wg); up=dot(v,wu)
            gh=dot(cotv[i],wd).astype(low).astype(f32)
            u2=gate*gate
            th=jnp.tanh(gelu_c*(gate+0.044715*(gate*u2)))
            act=0.5*gate*(1.0+th)
            slope=0.5*(1.0+th)+0.5*gate*(1.0-th*th)*(gelu_c*(1.0+3*0.044715*u2))
            hm=(act*up).astype(low); dg=(gh*up*slope).astype(low); du=(gh*act).astype(low)
            hd[b,0,d,:]=hm; hd[b,1,d,:]=dg; hd[b,2,d,:]=du
            yp=dot_nt(hm,wd); gp=dot_nt(dg,wg)+dot_nt(du,wu)
            if j: yp=yp+yy[i]; gp=gp+part[i]
            yy[i]=yp; part[i]=gp
            return 0
        lax.fori_loop(0,2,feed,0)
        o=pltpu.make_async_copy(hd.at[b],hdg_o.at[:,:,pl.ds(512*j,512)],lo.at[8+b]); o.start(); hout.append(o)
    give_m=[pltpu.make_async_copy(part,gnf_o,ll.at[9]),pltpu.make_async_copy(yy,yy_o,ll.at[10])]
    for g in give_m: g.start()
    for o in outs+hout[-2:]: o.wait()
    give_lt.wait(); give_mid.wait()
    for g in give_m: g.wait()
    give_c.wait_send(); give_r.wait_send(); give_s.wait_send()
    for g in give_h: g.wait_send()
    for p in range(h_parts):
        ha(p).wait_send(); hb(p).wait_send()
        @pl.when(inner)
        def _(): hc(p).wait_send()
    for t in range(n):
        s0(t).wait_send()
        s1a(t).wait_send(); s1b(t).wait_send()
        @pl.when(inner)
        def _(): s1c(t).wait_send()
        for a in range(2): s2(t,a).wait_send(); s3(t,a).wait_send()

def forward_call(weights, gains, hid, cot, segr, segc, base, ff_steps, cid=0):
    n=2+3*ff_steps
    S=jax.ShapeDtypeStruct; V=pltpu.VMEM; D=pltpu.SemaphoreType.DMA
    fw=512*ff_steps
    hbm=pl.BlockSpec(memory_space=pltpu.HBM); vm=pl.BlockSpec(memory_space=pltpu.VMEM)
    outs=(S((8,4,48,768),low),S((8,4,48,896),low),S((3*ff_steps,8,4,48,512),low),S((3,1536,512),low),S((3,512,fw),low),S((512,384),low),S((2,1024,384),low),S((2,1024,384),low),
          S((512,384),low),S((2,256,128),f32),S((2,256,1536),f32),S((2,256,1536),f32),S((8,1536),f32),S((2,8,1024),f32),S((2,256,128),f32),S((2,256,1536),f32),S((2,256,1536),low))
    ospec=[hbm]*17; ospec[12]=vm
    scratch=[V((2,4,256,1536),low),V((2,256,1536),low),V((2,8,1024),f32),V((2,256,128),f32),V((8,4,48,1664),low),V((3,8,4,48,512),low),
             V((512,384),low),V((2,1024,384),low),V((2,1024,384),low),V((512,384),low),V((2,256,128),f32),V((256,1280),f32),
             V((2,256,1536),f32),V((2,256,1536),f32),V((512,1536),low),V((2,3,512,512),low),V((2,256,1536),f32),V((3,1536,512),low),V((8,1536),f32),
             V((2,256,1536),f32),V((2,48,1664+1536*ff_steps),low),
             D((n,)),D((n,)),D((n,)),D((n,3)),D((n,4)),D((n,2)),D((n,2)),D((n,2)),D((n,2)),D((h_parts,3)),D((h_parts,4)),D((10,)),D((10,)),D((13,)),D((10,))]
    return pl.pallas_call(functools.partial(forward_kernel,ff_steps),out_shape=outs,
        in_specs=[vm]*8+[hbm]*4+[vm],out_specs=tuple(ospec),scratch_shapes=scratch,
        compiler_params=pltpu.CompilerParams(collective_id=cid,has_side_effects=True,vmem_limit_bytes=62*2**20))(*weights,gains,hid,cot,segr,segc,base)

def dot_tn(a,b):
    return lax.dot_general(a,b,(((0,),(0,)),((),())),preferred_element_type=jnp.float32)

part_slots=2
sum_slots=3
lag=6
def backward_kernel(chunks, ff_steps, w1, w2, lt_h, hdg, q_h, kk_h, vv_h, mx_h, lse_h, gnf_h, yy_h, mid_h, cot_h, segr_h, segc_h, hid_h, base, gains,
                    og, ou, od, oo, oq, ok, ov, oe, gin_o, bo_o, xg, xy, *rest):
    n=len(chunks)
    ra1=rest[0:n]; rb1=rest[n:2*n]; ra2=rest[2*n:3*n]; rb2=rest[3*n:4*n]; rz=rest[4*n:5*n]
    (fin,p,lt,gat,rbuf,wa,qq,kk,vv,mx,gm,lse,sr,sc,bias,dbias,dq,acc,dkv,rka,rkb,rkc,dk,dv,part,r3,hid,dtab,ext,cb,
     ll,lr,lo,s1,v1,s2,v2,s3,v3,s4,v4,ks,kr,xs,xr,lb)=rest[5*n:]
    dp,z,c,x,y=peers_of()
    sib=(dp+1-2*c,z); dx=(dp+2-4*x,z); dy=(lax.rem(dp+4,8),z)
    zs=[lax.rem(z+k,4) for k in (1,2,3)]; dz=[(dp,zz) for zz in zs]
    zb=lax.rem(z,2); pe=z+1-2*zb; mo=2-z//2; zo=2-2*(z//2)
    inner=(z==1)|(z==2); outer=(z==0)|(z==3)
    def ka(pp,recv=False): return remote(dkv.at[pp,pe],rka.at[pp],ks.at[pp,0],kr.at[pp,0],(dp,pe))
    def kc(pp): return remote(dkv.at[pp,pl.ds(zo,2)],rkc.at[pp],ks.at[pp,1],kr.at[pp,1],(dp,pe))
    def kb(pp,k): return remote(dkv.at[pp,zo+k],rkb.at[pp],ks.at[pp,2+k],kr.at[pp,2],(dp,zo+k))
    def relay(pp):
        @pl.when(inner)
        def _():
            kc(pp).wait_recv()
            for k in range(2):
                for j in range(2):
                    for r in range(2):
                        dkv[pp,zo+k,j,r]=(dkv[pp,zo+k,j,r].astype(f32)+rkc[pp,k,j,r].astype(f32)).astype(low)
                kb(pp,k).start()
    loads=[pltpu.make_async_copy(a,b,ll.at[i]) for i,(a,b) in enumerate((
        (lt_h.at[pl.ds(1,2)],lt),(w2.at[:,:,:,pl.ds(384,384)],wa.at[:,:,:,pl.ds(0,384)]),(q_h,qq),(kk_h,kk),(vv_h,vv),(mx_h,mx),(lse_h,lse),(segr_h,sr),(segc_h,sc),(hid_h,hid)))]
    for l in loads: l.start()
    slots=rbuf.shape[0]
    def fetch(t):
        kind,i,j=chunks[t][3]
        return pltpu.make_async_copy(hdg.at[i,:,pl.ds(512*j,512)],rbuf.at[t%slots],lr.at[t])
    feeds=[t for t in range(n) if chunks[t][3][0]=="feed"]
    for t in feeds[:slots]: fetch(t).start()
    greet([sib,dx,dy]+dz)
    load_n=pltpu.make_async_copy(lt_h.at[0],lt.at[1],ll.at[14])
    c1={}; c2={}; c3={}; c4={}; done=set()
    def once(*k):
        if k in done: return False
        done.add(k); return True
    def stage1(t):
        left,off,wd,src=chunks[t][:4]; b=t%part_slots
        if t>=part_slots:
            for d in c1[t-part_slots]: d.wait_send()
        if src[0]=="feed":
            fetch(t).wait()
            right=lambda: rbuf[t%slots]
        else:
            right=(lambda: mx[...],lambda: dq[...],lambda: dk[...],lambda: dv[...],None)[src[1]]
        if src==("ref",1,0): load_n.wait()
        if right is None:
            p[b,:,:,:,:,:,0:wd]=ext[...].T.astype(low).reshape(2,2,2,4,48,wd)
        else:
            def body(i,_):
                rs=pl.ds(pl.multiple_of(i*192,192),192)
                lhs=gat[rs,:] if left==3 else lt[left,rs,:]
                p[b,i//4,lax.rem(i//2,2),lax.rem(i,2),:,:,0:wd]=dot(lhs,right()).astype(low).reshape(4,48,wd)
                return 0
            lax.fori_loop(0,8,body,0)
        if t==feeds[-1]:
            load_n.start()
        if src[0]=="feed" and t+slots<n and chunks[t+slots][3][0]=="feed": fetch(t+slots).start()
        a=remote(p.at[b,:,1-x,0,:,:,pl.ds(0,wd)],ra1[t],s1.at[t,0],v1.at[t,0],dx)
        e=remote(p.at[b,1-y,:,1,:,:,pl.ds(0,wd)],rb1[t],s1.at[t,1],v1.at[t,1],dy)
        a.start(); e.start(); c1[t]=(a,e)
    def stage2(t):
        wd=chunks[t][2]; b=t%part_slots
        for d in c1[t]: d.wait_recv()
        def body(i,_):
            h=i//4; zz=lax.rem(i,4)
            ra1[t][h,zz]=ra1[t][h,zz]+p[b,h,x,0,zz,:,0:wd]
            rb1[t][h,zz]=rb1[t][h,zz]+p[b,y,h,1,zz,:,0:wd]
            return 0
        lax.fori_loop(0,8,body,0)
        a=remote(ra1[t].at[1-y],ra2[t],s2.at[t,0],v2.at[t,0],dy)
        e=remote(rb1[t].at[1-x],rb2[t],s2.at[t,1],v2.at[t,1],dx)
        a.start(); e.start(); c2[t]=(a,e)
    def stage3(t):
        for d in c2[t]: d.wait_recv()
        def body(zz,_):
            ra2[t][zz]=ra2[t][zz]+ra1[t][y,zz]
            rb2[t][zz]=rb2[t][zz]+rb1[t][x,zz]
            return 0
        lax.fori_loop(0,4,body,0)
        cs=[]
        for k in range(3):
            cs.append(remote(ra2[t].at[zs[k]],rz[t].at[k,0],s3.at[t,k,0],v3.at[t,k,0],dz[k]))
            cs.append(remote(rb2[t].at[zs[k]],rz[t].at[k,1],s3.at[t,k,1],v3.at[t,k,1],dz[k]))
        for d in cs: d.start()
        c3[t]=cs
    def place(t,pair,acts,half):
        o,offset,width,total=chunks[t][4]
        o=(og,ou,od,oo,oq,ok,ov,oe)[o]
        last=total-(width[1]+offset)
        def act(size):
            cols=pl.ds(pl.multiple_of(half*width[1]+offset,128),size)
            for m,how in zip(pair(None,size,cols,o),acts):
                if how: getattr(m,how)()
        if last>=width[0]: act(width[0])
        else:
            @pl.when(half==0)
            def _(): act(width[0])
            if last>0:
                @pl.when(half==1)
                def _(): act(last)
    def drain(t):
        place(t,lambda _,width,cols,o: (
            remote(fin.at[0,0,:,pl.ds(0,width)],o.at[:,cols],s4.at[t],v4.at[t],sib),
            pltpu.make_async_copy(fin.at[0,0,:,pl.ds(0,width)],o.at[:,cols],lo.at[t])),("wait_send","wait"),c)
    def arrive(t):
        place(t,lambda _,width,cols,o: (remote(fin.at[0,0,:,pl.ds(0,width)],o.at[:,cols],s4.at[t],v4.at[t],sib),),("wait_recv",),1-c)
    def stage4(t):
        wd=chunks[t][2]
        for d in c3[t]: d.wait_recv()
        f0=ra2[t][z].astype(f32); f1=rb2[t][z].astype(f32)
        for k in range(3):
            f0=f0+rz[t][k,0].astype(f32); f1=f1+rz[t][k,1].astype(f32)
        b=t%sum_slots
        if t>=sum_slots:
            drain(t-sum_slots)
        fin[b,0,:,0:wd]=f0; fin[b,1,:,0:wd]=f1
        place(t,lambda _,width,cols,o: (
            remote(fin.at[b,1-c,:,pl.ds(0,width)],o.at[:,cols],s4.at[t],v4.at[t],sib),
            pltpu.make_async_copy(fin.at[b,c,:,pl.ds(0,width)],o.at[:,cols],lo.at[t])),("start","start"),c)
    def step(s):
        for f,t in ((stage2,s),(stage1,s+2),(stage3,s-1),(stage4,s-lag)):
            if 0<=t<n and once(f.__name__,t): f(t)
    give_g=remote(gnf_h,xg,xs.at[1],xr.at[1],sib); give_g.start()
    give_y=remote(yy_h.at[1-c],xy,xs.at[2],xr.at[2],sib); give_y.start()
    loads[0].wait()
    stage1(0); stage1(1); once("stage1",0); once("stage1",1)
    for l in loads[1:]: l.wait()
    def wcol(a,b): return wa[:,:,:,a:b].reshape(1536,b-a)
    give_g.wait_recv()
    total=jnp.zeros((1,1536),f32)
    for i in range(4):
        r=i//2; a=pl.ds(128*(i%2),128); d=pl.ds(128*i,128)
        first=part.at[0,pl.ds(0,128)]; second=part.at[0,pl.ds(128,128)]; third=part.at[1,pl.ds(0,128)]
        moves=[pltpu.make_async_copy(f,g,lb.at[k]) for k,(f,g) in enumerate(((mid_h.at[r,a],first),(gnf_h.at[r,a],second),(xg.at[r,a],third),(cot_h.at[r,a],cb)))]
        for m in moves: m.start()
        for m in moves: m.wait()
        v=part[0,0:128,:]; gn=part[0,128:256,:]+part[1,0:128,:]
        s=lax.rsqrt(jnp.mean(v*v,axis=-1,keepdims=True)+epsilon)
        wg=gn*gains[1:2,:]
        g=cb[...].astype(f32)+(s*wg-v*(s*s*s)*jnp.mean(wg*v,axis=-1,keepdims=True))
        total=total+jnp.where(c==r,1.0,0.0)*jnp.sum(gn*v*s,axis=0,keepdims=True)
        part[1,128:256,:]=g
        @pl.when(c==r)
        def _():
            back=pltpu.make_async_copy(part.at[1,pl.ds(128,128)],gin_o.at[a],lb.at[4]); back.start(); back.wait()
        gat[:,d]=g.T.astype(low)
        gm[d,:]=dot(g.astype(low),wcol(0,384)).astype(low)
    ext[...]=jnp.zeros((128,1536),f32)
    def spread(v,row):
        upper=v.astype(low)
        ext[row:row+8,:]=upper.astype(f32)
        ext[row+8:row+16,:]=v-upper.astype(f32)
    spread(jnp.broadcast_to(total,(8,1536)),32)
    load_w=[pltpu.make_async_copy(w1,wa.at[:,:,:,pl.ds(0,768)],ll.at[13]),pltpu.make_async_copy(w2.at[:,:,:,pl.ds(0,384)],wa.at[:,:,:,pl.ds(768,384)],ll.at[15])]
    for l in load_w: l.start()
    step(0)
    dbias[...]=jnp.zeros((256,1280),f32)
    dtab[...]=jnp.zeros((8,1280),f32)
    at=1
    for h in range(6):
        odd=h%2; pair=pl.ds(128*(h//2),128); pp=h//2
        bias[...]=pltpu.roll(jnp.broadcast_to(base[h:h+1,:],(256,1280)),1024,1,stride=1,stride_axis=0)
        if not odd: acc[...]=jnp.zeros((2,2,1024,128),f32)
        def attend(i,_):
            r=i//2; d=pl.ds(pl.multiple_of(i*128,128),128)
            a=pl.ds(pl.multiple_of(lax.rem(i,2)*128,128),128)
            mine=(lanes((128,128))>=64) if odd else (lanes((128,128))<64)
            qh=jnp.where(mine,qq[d,pair].astype(f32),0.0).astype(low)
            gh=jnp.where(mine,gm[d,pair].astype(f32),0.0).astype(low)
            s=dot_nt(qh,kk[r,:,pair])+bias[a,0:1024]
            s=jnp.where(sc[r,a,0:1]==sr[r,0:1,:],s,-1000000000.0)
            pr=jnp.exp(s-lse[r,a,h:h+1])
            gp=dot_nt(gh,vv[r,:,pair])
            gl=(pr*(gp-jnp.sum(pr*gp,axis=-1,keepdims=True))).astype(low)
            wide=gl.astype(f32)
            dbias[a,0:1024]=wide+jnp.where(r==0,0.0,1.0)*dbias[a,0:1024]
            g=jnp.where(mine,dot(gl,kk[r,:,pair]),0.0)
            if odd: g=g+dq[d,pair].astype(f32)
            dq[d,pair]=g.astype(low)
            acc[0,r]=acc[0,r]+dot_tn(gl,qh)
            acc[1,r]=acc[1,r]+dot_tn(pr.astype(low),gh)
            return 0
        lax.fori_loop(0,4,attend,0)
        m=128
        v=dbias[0:128,:]+pltpu.roll(dbias[128:256,:],1280-128,1)
        while m>1:
            m//=2
            v=v[0:m]+pltpu.roll(v[m:2*m],1280-m,1)
        dtab[h:h+1,:]=pltpu.roll(v,256,1)
        if odd:
            for j in range(2):
                for r in range(2):
                    for zz in range(4):
                        dkv[pp,zz,j,r]=acc[j,r,256*zz:256*zz+256,:].astype(low)
            ka(pp).start()
            @pl.when(outer)
            def _(): kc(pp).start()
            step(at); at+=1
            if pp: relay(pp-1)
    tab=dtab[...]
    high=tab.astype(low); rest1=tab-high.astype(f32); mid1=rest1.astype(low); last=(rest1-mid1.astype(f32)).astype(low)
    shift=lax.broadcasted_iota(jnp.int32,(1280,128),0)-256-256*z
    spots=jnp.where(bucket_table(shift)==lanes((1280,128)),1.0,0.0).astype(low)
    tile=jnp.where(lax.rem(lanes((128,1536)),48)==lax.broadcasted_iota(jnp.int32,(128,1536),0),1.0,0.0).astype(low)
    found=dot(high,spots)+dot(mid1,spots)+dot(last,spots)
    upper=found.astype(low)
    ext[0:8,:]=dot(upper,tile)
    ext[8:16,:]=dot((found-upper.astype(f32)).astype(low),tile)
    give_y.wait_recv()
    for i in range(2):
        a=pl.ds(128*i,128)
        first=part.at[0,pl.ds(0,128)]; second=part.at[0,pl.ds(128,128)]; third=part.at[1,pl.ds(0,128)]
        moves=[pltpu.make_async_copy(f,g,lb.at[k]) for k,(f,g) in enumerate(((mid_h.at[c,a],first),(yy_h.at[c,a],second),(xy.at[a],third)))]
        for m in moves: m.start()
        for m in moves: m.wait()
        part[1,128:256,:]=part[0,0:128,:]+(part[0,128:256,:]+part[1,0:128,:])
        back=pltpu.make_async_copy(part.at[1,pl.ds(128,128)],bo_o.at[a],lb.at[4]); back.start(); back.wait()
    step(at); at+=1
    relay(2)
    while at<9:
        step(at); at+=1
    for pp in range(3):
        ka(pp).wait_recv(); kb(pp,0).wait_recv()
        for j,o in enumerate((dk,dv)):
            for r in range(2):
                v=dkv[pp,z,j,r].astype(f32)+rka[pp,j,r].astype(f32)+rkb[pp,j,r].astype(f32)
                o[256*r:256*r+256,128*pp:128*pp+128]=v.astype(low)
    step(at); at+=1
    for l in load_w: l.wait()
    def input_grad(i,_):
        d=pl.ds(pl.multiple_of(i*128,128),128); a=pl.ds(pl.multiple_of(lax.rem(i,2)*128,128),128)
        part[i//2,a,:]=dot_nt(dq[d,:],wcol(0,384))+dot_nt(dk[d,:],wcol(384,768))+dot_nt(dv[d,:],wcol(768,1152))
        return 0
    lax.fori_loop(0,4,input_grad,0)
    give=remote(part.at[1-c],r3,xs.at[0],xr.at[0],sib); give.start()
    step(at); at+=1
    give.wait_send()
    load_i=pltpu.make_async_copy(gin_o,part.at[1-c],lb.at[0]); load_i.start()
    give.wait_recv(); load_i.wait()
    def last_grad(i,total):
        a=pl.ds(pl.multiple_of(i*128,128),128)
        v=hid[a,:].astype(f32); gn=part[c,a,:]+r3[a,:]
        s=lax.rsqrt(jnp.mean(v*v,axis=-1,keepdims=True)+epsilon)
        wg=gn*gains[0:1,:]
        part[1-c,a,:]=part[1-c,a,:]+(s*wg-v*(s*s*s)*jnp.mean(wg*v,axis=-1,keepdims=True))
        return total+jnp.sum(gn*v*s,axis=0,keepdims=True)
    total=lax.fori_loop(0,2,last_grad,jnp.zeros((1,1536),f32))
    spread(jnp.broadcast_to(total,(8,1536)),16)
    give_i=pltpu.make_async_copy(part.at[1-c],gin_o,ll.at[12]); give_i.start()
    while at<n+lag:
        step(at); at+=1
    for t in range(n):
        arrive(t)
        if t>=n-sum_slots: drain(t)
        if t>=n-part_slots:
            for d in c1[t]: d.wait_send()
        for d in c2[t]: d.wait_send()
        for d in c3[t]: d.wait_send()
    for pp in range(3):
        ka(pp).wait_send()
        @pl.when(outer)
        def _(): kc(pp).wait_send()
        @pl.when(inner)
        def _(): kb(pp,0).wait_send(); kb(pp,1).wait_send()
    give_i.wait(); give_g.wait_send(); give_y.wait_send()

def backward_chunks(ff_steps,ff):
    fw=512*ff_steps
    chunks=[]
    for j in range(ff_steps):
        for left,i,o in ((0,1,0),(0,2,1),(1,0,2)):
            chunks.append((left,0,512,("feed",i,j),(o,512*j,(512,fw),ff)))
    for k in range(4): chunks.append((3 if k==0 else 1,0,384,("ref",k,0),(3+k,0,(384,384),768)))
    chunks.append((1,0,128,("ref",4,0),(7,0,(128,128),256)))
    return chunks

def backward_call(w1,w2,lt,hdg,q,kk,vv,mx,lse,gnf,yy,mid,cot,segr,segc,hid,base,gains,ff_steps,ff,cid=1):
    chunks=backward_chunks(ff_steps,ff); n=len(chunks)
    S=jax.ShapeDtypeStruct; V=pltpu.VMEM; D=pltpu.SemaphoreType.DMA
    hbm=pl.BlockSpec(memory_space=pltpu.HBM); vm=pl.BlockSpec(memory_space=pltpu.VMEM)
    ws=[k[2] for k in chunks]
    scratch=[V((2,4,48,k),low) for k in ws]*1+[V((2,4,48,k),low) for k in ws]+[V((4,48,k),low) for k in ws]+[V((4,48,k),low) for k in ws]+[V((3,2,48,k),low) for k in ws]
    scratch+=[V((sum_slots,2,48,512),f32),V((part_slots,2,2,2,4,48,512),low),V((2,1536,512),low),V((1536,512),low),V((2,512,512),low),V((8,4,48,1152),low),
      V((512,384),low),V((2,1024,384),low),V((2,1024,384),low),V((512,384),low),V((512,384),low),V((2,256,128),f32),V((2,8,1024),f32),V((2,256,128),f32),
      V((256,1280),f32),V((256,1280),f32),V((512,384),low),V((2,2,1024,128),f32),V((3,4,2,2,256,128),low),V((3,2,2,256,128),low),V((3,2,2,256,128),low),V((3,2,2,2,256,128),low),V((512,384),low),V((512,384),low),
      V((2,256,1536),f32),V((256,1536),f32),V((256,1536),low),V((8,1280),f32),V((128,1536),f32),V((128,1536),low)]
    scratch+=[D((16,)),D((n,)),D((n,)),D((n,2)),D((n,2)),D((n,2)),D((n,2)),D((n,3,2)),D((n,3,2)),D((n,)),D((n,)),D((3,4)),D((3,3)),D((3,)),D((3,)),D((5,))]
    return pl.pallas_call(functools.partial(backward_kernel,chunks,ff_steps),out_shape=(S((48,ff),f32),)*3+(S((48,768),f32),)*4+(S((48,256),f32),S((256,1536),f32),S((256,1536),f32),S((2,256,1536),f32),S((256,1536),f32)),
        in_specs=[hbm]*16+[vm]*2,out_specs=(hbm,)*12,scratch_shapes=scratch,
        compiler_params=pltpu.CompilerParams(collective_id=cid,has_side_effects=True,vmem_limit_bytes=62*2**20))(w1,w2,lt,hdg,q,kk,vv,mx,lse,gnf,yy,mid,cot,segr,segc,hid,base,gains)

def cut(v,h,w):
    n=v.shape[1]
    a=min(h*w,n); b=min((h+1)*w,n)
    p=v[:,a:b]
    return jnp.pad(p,((0,0),(0,w-(b-a)))) if b-a<w else p
def pack(wq,wk,wv,wo,ga,gf,wg,wu,wd,steps):
    gains=jnp.pad(jnp.stack([ga,gf],axis=1),((0,0),(0,126)))
    fw=512*steps
    rows=[]
    for h in (0,1):
        m=[cut(v,h,384) for v in (wq,wk,wv,wo.T)]+[gains]
        f=[cut(v,h,fw) for v in (wg,wu,wd.T)]
        for j in range(steps):
            m+=[v[:,512*j:512*j+512] for v in f]
        rows.append(jnp.concatenate(m,axis=1))
    return jnp.stack(rows)
def seg_ids(seg):
    n=seg.shape[1]
    place=jnp.arange(n,dtype=jnp.int32)
    ids=jnp.where(seg[0]>0,seg[0],-1-place).astype(jnp.float32)
    r=jnp.broadcast_to(ids[None],(8,n))
    mine=lax.dynamic_slice_in_dim(ids,lax.axis_index("seq")*256,256,0)
    return r, jnp.broadcast_to(mine[:,None],(256,128))
def base_of(table):
    off=jnp.arange(1280,dtype=jnp.int32)-256-256*lax.axis_index("seq")
    oh=(bucket_table(off)[:,None]==jnp.arange(32,dtype=jnp.int32)).astype(jnp.float32)
    c=lax.rem(lax.axis_index("dp"),2)
    tab=table.astype(jnp.float32)
    mine=jnp.where(c==0,tab[:,:6],tab[:,6:])
    b=jnp.einsum("ub,bh->hu",oh,mine,precision=lax.Precision.HIGHEST)
    return jnp.pad(b,((0,2),(0,0))), oh

def kernel_local(hid,seg,ga,wq,wk,wv,wo,tab,gf,wg,wu,wd,cot):
    ff=wg.shape[1]; steps=-(-ff//1024)
    gain_cols=jnp.pad(jnp.stack([ga,gf],axis=1),((0,0),(0,126)))
    r,s=seg_ids(seg); b=base_of(tab)[0]
    w1,w2,w,lt,hdg,q,kk,vv,mx,lse,gnf,yy,gains,segr,segc,mid,cot2=forward_call((wq,wk,wv,wo.T,wg,wu,wd.T),gain_cols,hid[0],cot[0],r,s,b,steps)
    og,ou,od,oo,oq,ok,ov,oe,gin,bo,_,_=backward_call(w1,w2,lt,hdg,q,kk,vv,mx,lse,gnf,yy,mid,cot2,segr,segc,hid[0],b,gains,steps,ff)
    e=oe.reshape(48,2,128)
    t=e[:32,:,0:8]+e[:32,:,8:16]
    table=t[:,:,:6].reshape(32,12)
    g=e[:,0]+e[:,1]
    gg=lambda a: g[:,a]+g[:,a+8]
    return (bo[None],gin[None],gg(16),oq,ok,ov,oo.T,table,gg(32),og,ou,od.T)


def solution(mesh):
    in_specs = (
        P("dp", "seq", None),
        P("dp", None),
        P(("dp", "seq")),
        P(("dp", "seq"), None),
        P(("dp", "seq"), None),
        P(("dp", "seq"), None),
        P(None, ("dp", "seq")),
        P(),
        P(("dp", "seq")),
        P(("dp", "seq"), None),
        P(("dp", "seq"), None),
        P(None, ("dp", "seq")),
        P("dp", "seq", None),
    )
    out_specs = (
        P("dp", "seq", None),
        P("dp", "seq", None),
        P(("dp", "seq")),
        P(("dp", "seq"), None),
        P(("dp", "seq"), None),
        P(("dp", "seq"), None),
        P(None, ("dp", "seq")),
        P(),
        P(("dp", "seq")),
        P(("dp", "seq"), None),
        P(("dp", "seq"), None),
        P(None, ("dp", "seq")),
    )
    small = mesh.shape["dp"] == 8 and mesh.shape["seq"] == 4
    local = kernel_local if small else plain_local
    return jax.shard_map(local, mesh=mesh, in_specs=in_specs, out_specs=out_specs, check_vma=False)
```

```python
import functools

import jax
import jax.numpy as jnp
from jax import lax
from jax.experimental import pallas as pl
from jax.experimental.pallas import tpu as pltpu
from jax.sharding import PartitionSpec as P

epsilon = 1e-06
far_bounds = (12, 16, 23, 32, 46, 64, 91)
highest = lax.Precision.HIGHEST
mesh_ids = pl.DeviceIdType.MESH


def bucket_table(offset):
    magnitude = jnp.abs(offset)
    distant = 8 + sum(((magnitude >= bound).astype(jnp.int32) for bound in far_bounds))
    signed_part = jnp.where(offset > 0, 16, 0).astype(jnp.int32)
    return signed_part + jnp.where(magnitude < 8, magnitude, distant)


def norm_scale(hidden):
    return lax.rsqrt(jnp.mean(hidden * hidden, axis=-1, keepdims=True) + epsilon)


def norm_backward(grad_normed, hidden, scale, gain):
    weighted = grad_normed * gain
    grad_gain = jnp.sum(grad_normed * hidden * scale, axis=0)
    grad_hidden = scale * weighted - hidden * (scale * scale * scale) * jnp.mean(
        weighted * hidden, axis=-1, keepdims=True
    )
    return (grad_hidden, grad_gain)


def scores_of(query_heads, key_heads, bias, allowed):
    raw_scores = jnp.einsum(
        "rqhd,rkhd->rhqk", query_heads, key_heads, preferred_element_type=jnp.float32
    )
    return jnp.where(allowed, raw_scores + bias[None], -1000000000.0)


def gather_rows(shard):
    return lax.all_gather(shard, ("dp", "seq"), axis=0, tiled=True)


def scatter_sum(parts):
    data_count = lax.axis_size("dp")
    piece_count = lax.axis_size("seq")
    shard_width = parts.shape[0] // (data_count * piece_count)
    split = parts.reshape(data_count, piece_count, shard_width, parts.shape[1])
    half = lax.psum_scatter(split, "dp", scatter_dimension=0, tiled=True)
    return lax.psum_scatter(half, "seq", scatter_dimension=1, tiled=True)[0, 0]


def plain_sums(pairs, extra):
    found = []
    for left, rights in pairs:
        for right in rights:
            part = jnp.einsum("td,tf->df", left, right, preferred_element_type=jnp.float32)
            found.append(scatter_sum(part.astype(jnp.bfloat16)).astype(jnp.float32))
    return found, scatter_sum(extra.astype(jnp.bfloat16)).astype(jnp.float32)


def plain_local(
    hidden_in,
    segment_ids,
    gain_attn,
    w_query,
    w_key,
    w_value,
    w_out,
    rel_table,
    gain_ff,
    w_gate,
    w_up,
    w_down,
    cotangent,
):
    row_count, local_len, model_width = hidden_in.shape
    row_length = segment_ids.shape[1]
    bucket_count, head_count = rel_table.shape
    token_count = row_count * local_len
    data_count = lax.axis_size("dp")
    piece_count = lax.axis_size("seq")
    shard_width = model_width // (data_count * piece_count)
    first_place = lax.axis_index("seq") * local_len
    query_place = first_place + jnp.arange(local_len, dtype=jnp.int32)
    key_place = jnp.arange(row_length, dtype=jnp.int32)
    buckets = bucket_table(key_place[None, :] - query_place[:, None])
    onehot = (buckets[:, :, None] == jnp.arange(bucket_count, dtype=jnp.int32)).astype(jnp.float32)
    bias = jnp.einsum("qkb,bh->hqk", onehot, rel_table.astype(jnp.float32), precision=highest)
    query_segs = lax.dynamic_slice_in_dim(segment_ids, first_place, local_len, 1)
    same_doc = query_segs[:, :, None] == segment_ids[:, None, :]
    visible = (segment_ids[:, None, :] > 0) | (query_place[:, None] == key_place[None, :])[None]
    allowed = (same_doc & visible)[:, None]
    inner = w_query.shape[1]
    ff_width = w_gate.shape[1]
    gains = jnp.pad(jnp.stack([gain_attn, gain_ff], axis=1), ((0, 0), (0, 126)))
    attn_full = gather_rows(jnp.concatenate([w_query, w_key, w_value, w_out.T, gains], axis=1))
    feed_full = gather_rows(jnp.concatenate([w_gate, w_up, w_down.T], axis=1))
    query_full = attn_full[:, :inner]
    key_full = attn_full[:, inner : 2 * inner]
    value_full = attn_full[:, 2 * inner : 3 * inner]
    out_full = attn_full[:, 3 * inner : 4 * inner].T
    gain_one = attn_full[:, 4 * inner]
    gain_two = attn_full[:, 4 * inner + 1]
    gate_full = feed_full[:, :ff_width]
    up_full = feed_full[:, ff_width : 2 * ff_width]
    down_full = feed_full[:, 2 * ff_width :].T
    gain_first = gain_one.astype(jnp.float32)
    residual_in = hidden_in.astype(jnp.float32).reshape(token_count, model_width)
    scale_first = norm_scale(residual_in)
    normed_first = (residual_in * scale_first * gain_first).astype(jnp.bfloat16)
    queries = jnp.dot(normed_first, query_full, preferred_element_type=jnp.float32).astype(
        jnp.bfloat16
    )
    keys_local = jnp.dot(normed_first, key_full, preferred_element_type=jnp.float32).astype(
        jnp.bfloat16
    )
    values_local = jnp.dot(normed_first, value_full, preferred_element_type=jnp.float32).astype(
        jnp.bfloat16
    )
    head_size = inner // head_count
    keys_row, values_row = (
        lax.all_gather(keys_local.reshape(row_count, local_len, inner), "seq", axis=1, tiled=True),
        lax.all_gather(
            values_local.reshape(row_count, local_len, inner), "seq", axis=1, tiled=True
        ),
    )
    query_heads = queries.reshape(row_count, local_len, head_count, head_size)
    key_heads = keys_row.reshape(row_count, row_length, head_count, head_size)
    value_heads = values_row.reshape(row_count, row_length, head_count, head_size)
    logits = scores_of(query_heads, key_heads, bias, allowed)
    row_max = jnp.max(logits, axis=-1, keepdims=True)
    exp_scores = jnp.exp(logits - row_max)
    denominator = jnp.sum(exp_scores, axis=-1, keepdims=True)
    probs_low = (exp_scores / denominator).astype(jnp.bfloat16)
    log_total = row_max + jnp.log(denominator)
    mixed = (
        jnp.einsum("rhqk,rkhd->rqhd", probs_low, value_heads, preferred_element_type=jnp.float32)
        .astype(jnp.bfloat16)
        .reshape(token_count, inner)
    )
    middle = residual_in + jnp.dot(mixed, out_full, preferred_element_type=jnp.float32)
    gain_second = gain_two.astype(jnp.float32)
    scale_second = norm_scale(middle)
    normed_second = (middle * scale_second * gain_second).astype(jnp.bfloat16)
    gate_pre = jnp.dot(normed_second, gate_full, preferred_element_type=jnp.float32)
    up_pre = jnp.dot(normed_second, up_full, preferred_element_type=jnp.float32)
    activated = jax.nn.gelu(gate_pre, approximate=True)
    hidden_mid = (activated * up_pre).astype(jnp.bfloat16)
    block_out = middle + jnp.dot(hidden_mid, down_full, preferred_element_type=jnp.float32)
    gain_second = gain_two.astype(jnp.float32)
    grad_out = cotangent.reshape(token_count, model_width)
    grad_hidden = (
        jnp.einsum("td,fd->tf", grad_out, down_full, preferred_element_type=jnp.float32)
        .astype(jnp.bfloat16)
        .astype(jnp.float32)
    )
    gelu_value, gelu_pull = jax.vjp(lambda value: jax.nn.gelu(value, approximate=True), gate_pre)
    grad_gate = gelu_pull(grad_hidden * up_pre)[0].astype(jnp.bfloat16)
    grad_up = (grad_hidden * gelu_value).astype(jnp.bfloat16)
    grad_normed_second = jnp.einsum(
        "tf,df->td", grad_gate, gate_full, preferred_element_type=jnp.float32
    ) + jnp.einsum("tf,df->td", grad_up, up_full, preferred_element_type=jnp.float32)
    grad_middle_norm, grad_gain_two = norm_backward(
        grad_normed_second, middle, scale_second, gain_second
    )
    grad_middle = grad_out.astype(jnp.float32) + grad_middle_norm
    grad_attended = grad_middle.astype(jnp.bfloat16)
    grad_mixed = jnp.einsum(
        "td,id->ti", grad_attended, out_full, preferred_element_type=jnp.float32
    ).astype(jnp.bfloat16)
    grad_heads = grad_mixed.reshape(row_count, local_len, head_count, head_size)
    logits_again = scores_of(query_heads, key_heads, bias, allowed)
    probs_again = jnp.exp(logits_again - log_total)
    probs_again_low = probs_again.astype(jnp.bfloat16)
    grad_probs = jnp.einsum(
        "rqhd,rkhd->rhqk", grad_heads, value_heads, preferred_element_type=jnp.float32
    )
    row_dot = jnp.sum(probs_again * grad_probs, axis=-1, keepdims=True)
    grad_logits = (probs_again * (grad_probs - row_dot)).astype(jnp.bfloat16)
    grad_bias = jnp.sum(grad_logits.astype(jnp.float32), axis=0)
    grad_table = jnp.einsum("qkb,hqk->bh", onehot, grad_bias, precision=highest)
    grad_queries = (
        jnp.einsum("rhqk,rkhd->rqhd", grad_logits, key_heads, preferred_element_type=jnp.float32)
        .astype(jnp.bfloat16)
        .reshape(token_count, inner)
    )
    grad_keys_row = jnp.einsum(
        "rhqk,rqhd->rkhd", grad_logits, query_heads, preferred_element_type=jnp.float32
    )
    grad_values_row = jnp.einsum(
        "rhqk,rqhd->rkhd", probs_again_low, grad_heads, preferred_element_type=jnp.float32
    )
    grad_keys_part, grad_values_part = (
        lax.psum_scatter(
            grad_keys_row.astype(jnp.bfloat16), "seq", scatter_dimension=1, tiled=True
        ).astype(jnp.float32),
        lax.psum_scatter(
            grad_values_row.astype(jnp.bfloat16), "seq", scatter_dimension=1, tiled=True
        ).astype(jnp.float32),
    )
    grad_keys = grad_keys_part.astype(jnp.bfloat16).reshape(token_count, inner)
    grad_values = grad_values_part.astype(jnp.bfloat16).reshape(token_count, inner)
    grad_normed_first = jnp.einsum(
        "ti,di->td", grad_queries, query_full, preferred_element_type=jnp.float32
    )
    grad_normed_first = grad_normed_first + jnp.einsum(
        "ti,di->td", grad_keys, key_full, preferred_element_type=jnp.float32
    )
    grad_normed_first = grad_normed_first + jnp.einsum(
        "ti,di->td", grad_values, value_full, preferred_element_type=jnp.float32
    )
    grad_first, grad_gain_one = norm_backward(
        grad_normed_first, residual_in, scale_first, gain_first
    )
    grad_input = grad_middle + grad_first
    device_count = data_count * piece_count
    table_size = bucket_count * head_count
    table_rows = -(-table_size // shard_width)
    table_block = jnp.pad(grad_table.reshape(-1), (0, table_rows * shard_width - table_size))
    table_block = jnp.broadcast_to(
        table_block.reshape(1, table_rows, shard_width), (device_count, table_rows, shard_width)
    )
    gain_block = jnp.stack([grad_gain_one, grad_gain_two], axis=0)
    gain_block = gain_block.reshape(2, device_count, shard_width).transpose(1, 0, 2)
    extra = jnp.concatenate([table_block, gain_block], axis=1).transpose(0, 2, 1)
    extra = extra.reshape(model_width, table_rows + 2)
    extra = jnp.pad(extra, ((0, 0), (0, -(table_rows + 2) % 128)))
    pairs = (
        (normed_second, (grad_gate, grad_up)),
        (grad_out, (hidden_mid,)),
        (grad_attended, (mixed,)),
        (normed_first, (grad_queries, grad_keys, grad_values)),
    )
    (gate_sum, up_sum, down_sum, out_sum, query_sum, key_sum, value_sum), extra_sum = plain_sums(
        pairs, extra
    )
    table_total = extra_sum[:, :table_rows].T.reshape(-1)[:table_size]
    table_total = table_total.reshape(bucket_count, head_count)
    grad_gain_one_shard = extra_sum[:, table_rows]
    grad_gain_two_shard = extra_sum[:, table_rows + 1]
    return (
        block_out.reshape(row_count, local_len, model_width),
        grad_input.reshape(row_count, local_len, model_width),
        grad_gain_one_shard,
        query_sum,
        key_sum,
        value_sum,
        out_sum.T,
        table_total,
        grad_gain_two_shard,
        gate_sum,
        up_sum,
        down_sum.T,
    )


gelu_c=0.7978845608028654

def peers_of():
    dp=lax.axis_index("dp"); z=lax.axis_index("seq")
    c=lax.rem(dp,2); x=lax.rem(dp//2,2); y=dp//4
    return dp,z,c,x,y

def remote(src,dst,ss,rs,dev):
    return pltpu.make_async_remote_copy(src_ref=src,dst_ref=dst,send_sem=ss,recv_sem=rs,device_id=dev,device_id_type=mesh_ids)

def dot(a,b):
    return jnp.dot(a,b,preferred_element_type=jnp.float32)

def dot_nt(a,b):
    return lax.dot_general(a,b,(((1,),(1,)),((),())),preferred_element_type=jnp.float32)

def lanes(shape):
    return lax.broadcasted_iota(jnp.int32,shape,len(shape)-1)

def greet(devices):
    bar=pltpu.get_barrier_semaphore()
    for d in devices: pl.semaphore_signal(bar,inc=1,device_id=d,device_id_type=mesh_ids)
    pl.semaphore_wait(bar,len(devices))

low=jnp.bfloat16
f32=jnp.float32

h_parts=4
across_first=2
def forward_kernel(ff_steps, w_q, w_k, w_v, w_o, w_g, w_u, w_d, gains, hid, cot, segr, segc, base,
                   w1, w2, w, lt_o, hdg_o, q_o, kk_o, vv_o, mx_o, lse_o, gnf_o, yy_o, gs_o, segr_o, segc_o, mid_o, cot_o,
                   hrow, cotv, sr, sc, wa, wf, qq, kk, vv, mx, lse, bias, part, mid, n2, hd, yy, lt, gs, r1, wp,
                   s0s, s0r, l0, s1s, s1r, s2s, s2r, s3s, s3r, hs, hr, xs, xr, ks, kr, ll, lo):
    cols=[(0,768),(768,896)]+[(1664+512*i,512) for i in range(3*ff_steps)]
    n=len(cols)
    dp,z,c,x,y=peers_of()
    q=dp//2; qx=2*y+1-x; qy=lax.rem(q+2,4); qd=3-q
    sib=(dp+1-2*c,z); dx=(2*qx+c,z); dy=(2*qy+c,z); dxy=(dx,dy)
    zb=lax.rem(z,2); pe=z+1-2*zb; mo=2-z//2; zo=2-2*(z//2)
    inner=(z==1)|(z==2); outer=(z==0)|(z==3)
    dpe=(dp,pe); dmo=(dp,mo)
    greet([sib,dx,dy]+[(dp,lax.rem(z+k,4)) for k in (1,2,3)])
    def cs(t): return pl.ds(cols[t][0],cols[t][1])
    def wr(t): return (w1,w2)[t] if t<2 else w.at[t-2]
    def s0(t,recv=False):
        return remote(wp.at[1-c,:,cs(t)], wr(t).at[(dp+1-2*c) if recv else dp,z], s0s.at[t], s0r.at[t], sib)
    def keep(t): return pltpu.make_async_copy(wp.at[c,:,cs(t)], wr(t).at[dp,z], l0.at[t])
    across=set(range(n-across_first,n))
    def group(t): return pl.ds(0,8) if t in across else pl.ds(2*q,2)
    def span(t): return z if t in across else pl.ds(0,4)
    tail=w_g.shape[1]-512*(2*ff_steps-1)
    narrow=set(range(n-3,n)) if 0<tail<512 and tail%128==0 else set()
    def each(t,act):
        if t in narrow:
            @pl.when(c==0)
            def _(): act(512)
            @pl.when(c==1)
            def _(): act(tail)
        else: act(cols[t][1])
    def s1a(t,wd,recv=False):
        r=wr(t).at[group(t), pe if recv else z, :, pl.ds(0,wd)]
        return remote(r,r,s1s.at[t,0],s1r.at[t,0],dpe)
    def s1b(t,wd):
        r=wr(t).at[group(t), z, :, pl.ds(0,wd)]
        return remote(r,r,s1s.at[t,1],s1r.at[t,1+zb],dmo)
    def s1bw(t,k,wd):
        r=wr(t).at[group(t), zo+k, :, pl.ds(0,wd)]
        return remote(r,r,s1s.at[t,1],s1r.at[t,1+k],dmo)
    def s1c(t,wd):
        r=wr(t).at[group(t), pl.ds(zo,2), :, pl.ds(0,wd)]
        return remote(r,r,s1s.at[t,2],s1r.at[t,3],dpe)
    def s2(t,a,wd,recv=False):
        r=wr(t).at[pl.ds(2*((qx,qy)[a] if recv else q),2), span(t), :, pl.ds(0,wd)]
        return remote(r,r,s2s.at[t,a],s2r.at[t,a],dxy[a])
    def s3(t,a,wd,recv=False):
        r=wr(t).at[2*(qd if recv else (qy,qx)[a])+a, span(t), :, pl.ds(0,wd)]
        return remote(r,r,s3s.at[t,a],s3r.at[t,a],dxy[a])
    def z_go(t): each(t,lambda wd: (s1a(t,wd).start(),s1b(t,wd).start()))
    def z_on(t):
        @pl.when(inner)
        def _(): each(t,lambda wd: (s1bw(t,0,wd).wait_recv(),s1bw(t,1,wd).wait_recv(),s1c(t,wd).start()))
    def z_in(t):
        each(t,lambda wd: s1a(t,wd,True).wait_recv())
        @pl.when(outer)
        def _(): each(t,lambda wd: s1c(t,wd).wait_recv())
    def xy_go(t,f): each(t,lambda wd: [f(t,a,wd).start() for a in range(2)])
    def xy_in(t,f): each(t,lambda wd: [f(t,a,wd,True).wait_recv() for a in range(2)])
    hp=hrow.shape[2]//h_parts
    def ht(p): return pl.ds(p*hp,hp)
    def ha(p,recv=False): return remote(hid.at[ht(p)],hrow.at[c,pe if recv else z,ht(p)],hs.at[p,0],hr.at[p,0],dpe)
    def hb(p): return remote(hid.at[ht(p)],hrow.at[c,z,ht(p)],hs.at[p,1],hr.at[p,1+zb],dmo)
    def hbw(p,k): return remote(hid.at[ht(p)],hrow.at[c,zo+k,ht(p)],hs.at[p,1],hr.at[p,1+k],dmo)
    def hc(p):
        r=hrow.at[c,pl.ds(zo,2),ht(p)]
        return remote(r,r,hs.at[p,2],hr.at[p,3],dpe)
    done=set()
    def once(*k):
        if k in done: return False
        done.add(k); return True
    def start1(t):
        if t<n and t not in across and once(1,t):
            keep(t).wait(); s0(t,True).wait_recv(); z_go(t)
    def across1(t):
        keep(t).wait(); s0(t,True).wait_recv(); xy_go(t,s2)
    def across2(t): xy_in(t,s2); xy_go(t,s3)
    def across3(t): xy_in(t,s3); z_go(t)
    def across4(t): z_on(t)
    def across5(t): z_in(t)
    def forward(t):
        if t<n and t not in across and once(5,t): z_on(t)
    def start2(t):
        forward(t)
        if t<n and t not in across and once(2,t):
            z_in(t); xy_go(t,s2)
    def start3(t):
        if 0<=t<n and t not in across and once(3,t):
            xy_in(t,s2); xy_go(t,s3)
    def finish(t):
        if 0<=t<n and t not in across and once(4,t): xy_in(t,s3)
    def advance(t):
        for u in range(t+4): start1(u)
        for f,u in ((forward,t+1),(start2,t),(start3,t-1),(finish,t-2)):
            for v in range(u+1): f(v)
    def h_go(p): ha(p).start(); hb(p).start()
    def h_on(p):
        @pl.when(inner)
        def _():
            hbw(p,0).wait_recv(); hbw(p,1).wait_recv(); hc(p).start()
    for h in range(2):
        for i,v in enumerate((w_q,w_k,w_v,w_o)): wp[h,:,384*i:384*i+384]=v[:,384*h:384*h+384]
        wp[h,:,1536:1664]=gains[...]
        for j in range(ff_steps):
            for i,v in enumerate((w_g,w_u,w_d)):
                a=1664+1536*j+512*i; f=512*(ff_steps*h+j); g=min(512,v.shape[1]-f)
                if g>0: wp[h,:,a:a+g]=v[:,f:f+g]
                if g<512: wp[h,:,a+max(g,0):a+512]=jnp.zeros((48,512-max(g,0)),low)
    keep_h=pltpu.make_async_copy(hid,hrow.at[c,z],ll.at[0]); keep_h.start()
    keep_c=pltpu.make_async_copy(cot,cotv.at[c],ll.at[1]); keep_c.start()
    keep_r=pltpu.make_async_copy(segr,sr.at[c],ll.at[2]); keep_r.start()
    keep_s=pltpu.make_async_copy(segc,sc.at[c],ll.at[3]); keep_s.start()
    for t in [*range(3),*sorted(across)]: s0(t).start(); keep(t).start()
    give_h=[remote(hid,hrow.at[c,z],xs.at[3],xr.at[3],sib)]; give_h[0].start()
    give_c=remote(cot,cotv.at[c],xs.at[0],xr.at[0],sib); give_c.start()
    give_r=remote(segr,sr.at[c],xs.at[1],xr.at[1],sib); give_r.start()
    give_s=remote(segc,sc.at[c],xs.at[2],xr.at[2],sib); give_s.start()
    for t in range(3,n-across_first): s0(t).start(); keep(t).start()
    start1(0); start1(1); start1(2); h_go(0)
    for t in sorted(across): across1(t)
    forward(0); start2(0); forward(1); start2(1); forward(2)
    h_on(0); start1(3); h_go(1)
    for t in sorted(across): across2(t)
    start3(0); start2(2)
    keep_h.wait(); keep_c.wait(); keep_r.wait(); keep_s.wait()
    remote(segr,sr.at[1-c],xs.at[1],xr.at[1],sib).wait_recv()
    remote(segc,sc.at[1-c],xs.at[2],xr.at[2],sib).wait_recv()
    remote(cot,cotv.at[1-c],xs.at[0],xr.at[0],sib).wait_recv()
    remote(hid,hrow.at[1-c,z],xs.at[3],xr.at[3],sib).wait_recv()
    start3(1); forward(3); h_on(1); start1(4); h_go(2)
    finish(0); finish(1)
    load_a=[pltpu.make_async_copy(w1,wa.at[:,:,:,pl.ds(0,768)],ll.at[4]),pltpu.make_async_copy(w2,wa.at[:,:,:,pl.ds(768,896)],ll.at[11])]
    for l in load_a: l.start()
    start3(2); start2(3); forward(4); h_on(2); start1(5); h_go(3)
    for l in load_a: l.wait()
    def wcol(a,b): return wa[:,:,:,a:b].reshape(1536,b-a)
    pick=(lanes((8,128))==lax.broadcasted_iota(jnp.int32,(8,128),0)).astype(low)
    gs[...]=dot_nt(pick,wcol(1536,1664))
    def transpose_cot(i,_):
        lt[2,:,pl.ds(pl.multiple_of(i*128,128),128)]=cotv[i//2,pl.ds(pl.multiple_of(lax.rem(i,2)*128,128),128),:].astype(f32).T.astype(low)
        return 0
    lax.fori_loop(0,4,transpose_cot,0)
    def normed(v,row):
        s=lax.rsqrt(jnp.mean(v*v,axis=-1,keepdims=True)+epsilon)
        return v*s*gs[row:row+1,:]
    def queries(i,_):
        a=pl.ds(pl.multiple_of(lax.rem(i,2)*128,128),128)
        v=normed(hrow[i//2,z,a,:].astype(f32),0)
        d=pl.ds(pl.multiple_of(i*128,128),128)
        qq[d,:]=dot(v.astype(low),wcol(0,384)).astype(low)
        lt[0,:,d]=v.T.astype(low)
        return 0
    lax.fori_loop(0,4,queries,0)
    def share(p,k,recv=False):
        r=hrow.at[1-c if recv else c,lax.rem(z+k,4),ht(p)]
        return remote(r,r,ks.at[p,k-1],kr.at[p,k-1],sib)
    def keys(r,p):
        v=jnp.concatenate([normed(hrow[r,zz,p*hp:p*hp+hp,:].astype(f32),0).astype(low) for zz in range(4)],axis=0)
        for o,w0 in ((kk,384),(vv,768)):
            d=dot(v,wcol(w0,w0+384)).astype(low)
            for zz in range(4): o[r,256*zz+p*hp:256*zz+p*hp+hp,:]=d[zz*hp:zz*hp+hp]
    def arrive(p):
        ha(p,True).wait_recv()
        @pl.when(outer)
        def _(): hc(p).wait_recv()
        for k in (1,2,3): share(p,k).start()
        keys(c,p)
    def other(p):
        for k in (1,2,3): share(p,k,True).wait_recv()
        keys(1-c,p)
    arrive(0)
    start2(4); start3(3); finish(2); forward(5); h_on(3)
    arrive(1); other(0)
    start2(5); start3(4)
    arrive(2); other(1)
    arrive(3); other(2); other(3)
    advance(6)
    for t in sorted(across)[:1]: across3(t)
    for h in range(6):
        pair=pl.ds(128*(h//2),128); odd=h%2
        bias[...]=pltpu.roll(jnp.broadcast_to(base[h:h+1,:],(256,1280)),1024,1,stride=1,stride_axis=0)
        def attend(i,_):
            r=i//2; d=pl.ds(pl.multiple_of(i*128,128),128)
            a=pl.ds(pl.multiple_of(lax.rem(i,2)*128,128),128)
            mine=(lanes((128,128))>=64) if odd else (lanes((128,128))<64)
            qh=jnp.where(mine,qq[d,pair].astype(f32),0.0).astype(low)
            s=dot_nt(qh,kk[r,:,pair])+bias[a,0:1024]
            s=jnp.where(sc[r,a,0:1]==sr[r,0:1,:],s,-1000000000.0)
            m=jnp.max(s,axis=-1,keepdims=True)
            e=jnp.exp(s-m)
            l=jnp.sum(e,axis=-1,keepdims=True)
            p=(e*(1.0/l)).astype(low)
            o=dot(p,vv[r,:,pair])
            if odd: o=jnp.where(mine,o,mx[d,pair].astype(f32))
            mx[d,pair]=o.astype(low)
            lse[r,a,:]=jnp.where(lanes((128,128))==h,m+jnp.log(l),lse[r,a,:]) if h else jnp.broadcast_to(m+jnp.log(l),(128,128))
            return 0
        lax.fori_loop(0,4,attend,0)
        if h in (1,3): advance(7+h//2)
        if h==3:
            for t in sorted(across)[:1]: across4(t)
            for t in sorted(across)[1:]: across3(t)
    def project(i,_):
        part[i//2,pl.ds(pl.multiple_of(lax.rem(i,2)*128,128),128),:]=dot_nt(mx[pl.ds(pl.multiple_of(i*128,128),128),:],wcol(1152,1536))
        return 0
    lax.fori_loop(0,4,project,0)
    give_p=remote(part,r1,xs.at[4],xr.at[4],sib); give_p.start()
    advance(9)
    outs=[pltpu.make_async_copy(a,b,lo.at[i]) for i,(a,b) in enumerate(((qq,q_o),(kk,kk_o),(vv,vv_o),(mx,mx_o),(lse,lse_o),(sr,segr_o),(sc,segc_o),(cotv,cot_o)))]
    for o in outs: o.start()
    give_p.wait_recv()
    def middle(i,_):
        a=pl.ds(pl.multiple_of(lax.rem(i,2)*128,128),128); r=i//2
        d=pl.ds(pl.multiple_of(i*128,128),128)
        v=hrow[r,z,a,:].astype(f32)+(part[r,a,:]+r1[r,a,:])
        mid[r,a,:]=v
        v=normed(v,1)
        n2[d,:]=v.astype(low)
        lt[1,:,d]=v.T.astype(low)
        return 0
    lax.fori_loop(0,4,middle,0)
    give_p.wait_send()
    give_lt=pltpu.make_async_copy(lt,lt_o,ll.at[5]); give_lt.start()
    give_mid=pltpu.make_async_copy(mid,mid_o,ll.at[12]); give_mid.start()
    gs_o[...]=gs[...]
    advance(10)
    for t in sorted(across)[1:]: across4(t)
    hout=[]
    for j in range(ff_steps):
        if j:
            for t in range(4+3*j,7+3*j) if j==ff_steps-1 else [10+j]: advance(t)
            if j==ff_steps-1:
                for t in sorted(across): across5(t)
        def load(act):
            def piece(i): each(2+3*j+i,lambda wd: act(pltpu.make_async_copy(w.at[3*j+i,:,:,:,pl.ds(0,wd)],wf.at[i,:,:,:,pl.ds(0,wd)],ll.at[6+i])))
            for i in range(3): piece(i)
        if 2+3*j in narrow:
            @pl.when(c==1)
            def _(): wf[:,:,:,:,tail:512]=jnp.zeros((3,8,4,48,512-tail),low)
        load(lambda m: m.start())
        b=j%2
        if j>=2: hout[j-2].wait()
        load(lambda m: m.wait())
        def feed(i,_):
            d=pl.ds(pl.multiple_of(i*256,256),256)
            v=n2[d,:]
            wg=wf[0].reshape(1536,512); wu=wf[1].reshape(1536,512); wd=wf[2].reshape(1536,512)
            gate=dot(v,wg); up=dot(v,wu)
            gh=dot(cotv[i],wd).astype(low).astype(f32)
            u2=gate*gate
            th=jnp.tanh(gelu_c*(gate+0.044715*(gate*u2)))
            act=0.5*gate*(1.0+th)
            slope=0.5*(1.0+th)+0.5*gate*(1.0-th*th)*(gelu_c*(1.0+3*0.044715*u2))
            hm=(act*up).astype(low); dg=(gh*up*slope).astype(low); du=(gh*act).astype(low)
            hd[b,0,d,:]=hm; hd[b,1,d,:]=dg; hd[b,2,d,:]=du
            yp=dot_nt(hm,wd); gp=dot_nt(dg,wg)+dot_nt(du,wu)
            if j: yp=yp+yy[i]; gp=gp+part[i]
            yy[i]=yp; part[i]=gp
            return 0
        lax.fori_loop(0,2,feed,0)
        o=pltpu.make_async_copy(hd.at[b],hdg_o.at[:,:,pl.ds(512*j,512)],lo.at[8+b]); o.start(); hout.append(o)
    give_m=[pltpu.make_async_copy(part,gnf_o,ll.at[9]),pltpu.make_async_copy(yy,yy_o,ll.at[10])]
    for g in give_m: g.start()
    for o in outs+hout[-2:]: o.wait()
    give_lt.wait(); give_mid.wait()
    for g in give_m: g.wait()
    give_c.wait_send(); give_r.wait_send(); give_s.wait_send()
    for g in give_h: g.wait_send()
    for p in range(h_parts):
        for k in (1,2,3): share(p,k).wait_send()
        ha(p).wait_send(); hb(p).wait_send()
        @pl.when(inner)
        def _(): hc(p).wait_send()
    for t in range(n):
        s0(t).wait_send()
        each(t,lambda wd: [g.wait_send() for g in (s1a(t,wd),s1b(t,wd),s2(t,0,wd),s2(t,1,wd),s3(t,0,wd),s3(t,1,wd))])
        @pl.when(inner)
        def _(): each(t,lambda wd: s1c(t,wd).wait_send())

def forward_call(weights, gains, hid, cot, segr, segc, base, ff_steps, cid=0):
    n=2+3*ff_steps
    S=jax.ShapeDtypeStruct; V=pltpu.VMEM; D=pltpu.SemaphoreType.DMA
    fw=512*ff_steps
    hbm=pl.BlockSpec(memory_space=pltpu.HBM); vm=pl.BlockSpec(memory_space=pltpu.VMEM)
    outs=(S((8,4,48,768),low),S((8,4,48,896),low),S((3*ff_steps,8,4,48,512),low),S((3,1536,512),low),S((3,512,fw),low),S((512,384),low),S((2,1024,384),low),S((2,1024,384),low),
          S((512,384),low),S((2,256,128),f32),S((2,256,1536),f32),S((2,256,1536),f32),S((8,1536),f32),S((2,8,1024),f32),S((2,256,128),f32),S((2,256,1536),f32),S((2,256,1536),low))
    ospec=[hbm]*17; ospec[12]=vm
    scratch=[V((2,4,256,1536),low),V((2,256,1536),low),V((2,8,1024),f32),V((2,256,128),f32),V((8,4,48,1664),low),V((3,8,4,48,512),low),
             V((512,384),low),V((2,1024,384),low),V((2,1024,384),low),V((512,384),low),V((2,256,128),f32),V((256,1280),f32),
             V((2,256,1536),f32),V((2,256,1536),f32),V((512,1536),low),V((2,3,512,512),low),V((2,256,1536),f32),V((3,1536,512),low),V((8,1536),f32),
             V((2,256,1536),f32),V((2,48,1664+1536*ff_steps),low),
             D((n,)),D((n,)),D((n,)),D((n,3)),D((n,4)),D((n,2)),D((n,2)),D((n,2)),D((n,2)),D((h_parts,3)),D((h_parts,4)),D((10,)),D((10,)),D((h_parts,3)),D((h_parts,3)),D((13,)),D((10,))]
    return pl.pallas_call(functools.partial(forward_kernel,ff_steps),out_shape=outs,
        in_specs=[vm]*8+[hbm]*4+[vm],out_specs=tuple(ospec),scratch_shapes=scratch,
        compiler_params=pltpu.CompilerParams(collective_id=cid,has_side_effects=True,vmem_limit_bytes=62*2**20))(*weights,gains,hid,cot,segr,segc,base)

def dot_tn(a,b):
    return lax.dot_general(a,b,(((0,),(0,)),((),())),preferred_element_type=jnp.float32)

part_slots=2
sum_slots=3
lag=6
def backward_kernel(chunks, ff_steps, w1, w2, lt_h, hdg, q_h, kk_h, vv_h, mx_h, lse_h, gnf_h, yy_h, mid_h, cot_h, segr_h, segc_h, hid_h, base, gains,
                    og, ou, od, oo, oq, ok, ov, oe, gin_o, bo_o, xg, xy, *rest):
    n=len(chunks)
    ra1=rest[0:n]; rb1=rest[n:2*n]; ra2=rest[2*n:3*n]; rb2=rest[3*n:4*n]; rz=rest[4*n:5*n]
    (fin,p,lt,gat,rbuf,wa,qq,kk,vv,mx,gm,lse,sr,sc,bias,dbias,dq,acc,dkv,rka,rkb,rkc,dk,dv,part,r3,hid,dtab,ext,cb,
     ll,lr,lo,s1,v1,s2,v2,s3,v3,s4,v4,ks,kr,xs,xr,lb)=rest[5*n:]
    dp,z,c,x,y=peers_of()
    sib=(dp+1-2*c,z); dx=(dp+2-4*x,z); dy=(lax.rem(dp+4,8),z)
    zs=[lax.rem(z+k,4) for k in (1,2,3)]; dz=[(dp,zz) for zz in zs]
    zb=lax.rem(z,2); pe=z+1-2*zb; mo=2-z//2; zo=2-2*(z//2)
    inner=(z==1)|(z==2); outer=(z==0)|(z==3)
    def ka(pp,recv=False): return remote(dkv.at[pp,pe],rka.at[pp],ks.at[pp,0],kr.at[pp,0],(dp,pe))
    def kc(pp): return remote(dkv.at[pp,pl.ds(zo,2)],rkc.at[pp],ks.at[pp,1],kr.at[pp,1],(dp,pe))
    def kb(pp,k): return remote(dkv.at[pp,zo+k],rkb.at[pp],ks.at[pp,2+k],kr.at[pp,2],(dp,zo+k))
    def relay(pp):
        @pl.when(inner)
        def _():
            kc(pp).wait_recv()
            for k in range(2):
                for j in range(2):
                    for r in range(2):
                        dkv[pp,zo+k,j,r]=(dkv[pp,zo+k,j,r].astype(f32)+rkc[pp,k,j,r].astype(f32)).astype(low)
                kb(pp,k).start()
    loads=[pltpu.make_async_copy(a,b,ll.at[i]) for i,(a,b) in enumerate((
        (lt_h.at[pl.ds(1,2)],lt),(w2.at[:,:,:,pl.ds(384,384)],wa.at[:,:,:,pl.ds(0,384)]),(q_h,qq),(kk_h,kk),(vv_h,vv),(mx_h,mx),(lse_h,lse),(segr_h,sr),(segc_h,sc),(hid_h,hid)))]
    for l in loads: l.start()
    slots=rbuf.shape[0]
    def fetch(t):
        kind,i,j=chunks[t][3]
        return pltpu.make_async_copy(hdg.at[i,:,pl.ds(512*j,512)],rbuf.at[t%slots],lr.at[t])
    feeds=[t for t in range(n) if chunks[t][3][0]=="feed"]
    for t in feeds[:slots]: fetch(t).start()
    greet([sib,dx,dy]+dz)
    load_n=pltpu.make_async_copy(lt_h.at[0],lt.at[1],ll.at[14])
    done=set()
    def once(*k):
        if k in done: return False
        done.add(k); return True
    def each(t,act):
        width,fw=chunks[t][4][2]; tail=chunks[t][4][3]-fw-chunks[t][4][1]
        if 0<tail<width:
            @pl.when(c==0)
            def _(): act(pl.ds(0,width))
            @pl.when(c==1)
            def _(): act(pl.ds(0,tail))
        else: act(pl.ds(0,width))
    def hop1(t,wd):
        b=t%part_slots
        return (remote(p.at[b,:,1-x,0,:,:,wd],ra1[t].at[:,:,:,wd],s1.at[t,0],v1.at[t,0],dx),
                remote(p.at[b,1-y,:,1,:,:,wd],rb1[t].at[:,:,:,wd],s1.at[t,1],v1.at[t,1],dy))
    def hop2(t,wd):
        return (remote(ra1[t].at[1-y,:,:,wd],ra2[t].at[:,:,wd],s2.at[t,0],v2.at[t,0],dy),
                remote(rb1[t].at[1-x,:,:,wd],rb2[t].at[:,:,wd],s2.at[t,1],v2.at[t,1],dx))
    def hop3(t,wd):
        return [remote(r[t].at[zs[k],:,wd],rz[t].at[k,i,:,wd],s3.at[t,k,i],v3.at[t,k,i],dz[k]) for k in range(3) for i,r in enumerate((ra2,rb2))]
    def go(t,f): each(t,lambda wd: [d.start() for d in f(t,wd)])
    def came(t,f): each(t,lambda wd: [d.wait_recv() for d in f(t,wd)])
    def went(t,f): each(t,lambda wd: [d.wait_send() for d in f(t,wd)])
    def stage1(t):
        left,off,wd,src=chunks[t][:4]; b=t%part_slots
        if t>=part_slots:
            went(t-part_slots,hop1)
        if src[0]=="feed":
            fetch(t).wait()
            right=lambda: rbuf[t%slots]
        else:
            right=(lambda: mx[...],lambda: dq[...],lambda: dk[...],lambda: dv[...],None)[src[1]]
        if src==("ref",1,0): load_n.wait()
        if right is None:
            p[b,:,:,:,:,:,0:wd]=ext[...].T.astype(low).reshape(2,2,2,4,48,wd)
        else:
            def body(i,_):
                rs=pl.ds(pl.multiple_of(i*192,192),192)
                lhs=gat[rs,:] if left==3 else lt[left,rs,:]
                p[b,i//4,lax.rem(i//2,2),lax.rem(i,2),:,:,0:wd]=dot(lhs,right()).astype(low).reshape(4,48,wd)
                return 0
            lax.fori_loop(0,8,body,0)
        if t==feeds[-1]:
            load_n.start()
        if src[0]=="feed" and t+slots<n and chunks[t+slots][3][0]=="feed": fetch(t+slots).start()
        go(t,hop1)
    def stage2(t):
        wd=chunks[t][2]; b=t%part_slots
        came(t,hop1)
        def body(i,_):
            h=i//4; zz=lax.rem(i,4)
            ra1[t][h,zz]=ra1[t][h,zz]+p[b,h,x,0,zz,:,0:wd]
            rb1[t][h,zz]=rb1[t][h,zz]+p[b,y,h,1,zz,:,0:wd]
            return 0
        lax.fori_loop(0,8,body,0)
        go(t,hop2)
    def stage3(t):
        came(t,hop2)
        def body(zz,_):
            ra2[t][zz]=ra2[t][zz]+ra1[t][y,zz]
            rb2[t][zz]=rb2[t][zz]+rb1[t][x,zz]
            return 0
        lax.fori_loop(0,4,body,0)
        go(t,hop3)
    def place(t,pair,acts,half):
        o,offset,width,total=chunks[t][4]
        o=(og,ou,od,oo,oq,ok,ov,oe)[o]
        last=total-(width[1]+offset)
        def act(size):
            cols=pl.ds(pl.multiple_of(half*width[1]+offset,128),size)
            for m,how in zip(pair(None,size,cols,o),acts):
                if how: getattr(m,how)()
        if last>=width[0]: act(width[0])
        else:
            @pl.when(half==0)
            def _(): act(width[0])
            if last>0:
                @pl.when(half==1)
                def _(): act(last)
    def drain(t):
        place(t,lambda _,width,cols,o: (
            remote(fin.at[0,0,:,pl.ds(0,width)],o.at[:,cols],s4.at[t],v4.at[t],sib),
            pltpu.make_async_copy(fin.at[0,0,:,pl.ds(0,width)],o.at[:,cols],lo.at[t])),("wait_send","wait"),c)
    def arrive(t):
        place(t,lambda _,width,cols,o: (remote(fin.at[0,0,:,pl.ds(0,width)],o.at[:,cols],s4.at[t],v4.at[t],sib),),("wait_recv",),1-c)
    def stage4(t):
        wd=chunks[t][2]
        came(t,hop3)
        f0=ra2[t][z].astype(f32); f1=rb2[t][z].astype(f32)
        for k in range(3):
            f0=f0+rz[t][k,0].astype(f32); f1=f1+rz[t][k,1].astype(f32)
        b=t%sum_slots
        if t>=sum_slots:
            drain(t-sum_slots)
        fin[b,0,:,0:wd]=f0; fin[b,1,:,0:wd]=f1
        place(t,lambda _,width,cols,o: (
            remote(fin.at[b,1-c,:,pl.ds(0,width)],o.at[:,cols],s4.at[t],v4.at[t],sib),
            pltpu.make_async_copy(fin.at[b,c,:,pl.ds(0,width)],o.at[:,cols],lo.at[t])),("start","start"),c)
    def step(s):
        for f,t in ((stage2,s),(stage1,s+2),(stage3,s-1),(stage4,s-lag)):
            if 0<=t<n and once(f.__name__,t): f(t)
    give_g=remote(gnf_h,xg,xs.at[1],xr.at[1],sib); give_g.start()
    give_y=remote(yy_h.at[1-c],xy,xs.at[2],xr.at[2],sib); give_y.start()
    loads[0].wait()
    stage1(0); stage1(1); once("stage1",0); once("stage1",1)
    for l in loads[1:]: l.wait()
    def wcol(a,b): return wa[:,:,:,a:b].reshape(1536,b-a)
    give_g.wait_recv()
    total=jnp.zeros((1,1536),f32)
    for i in range(4):
        r=i//2; a=pl.ds(128*(i%2),128); d=pl.ds(128*i,128)
        first=part.at[0,pl.ds(0,128)]; second=part.at[0,pl.ds(128,128)]; third=part.at[1,pl.ds(0,128)]
        moves=[pltpu.make_async_copy(f,g,lb.at[k]) for k,(f,g) in enumerate(((mid_h.at[r,a],first),(gnf_h.at[r,a],second),(xg.at[r,a],third),(cot_h.at[r,a],cb)))]
        for m in moves: m.start()
        for m in moves: m.wait()
        v=part[0,0:128,:]; gn=part[0,128:256,:]+part[1,0:128,:]
        s=lax.rsqrt(jnp.mean(v*v,axis=-1,keepdims=True)+epsilon)
        wg=gn*gains[1:2,:]
        g=cb[...].astype(f32)+(s*wg-v*(s*s*s)*jnp.mean(wg*v,axis=-1,keepdims=True))
        total=total+jnp.where(c==r,1.0,0.0)*jnp.sum(gn*v*s,axis=0,keepdims=True)
        part[1,128:256,:]=g
        @pl.when(c==r)
        def _():
            back=pltpu.make_async_copy(part.at[1,pl.ds(128,128)],gin_o.at[a],lb.at[4]); back.start(); back.wait()
        gat[:,d]=g.T.astype(low)
        gm[d,:]=dot(g.astype(low),wcol(0,384)).astype(low)
    ext[...]=jnp.zeros((128,1536),f32)
    def spread(v,row):
        upper=v.astype(low)
        ext[row:row+8,:]=upper.astype(f32)
        ext[row+8:row+16,:]=v-upper.astype(f32)
    spread(jnp.broadcast_to(total,(8,1536)),32)
    load_w=[pltpu.make_async_copy(w1,wa.at[:,:,:,pl.ds(0,768)],ll.at[13]),pltpu.make_async_copy(w2.at[:,:,:,pl.ds(0,384)],wa.at[:,:,:,pl.ds(768,384)],ll.at[15])]
    for l in load_w: l.start()
    step(0)
    dbias[...]=jnp.zeros((256,1280),f32)
    dtab[...]=jnp.zeros((8,1280),f32)
    at=1
    for h in range(6):
        odd=h%2; pair=pl.ds(128*(h//2),128); pp=h//2
        bias[...]=pltpu.roll(jnp.broadcast_to(base[h:h+1,:],(256,1280)),1024,1,stride=1,stride_axis=0)
        if not odd: acc[...]=jnp.zeros((2,2,1024,128),f32)
        def attend(i,_):
            r=i//2; d=pl.ds(pl.multiple_of(i*128,128),128)
            a=pl.ds(pl.multiple_of(lax.rem(i,2)*128,128),128)
            mine=(lanes((128,128))>=64) if odd else (lanes((128,128))<64)
            qh=jnp.where(mine,qq[d,pair].astype(f32),0.0).astype(low)
            gh=jnp.where(mine,gm[d,pair].astype(f32),0.0).astype(low)
            s=dot_nt(qh,kk[r,:,pair])+bias[a,0:1024]
            s=jnp.where(sc[r,a,0:1]==sr[r,0:1,:],s,-1000000000.0)
            pr=jnp.exp(s-lse[r,a,h:h+1])
            gp=dot_nt(gh,vv[r,:,pair])
            gl=(pr*(gp-jnp.sum(pr*gp,axis=-1,keepdims=True))).astype(low)
            wide=gl.astype(f32)
            dbias[a,0:1024]=wide+jnp.where(r==0,0.0,1.0)*dbias[a,0:1024]
            g=jnp.where(mine,dot(gl,kk[r,:,pair]),0.0)
            if odd: g=g+dq[d,pair].astype(f32)
            dq[d,pair]=g.astype(low)
            acc[0,r]=acc[0,r]+dot_tn(gl,qh)
            acc[1,r]=acc[1,r]+dot_tn(pr.astype(low),gh)
            return 0
        lax.fori_loop(0,4,attend,0)
        m=128
        v=dbias[0:128,:]+pltpu.roll(dbias[128:256,:],1280-128,1)
        while m>1:
            m//=2
            v=v[0:m]+pltpu.roll(v[m:2*m],1280-m,1)
        dtab[h:h+1,:]=pltpu.roll(v,256,1)
        if odd:
            for j in range(2):
                for r in range(2):
                    for zz in range(4):
                        dkv[pp,zz,j,r]=acc[j,r,256*zz:256*zz+256,:].astype(low)
            ka(pp).start()
            @pl.when(outer)
            def _(): kc(pp).start()
            step(at); at+=1
            if pp: relay(pp-1)
    tab=dtab[...]
    high=tab.astype(low); rest1=tab-high.astype(f32); mid1=rest1.astype(low); last=(rest1-mid1.astype(f32)).astype(low)
    shift=lax.broadcasted_iota(jnp.int32,(1280,128),0)-256-256*z
    spots=jnp.where(bucket_table(shift)==lanes((1280,128)),1.0,0.0).astype(low)
    tile=jnp.where(lax.rem(lanes((128,1536)),48)==lax.broadcasted_iota(jnp.int32,(128,1536),0),1.0,0.0).astype(low)
    found=dot(high,spots)+dot(mid1,spots)+dot(last,spots)
    upper=found.astype(low)
    ext[0:8,:]=dot(upper,tile)
    ext[8:16,:]=dot((found-upper.astype(f32)).astype(low),tile)
    give_y.wait_recv()
    for i in range(2):
        a=pl.ds(128*i,128)
        first=part.at[0,pl.ds(0,128)]; second=part.at[0,pl.ds(128,128)]; third=part.at[1,pl.ds(0,128)]
        moves=[pltpu.make_async_copy(f,g,lb.at[k]) for k,(f,g) in enumerate(((mid_h.at[c,a],first),(yy_h.at[c,a],second),(xy.at[a],third)))]
        for m in moves: m.start()
        for m in moves: m.wait()
        part[1,128:256,:]=part[0,0:128,:]+(part[0,128:256,:]+part[1,0:128,:])
        back=pltpu.make_async_copy(part.at[1,pl.ds(128,128)],bo_o.at[a],lb.at[4]); back.start(); back.wait()
    step(at); at+=1
    relay(2)
    while at<9:
        step(at); at+=1
    for pp in range(3):
        ka(pp).wait_recv(); kb(pp,0).wait_recv()
        for j,o in enumerate((dk,dv)):
            for r in range(2):
                v=dkv[pp,z,j,r].astype(f32)+rka[pp,j,r].astype(f32)+rkb[pp,j,r].astype(f32)
                o[256*r:256*r+256,128*pp:128*pp+128]=v.astype(low)
    step(at); at+=1
    for l in load_w: l.wait()
    def input_grad(i,_):
        d=pl.ds(pl.multiple_of(i*128,128),128); a=pl.ds(pl.multiple_of(lax.rem(i,2)*128,128),128)
        part[i//2,a,:]=dot_nt(dq[d,:],wcol(0,384))+dot_nt(dk[d,:],wcol(384,768))+dot_nt(dv[d,:],wcol(768,1152))
        return 0
    lax.fori_loop(0,4,input_grad,0)
    give=remote(part.at[1-c],r3,xs.at[0],xr.at[0],sib); give.start()
    step(at); at+=1
    give.wait_send()
    load_i=pltpu.make_async_copy(gin_o,part.at[1-c],lb.at[0]); load_i.start()
    give.wait_recv(); load_i.wait()
    def last_grad(i,total):
        a=pl.ds(pl.multiple_of(i*128,128),128)
        v=hid[a,:].astype(f32); gn=part[c,a,:]+r3[a,:]
        s=lax.rsqrt(jnp.mean(v*v,axis=-1,keepdims=True)+epsilon)
        wg=gn*gains[0:1,:]
        part[1-c,a,:]=part[1-c,a,:]+(s*wg-v*(s*s*s)*jnp.mean(wg*v,axis=-1,keepdims=True))
        return total+jnp.sum(gn*v*s,axis=0,keepdims=True)
    total=lax.fori_loop(0,2,last_grad,jnp.zeros((1,1536),f32))
    spread(jnp.broadcast_to(total,(8,1536)),16)
    give_i=pltpu.make_async_copy(part.at[1-c],gin_o,ll.at[12]); give_i.start()
    while at<n+lag:
        step(at); at+=1
    for t in range(n):
        arrive(t)
        if t>=n-sum_slots: drain(t)
        if t>=n-part_slots:
            went(t,hop1)
        went(t,hop2); went(t,hop3)
    for pp in range(3):
        ka(pp).wait_send()
        @pl.when(outer)
        def _(): kc(pp).wait_send()
        @pl.when(inner)
        def _(): kb(pp,0).wait_send(); kb(pp,1).wait_send()
    give_i.wait(); give_g.wait_send(); give_y.wait_send()

def backward_chunks(ff_steps,ff):
    fw=512*ff_steps
    chunks=[]
    for j in range(ff_steps):
        for left,i,o in ((0,1,0),(0,2,1),(1,0,2)):
            chunks.append((left,0,512,("feed",i,j),(o,512*j,(512,fw),ff)))
    for k in range(4): chunks.append((3 if k==0 else 1,0,384,("ref",k,0),(3+k,0,(384,384),768)))
    chunks.append((1,0,128,("ref",4,0),(7,0,(128,128),256)))
    return chunks

def backward_call(w1,w2,lt,hdg,q,kk,vv,mx,lse,gnf,yy,mid,cot,segr,segc,hid,base,gains,ff_steps,ff,cid=1):
    chunks=backward_chunks(ff_steps,ff); n=len(chunks)
    S=jax.ShapeDtypeStruct; V=pltpu.VMEM; D=pltpu.SemaphoreType.DMA
    hbm=pl.BlockSpec(memory_space=pltpu.HBM); vm=pl.BlockSpec(memory_space=pltpu.VMEM)
    ws=[k[2] for k in chunks]
    scratch=[V((2,4,48,k),low) for k in ws]*1+[V((2,4,48,k),low) for k in ws]+[V((4,48,k),low) for k in ws]+[V((4,48,k),low) for k in ws]+[V((3,2,48,k),low) for k in ws]
    scratch+=[V((sum_slots,2,48,512),f32),V((part_slots,2,2,2,4,48,512),low),V((2,1536,512),low),V((1536,512),low),V((2,512,512),low),V((8,4,48,1152),low),
      V((512,384),low),V((2,1024,384),low),V((2,1024,384),low),V((512,384),low),V((512,384),low),V((2,256,128),f32),V((2,8,1024),f32),V((2,256,128),f32),
      V((256,1280),f32),V((256,1280),f32),V((512,384),low),V((2,2,1024,128),f32),V((3,4,2,2,256,128),low),V((3,2,2,256,128),low),V((3,2,2,256,128),low),V((3,2,2,2,256,128),low),V((512,384),low),V((512,384),low),
      V((2,256,1536),f32),V((256,1536),f32),V((256,1536),low),V((8,1280),f32),V((128,1536),f32),V((128,1536),low)]
    scratch+=[D((16,)),D((n,)),D((n,)),D((n,2)),D((n,2)),D((n,2)),D((n,2)),D((n,3,2)),D((n,3,2)),D((n,)),D((n,)),D((3,4)),D((3,3)),D((3,)),D((3,)),D((5,))]
    return pl.pallas_call(functools.partial(backward_kernel,chunks,ff_steps),out_shape=(S((48,ff),f32),)*3+(S((48,768),f32),)*4+(S((48,256),f32),S((256,1536),f32),S((256,1536),f32),S((2,256,1536),f32),S((256,1536),f32)),
        in_specs=[hbm]*16+[vm]*2,out_specs=(hbm,)*12,scratch_shapes=scratch,
        compiler_params=pltpu.CompilerParams(collective_id=cid,has_side_effects=True,vmem_limit_bytes=62*2**20))(w1,w2,lt,hdg,q,kk,vv,mx,lse,gnf,yy,mid,cot,segr,segc,hid,base,gains)

def cut(v,h,w):
    n=v.shape[1]
    a=min(h*w,n); b=min((h+1)*w,n)
    p=v[:,a:b]
    return jnp.pad(p,((0,0),(0,w-(b-a)))) if b-a<w else p
def pack(wq,wk,wv,wo,ga,gf,wg,wu,wd,steps):
    gains=jnp.pad(jnp.stack([ga,gf],axis=1),((0,0),(0,126)))
    fw=512*steps
    rows=[]
    for h in (0,1):
        m=[cut(v,h,384) for v in (wq,wk,wv,wo.T)]+[gains]
        f=[cut(v,h,fw) for v in (wg,wu,wd.T)]
        for j in range(steps):
            m+=[v[:,512*j:512*j+512] for v in f]
        rows.append(jnp.concatenate(m,axis=1))
    return jnp.stack(rows)
def seg_ids(seg):
    n=seg.shape[1]
    place=jnp.arange(n,dtype=jnp.int32)
    ids=jnp.where(seg[0]>0,seg[0],-1-place).astype(jnp.float32)
    r=jnp.broadcast_to(ids[None],(8,n))
    mine=lax.dynamic_slice_in_dim(ids,lax.axis_index("seq")*256,256,0)
    return r, jnp.broadcast_to(mine[:,None],(256,128))
def base_of(table):
    off=jnp.arange(1280,dtype=jnp.int32)-256-256*lax.axis_index("seq")
    oh=(bucket_table(off)[:,None]==jnp.arange(32,dtype=jnp.int32)).astype(jnp.float32)
    c=lax.rem(lax.axis_index("dp"),2)
    tab=table.astype(jnp.float32)
    mine=jnp.where(c==0,tab[:,:6],tab[:,6:])
    b=jnp.einsum("ub,bh->hu",oh,mine,precision=lax.Precision.HIGHEST)
    return jnp.pad(b,((0,2),(0,0))), oh

def kernel_local(hid,seg,ga,wq,wk,wv,wo,tab,gf,wg,wu,wd,cot):
    ff=wg.shape[1]; steps=-(-ff//1024)
    gain_cols=jnp.pad(jnp.stack([ga,gf],axis=1),((0,0),(0,126)))
    r,s=seg_ids(seg); b=base_of(tab)[0]
    w1,w2,w,lt,hdg,q,kk,vv,mx,lse,gnf,yy,gains,segr,segc,mid,cot2=forward_call((wq,wk,wv,wo.T,wg,wu,wd.T),gain_cols,hid[0],cot[0],r,s,b,steps)
    og,ou,od,oo,oq,ok,ov,oe,gin,bo,_,_=backward_call(w1,w2,lt,hdg,q,kk,vv,mx,lse,gnf,yy,mid,cot2,segr,segc,hid[0],b,gains,steps,ff)
    e=oe.reshape(48,2,128)
    t=e[:32,:,0:8]+e[:32,:,8:16]
    table=t[:,:,:6].reshape(32,12)
    g=e[:,0]+e[:,1]
    gg=lambda a: g[:,a]+g[:,a+8]
    return (bo[None],gin[None],gg(16),oq,ok,ov,oo.T,table,gg(32),og,ou,od.T)


def solution(mesh):
    in_specs = (
        P("dp", "seq", None),
        P("dp", None),
        P(("dp", "seq")),
        P(("dp", "seq"), None),
        P(("dp", "seq"), None),
        P(("dp", "seq"), None),
        P(None, ("dp", "seq")),
        P(),
        P(("dp", "seq")),
        P(("dp", "seq"), None),
        P(("dp", "seq"), None),
        P(None, ("dp", "seq")),
        P("dp", "seq", None),
    )
    out_specs = (
        P("dp", "seq", None),
        P("dp", "seq", None),
        P(("dp", "seq")),
        P(("dp", "seq"), None),
        P(("dp", "seq"), None),
        P(("dp", "seq"), None),
        P(None, ("dp", "seq")),
        P(),
        P(("dp", "seq")),
        P(("dp", "seq"), None),
        P(("dp", "seq"), None),
        P(None, ("dp", "seq")),
    )
    small = mesh.shape["dp"] == 8 and mesh.shape["seq"] == 4
    local = kernel_local if small else plain_local
    return jax.shard_map(local, mesh=mesh, in_specs=in_specs, out_specs=out_specs, check_vma=False)
```

```python
import functools

import jax
import jax.numpy as jnp
from jax import lax
from jax.experimental import pallas as pl
from jax.experimental.pallas import tpu as pltpu
from jax.sharding import PartitionSpec as P

epsilon = 1e-06
far_bounds = (12, 16, 23, 32, 46, 64, 91)
highest = lax.Precision.HIGHEST
mesh_ids = pl.DeviceIdType.MESH


def bucket_table(offset):
    magnitude = jnp.abs(offset)
    distant = 8 + sum(((magnitude >= bound).astype(jnp.int32) for bound in far_bounds))
    signed_part = jnp.where(offset > 0, 16, 0).astype(jnp.int32)
    return signed_part + jnp.where(magnitude < 8, magnitude, distant)


def norm_scale(hidden):
    return lax.rsqrt(jnp.mean(hidden * hidden, axis=-1, keepdims=True) + epsilon)


def norm_backward(grad_normed, hidden, scale, gain):
    weighted = grad_normed * gain
    grad_gain = jnp.sum(grad_normed * hidden * scale, axis=0)
    grad_hidden = scale * weighted - hidden * (scale * scale * scale) * jnp.mean(
        weighted * hidden, axis=-1, keepdims=True
    )
    return (grad_hidden, grad_gain)


def scores_of(query_heads, key_heads, bias, allowed):
    raw_scores = jnp.einsum(
        "rqhd,rkhd->rhqk", query_heads, key_heads, preferred_element_type=jnp.float32
    )
    return jnp.where(allowed, raw_scores + bias[None], -1000000000.0)


def gather_rows(shard):
    return lax.all_gather(shard, ("dp", "seq"), axis=0, tiled=True)


def scatter_sum(parts):
    data_count = lax.axis_size("dp")
    piece_count = lax.axis_size("seq")
    shard_width = parts.shape[0] // (data_count * piece_count)
    split = parts.reshape(data_count, piece_count, shard_width, parts.shape[1])
    half = lax.psum_scatter(split, "dp", scatter_dimension=0, tiled=True)
    return lax.psum_scatter(half, "seq", scatter_dimension=1, tiled=True)[0, 0]


def plain_sums(pairs, extra):
    found = []
    for left, rights in pairs:
        for right in rights:
            part = jnp.einsum("td,tf->df", left, right, preferred_element_type=jnp.float32)
            found.append(scatter_sum(part.astype(jnp.bfloat16)).astype(jnp.float32))
    return found, scatter_sum(extra.astype(jnp.bfloat16)).astype(jnp.float32)


def plain_local(
    hidden_in,
    segment_ids,
    gain_attn,
    w_query,
    w_key,
    w_value,
    w_out,
    rel_table,
    gain_ff,
    w_gate,
    w_up,
    w_down,
    cotangent,
):
    row_count, local_len, model_width = hidden_in.shape
    row_length = segment_ids.shape[1]
    bucket_count, head_count = rel_table.shape
    token_count = row_count * local_len
    data_count = lax.axis_size("dp")
    piece_count = lax.axis_size("seq")
    shard_width = model_width // (data_count * piece_count)
    first_place = lax.axis_index("seq") * local_len
    query_place = first_place + jnp.arange(local_len, dtype=jnp.int32)
    key_place = jnp.arange(row_length, dtype=jnp.int32)
    buckets = bucket_table(key_place[None, :] - query_place[:, None])
    onehot = (buckets[:, :, None] == jnp.arange(bucket_count, dtype=jnp.int32)).astype(jnp.float32)
    bias = jnp.einsum("qkb,bh->hqk", onehot, rel_table.astype(jnp.float32), precision=highest)
    query_segs = lax.dynamic_slice_in_dim(segment_ids, first_place, local_len, 1)
    same_doc = query_segs[:, :, None] == segment_ids[:, None, :]
    visible = (segment_ids[:, None, :] > 0) | (query_place[:, None] == key_place[None, :])[None]
    allowed = (same_doc & visible)[:, None]
    inner = w_query.shape[1]
    ff_width = w_gate.shape[1]
    gains = jnp.pad(jnp.stack([gain_attn, gain_ff], axis=1), ((0, 0), (0, 126)))
    attn_full = gather_rows(jnp.concatenate([w_query, w_key, w_value, w_out.T, gains], axis=1))
    feed_full = gather_rows(jnp.concatenate([w_gate, w_up, w_down.T], axis=1))
    query_full = attn_full[:, :inner]
    key_full = attn_full[:, inner : 2 * inner]
    value_full = attn_full[:, 2 * inner : 3 * inner]
    out_full = attn_full[:, 3 * inner : 4 * inner].T
    gain_one = attn_full[:, 4 * inner]
    gain_two = attn_full[:, 4 * inner + 1]
    gate_full = feed_full[:, :ff_width]
    up_full = feed_full[:, ff_width : 2 * ff_width]
    down_full = feed_full[:, 2 * ff_width :].T
    gain_first = gain_one.astype(jnp.float32)
    residual_in = hidden_in.astype(jnp.float32).reshape(token_count, model_width)
    scale_first = norm_scale(residual_in)
    normed_first = (residual_in * scale_first * gain_first).astype(jnp.bfloat16)
    queries = jnp.dot(normed_first, query_full, preferred_element_type=jnp.float32).astype(
        jnp.bfloat16
    )
    keys_local = jnp.dot(normed_first, key_full, preferred_element_type=jnp.float32).astype(
        jnp.bfloat16
    )
    values_local = jnp.dot(normed_first, value_full, preferred_element_type=jnp.float32).astype(
        jnp.bfloat16
    )
    head_size = inner // head_count
    keys_row, values_row = (
        lax.all_gather(keys_local.reshape(row_count, local_len, inner), "seq", axis=1, tiled=True),
        lax.all_gather(
            values_local.reshape(row_count, local_len, inner), "seq", axis=1, tiled=True
        ),
    )
    query_heads = queries.reshape(row_count, local_len, head_count, head_size)
    key_heads = keys_row.reshape(row_count, row_length, head_count, head_size)
    value_heads = values_row.reshape(row_count, row_length, head_count, head_size)
    logits = scores_of(query_heads, key_heads, bias, allowed)
    row_max = jnp.max(logits, axis=-1, keepdims=True)
    exp_scores = jnp.exp(logits - row_max)
    denominator = jnp.sum(exp_scores, axis=-1, keepdims=True)
    probs_low = (exp_scores / denominator).astype(jnp.bfloat16)
    log_total = row_max + jnp.log(denominator)
    mixed = (
        jnp.einsum("rhqk,rkhd->rqhd", probs_low, value_heads, preferred_element_type=jnp.float32)
        .astype(jnp.bfloat16)
        .reshape(token_count, inner)
    )
    middle = residual_in + jnp.dot(mixed, out_full, preferred_element_type=jnp.float32)
    gain_second = gain_two.astype(jnp.float32)
    scale_second = norm_scale(middle)
    normed_second = (middle * scale_second * gain_second).astype(jnp.bfloat16)
    gate_pre = jnp.dot(normed_second, gate_full, preferred_element_type=jnp.float32)
    up_pre = jnp.dot(normed_second, up_full, preferred_element_type=jnp.float32)
    activated = jax.nn.gelu(gate_pre, approximate=True)
    hidden_mid = (activated * up_pre).astype(jnp.bfloat16)
    block_out = middle + jnp.dot(hidden_mid, down_full, preferred_element_type=jnp.float32)
    gain_second = gain_two.astype(jnp.float32)
    grad_out = cotangent.reshape(token_count, model_width)
    grad_hidden = (
        jnp.einsum("td,fd->tf", grad_out, down_full, preferred_element_type=jnp.float32)
        .astype(jnp.bfloat16)
        .astype(jnp.float32)
    )
    gelu_value, gelu_pull = jax.vjp(lambda value: jax.nn.gelu(value, approximate=True), gate_pre)
    grad_gate = gelu_pull(grad_hidden * up_pre)[0].astype(jnp.bfloat16)
    grad_up = (grad_hidden * gelu_value).astype(jnp.bfloat16)
    grad_normed_second = jnp.einsum(
        "tf,df->td", grad_gate, gate_full, preferred_element_type=jnp.float32
    ) + jnp.einsum("tf,df->td", grad_up, up_full, preferred_element_type=jnp.float32)
    grad_middle_norm, grad_gain_two = norm_backward(
        grad_normed_second, middle, scale_second, gain_second
    )
    grad_middle = grad_out.astype(jnp.float32) + grad_middle_norm
    grad_attended = grad_middle.astype(jnp.bfloat16)
    grad_mixed = jnp.einsum(
        "td,id->ti", grad_attended, out_full, preferred_element_type=jnp.float32
    ).astype(jnp.bfloat16)
    grad_heads = grad_mixed.reshape(row_count, local_len, head_count, head_size)
    logits_again = scores_of(query_heads, key_heads, bias, allowed)
    probs_again = jnp.exp(logits_again - log_total)
    probs_again_low = probs_again.astype(jnp.bfloat16)
    grad_probs = jnp.einsum(
        "rqhd,rkhd->rhqk", grad_heads, value_heads, preferred_element_type=jnp.float32
    )
    row_dot = jnp.sum(probs_again * grad_probs, axis=-1, keepdims=True)
    grad_logits = (probs_again * (grad_probs - row_dot)).astype(jnp.bfloat16)
    grad_bias = jnp.sum(grad_logits.astype(jnp.float32), axis=0)
    grad_table = jnp.einsum("qkb,hqk->bh", onehot, grad_bias, precision=highest)
    grad_queries = (
        jnp.einsum("rhqk,rkhd->rqhd", grad_logits, key_heads, preferred_element_type=jnp.float32)
        .astype(jnp.bfloat16)
        .reshape(token_count, inner)
    )
    grad_keys_row = jnp.einsum(
        "rhqk,rqhd->rkhd", grad_logits, query_heads, preferred_element_type=jnp.float32
    )
    grad_values_row = jnp.einsum(
        "rhqk,rqhd->rkhd", probs_again_low, grad_heads, preferred_element_type=jnp.float32
    )
    grad_keys_part, grad_values_part = (
        lax.psum_scatter(
            grad_keys_row.astype(jnp.bfloat16), "seq", scatter_dimension=1, tiled=True
        ).astype(jnp.float32),
        lax.psum_scatter(
            grad_values_row.astype(jnp.bfloat16), "seq", scatter_dimension=1, tiled=True
        ).astype(jnp.float32),
    )
    grad_keys = grad_keys_part.astype(jnp.bfloat16).reshape(token_count, inner)
    grad_values = grad_values_part.astype(jnp.bfloat16).reshape(token_count, inner)
    grad_normed_first = jnp.einsum(
        "ti,di->td", grad_queries, query_full, preferred_element_type=jnp.float32
    )
    grad_normed_first = grad_normed_first + jnp.einsum(
        "ti,di->td", grad_keys, key_full, preferred_element_type=jnp.float32
    )
    grad_normed_first = grad_normed_first + jnp.einsum(
        "ti,di->td", grad_values, value_full, preferred_element_type=jnp.float32
    )
    grad_first, grad_gain_one = norm_backward(
        grad_normed_first, residual_in, scale_first, gain_first
    )
    grad_input = grad_middle + grad_first
    device_count = data_count * piece_count
    table_size = bucket_count * head_count
    table_rows = -(-table_size // shard_width)
    table_block = jnp.pad(grad_table.reshape(-1), (0, table_rows * shard_width - table_size))
    table_block = jnp.broadcast_to(
        table_block.reshape(1, table_rows, shard_width), (device_count, table_rows, shard_width)
    )
    gain_block = jnp.stack([grad_gain_one, grad_gain_two], axis=0)
    gain_block = gain_block.reshape(2, device_count, shard_width).transpose(1, 0, 2)
    extra = jnp.concatenate([table_block, gain_block], axis=1).transpose(0, 2, 1)
    extra = extra.reshape(model_width, table_rows + 2)
    extra = jnp.pad(extra, ((0, 0), (0, -(table_rows + 2) % 128)))
    pairs = (
        (normed_second, (grad_gate, grad_up)),
        (grad_out, (hidden_mid,)),
        (grad_attended, (mixed,)),
        (normed_first, (grad_queries, grad_keys, grad_values)),
    )
    (gate_sum, up_sum, down_sum, out_sum, query_sum, key_sum, value_sum), extra_sum = plain_sums(
        pairs, extra
    )
    table_total = extra_sum[:, :table_rows].T.reshape(-1)[:table_size]
    table_total = table_total.reshape(bucket_count, head_count)
    grad_gain_one_shard = extra_sum[:, table_rows]
    grad_gain_two_shard = extra_sum[:, table_rows + 1]
    return (
        block_out.reshape(row_count, local_len, model_width),
        grad_input.reshape(row_count, local_len, model_width),
        grad_gain_one_shard,
        query_sum,
        key_sum,
        value_sum,
        out_sum.T,
        table_total,
        grad_gain_two_shard,
        gate_sum,
        up_sum,
        down_sum.T,
    )


gelu_c=0.7978845608028654

def peers_of():
    dp=lax.axis_index("dp"); z=lax.axis_index("seq")
    c=lax.rem(dp,2); x=lax.rem(dp//2,2); y=dp//4
    return dp,z,c,x,y

def remote(src,dst,ss,rs,dev):
    return pltpu.make_async_remote_copy(src_ref=src,dst_ref=dst,send_sem=ss,recv_sem=rs,device_id=dev,device_id_type=mesh_ids)

def dot(a,b):
    return jnp.dot(a,b,preferred_element_type=jnp.float32)

def dot_nt(a,b):
    return lax.dot_general(a,b,(((1,),(1,)),((),())),preferred_element_type=jnp.float32)

def lanes(shape):
    return lax.broadcasted_iota(jnp.int32,shape,len(shape)-1)

def greet(devices):
    bar=pltpu.get_barrier_semaphore()
    for d in devices: pl.semaphore_signal(bar,inc=1,device_id=d,device_id_type=mesh_ids)
    return lambda: pl.semaphore_wait(bar,len(devices))

low=jnp.bfloat16
f32=jnp.float32

h_parts=4
across_first=2
def forward_kernel(ff_steps, w_q, w_k, w_v, w_o, w_g, w_u, w_d, gains, hid, cot, segr, segc, base,
                   w1, w2, w, lt_o, hdg_o, q_o, kk_o, vv_o, mx_o, lse_o, gnf_o, yy_o, gs_o, segr_o, segc_o, mid_o, cot_o,
                   hrow, cotv, sr, sc, wa, wf, qq, kk, vv, mx, lse, bias, part, mid, n2, hd, yy, lt, gs, r1, wp,
                   s0s, s0r, l0, s1s, s1r, s2s, s2r, s3s, s3r, hs, hr, xs, xr, ks, kr, ll, lo):
    cols=[(0,768),(768,896)]+[(1664+512*i,512) for i in range(3*ff_steps)]
    n=len(cols)
    dp,z,c,x,y=peers_of()
    q=dp//2; qx=2*y+1-x; qy=lax.rem(q+2,4); qd=3-q
    sib=(dp+1-2*c,z); dx=(2*qx+c,z); dy=(2*qy+c,z); dxy=(dx,dy)
    zb=lax.rem(z,2); pe=z+1-2*zb; mo=2-z//2; zo=2-2*(z//2)
    inner=(z==1)|(z==2); outer=(z==0)|(z==3)
    dpe=(dp,pe); dmo=(dp,mo)
    all_in=greet([sib,dx,dy]+[(dp,lax.rem(z+k,4)) for k in (1,2,3)])
    def cs(t): return pl.ds(cols[t][0],cols[t][1])
    def wr(t): return (w1,w2)[t] if t<2 else w.at[t-2]
    def s0(t,recv=False):
        return remote(wp.at[1-c,:,cs(t)], wr(t).at[(dp+1-2*c) if recv else dp,z], s0s.at[t], s0r.at[t], sib)
    def keep(t): return pltpu.make_async_copy(wp.at[c,:,cs(t)], wr(t).at[dp,z], l0.at[t])
    across=set(range(n-across_first,n))
    def group(t): return pl.ds(0,8) if t in across else pl.ds(2*q,2)
    def span(t): return z if t in across else pl.ds(0,4)
    tail=w_g.shape[1]-512*(2*ff_steps-1)
    narrow=set(range(n-3,n)) if 0<tail<512 and tail%128==0 else set()
    def each(t,act):
        if t in narrow:
            @pl.when(c==0)
            def _(): act(512)
            @pl.when(c==1)
            def _(): act(tail)
        else: act(cols[t][1])
    def s1a(t,wd,recv=False):
        r=wr(t).at[group(t), pe if recv else z, :, pl.ds(0,wd)]
        return remote(r,r,s1s.at[t,0],s1r.at[t,0],dpe)
    def s1b(t,wd):
        r=wr(t).at[group(t), z, :, pl.ds(0,wd)]
        return remote(r,r,s1s.at[t,1],s1r.at[t,1+zb],dmo)
    def s1bw(t,k,wd):
        r=wr(t).at[group(t), zo+k, :, pl.ds(0,wd)]
        return remote(r,r,s1s.at[t,1],s1r.at[t,1+k],dmo)
    def s1c(t,wd):
        r=wr(t).at[group(t), pl.ds(zo,2), :, pl.ds(0,wd)]
        return remote(r,r,s1s.at[t,2],s1r.at[t,3],dpe)
    def s2(t,a,wd,recv=False):
        r=wr(t).at[pl.ds(2*((qx,qy)[a] if recv else q),2), span(t), :, pl.ds(0,wd)]
        return remote(r,r,s2s.at[t,a],s2r.at[t,a],dxy[a])
    def s3(t,a,wd,recv=False):
        r=wr(t).at[2*(qd if recv else (qy,qx)[a])+a, span(t), :, pl.ds(0,wd)]
        return remote(r,r,s3s.at[t,a],s3r.at[t,a],dxy[a])
    def z_go(t): each(t,lambda wd: (s1a(t,wd).start(),s1b(t,wd).start()))
    def z_on(t):
        @pl.when(inner)
        def _(): each(t,lambda wd: (s1bw(t,0,wd).wait_recv(),s1bw(t,1,wd).wait_recv(),s1c(t,wd).start()))
    def z_in(t):
        each(t,lambda wd: s1a(t,wd,True).wait_recv())
        @pl.when(outer)
        def _(): each(t,lambda wd: s1c(t,wd).wait_recv())
    def xy_go(t,f): each(t,lambda wd: [f(t,a,wd).start() for a in range(2)])
    def xy_in(t,f): each(t,lambda wd: [f(t,a,wd,True).wait_recv() for a in range(2)])
    hp=hrow.shape[2]//h_parts
    def ht(p): return pl.ds(p*hp,hp)
    def ha(p,recv=False): return remote(hid.at[ht(p)],hrow.at[c,pe if recv else z,ht(p)],hs.at[p,0],hr.at[p,0],dpe)
    def hb(p): return remote(hid.at[ht(p)],hrow.at[c,z,ht(p)],hs.at[p,1],hr.at[p,1+zb],dmo)
    def hbw(p,k): return remote(hid.at[ht(p)],hrow.at[c,zo+k,ht(p)],hs.at[p,1],hr.at[p,1+k],dmo)
    def hc(p):
        r=hrow.at[c,pl.ds(zo,2),ht(p)]
        return remote(r,r,hs.at[p,2],hr.at[p,3],dpe)
    done=set()
    def once(*k):
        if k in done: return False
        done.add(k); return True
    def start1(t):
        if t<n and t not in across and once(1,t):
            keep(t).wait(); s0(t,True).wait_recv(); z_go(t)
    def across1(t):
        keep(t).wait(); s0(t,True).wait_recv(); xy_go(t,s2)
    def across2(t): xy_in(t,s2); xy_go(t,s3)
    def across3(t): xy_in(t,s3); z_go(t)
    def across4(t): z_on(t)
    def across5(t): z_in(t)
    def forward(t):
        if t<n and t not in across and once(5,t): z_on(t)
    def start2(t):
        forward(t)
        if t<n and t not in across and once(2,t):
            z_in(t); xy_go(t,s2)
    def start3(t):
        if 0<=t<n and t not in across and once(3,t):
            xy_in(t,s2); xy_go(t,s3)
    def finish(t):
        if 0<=t<n and t not in across and once(4,t): xy_in(t,s3)
    def advance(t):
        for u in range(t+4): start1(u)
        for f,u in ((forward,t+1),(start2,t),(start3,t-1),(finish,t-2)):
            for v in range(u+1): f(v)
    def h_go(p): ha(p).start(); hb(p).start()
    def h_on(p):
        @pl.when(inner)
        def _():
            hbw(p,0).wait_recv(); hbw(p,1).wait_recv(); hc(p).start()
    for h in range(2):
        for i,v in enumerate((w_q,w_k,w_v,w_o)): wp[h,:,384*i:384*i+384]=v[:,384*h:384*h+384]
        wp[h,:,1536:1664]=jnp.zeros((48,128),low)
        wp[h,:,1536:1538]=gains[...]
        for j in range(ff_steps):
            for i,v in enumerate((w_g,w_u,w_d)):
                a=1664+1536*j+512*i; f=512*(ff_steps*h+j); g=min(512,v.shape[1]-f)
                if g>0: wp[h,:,a:a+g]=v[:,f:f+g]
                if g<512: wp[h,:,a+max(g,0):a+512]=jnp.zeros((48,512-max(g,0)),low)
    keep_h=pltpu.make_async_copy(hid,hrow.at[c,z],ll.at[0]); keep_h.start()
    keep_c=pltpu.make_async_copy(cot,cotv.at[c],ll.at[1]); keep_c.start()
    keep_r=pltpu.make_async_copy(segr,sr.at[c],ll.at[2]); keep_r.start()
    keep_s=pltpu.make_async_copy(segc,sc.at[c],ll.at[3]); keep_s.start()
    for t in range(n): keep(t).start()
    all_in()
    for t in [*range(3),*sorted(across)]: s0(t).start()
    give_h=[remote(hid,hrow.at[c,z],xs.at[3],xr.at[3],sib)]; give_h[0].start()
    give_c=remote(cot,cotv.at[c],xs.at[0],xr.at[0],sib); give_c.start()
    give_r=remote(segr,sr.at[c],xs.at[1],xr.at[1],sib); give_r.start()
    give_s=remote(segc,sc.at[c],xs.at[2],xr.at[2],sib); give_s.start()
    for t in range(3,n-across_first): s0(t).start()
    start1(0); start1(1); start1(2); h_go(0)
    for t in sorted(across): across1(t)
    forward(0); start2(0); forward(1); start2(1); forward(2)
    h_on(0); start1(3); h_go(1)
    for t in sorted(across): across2(t)
    start3(0); start2(2)
    keep_h.wait(); keep_c.wait(); keep_r.wait(); keep_s.wait()
    remote(segr,sr.at[1-c],xs.at[1],xr.at[1],sib).wait_recv()
    remote(segc,sc.at[1-c],xs.at[2],xr.at[2],sib).wait_recv()
    remote(cot,cotv.at[1-c],xs.at[0],xr.at[0],sib).wait_recv()
    remote(hid,hrow.at[1-c,z],xs.at[3],xr.at[3],sib).wait_recv()
    start3(1); forward(3); h_on(1); start1(4); h_go(2)
    finish(0); finish(1)
    load_a=[pltpu.make_async_copy(w1,wa.at[:,:,:,pl.ds(0,768)],ll.at[4]),pltpu.make_async_copy(w2,wa.at[:,:,:,pl.ds(768,896)],ll.at[11])]
    for l in load_a: l.start()
    start3(2); start2(3); forward(4); h_on(2); start1(5); h_go(3)
    for l in load_a: l.wait()
    def wcol(a,b): return wa[:,:,:,a:b].reshape(1536,b-a)
    pick=(lanes((8,128))==lax.broadcasted_iota(jnp.int32,(8,128),0)).astype(low)
    gs[...]=dot_nt(pick,wcol(1536,1664))
    def transpose_cot(i,_):
        lt[2,:,pl.ds(pl.multiple_of(i*128,128),128)]=cotv[i//2,pl.ds(pl.multiple_of(lax.rem(i,2)*128,128),128),:].astype(f32).T.astype(low)
        return 0
    lax.fori_loop(0,4,transpose_cot,0)
    def normed(v,row):
        s=lax.rsqrt(jnp.mean(v*v,axis=-1,keepdims=True)+epsilon)
        return v*s*gs[row:row+1,:]
    def queries(i,_):
        a=pl.ds(pl.multiple_of(lax.rem(i,2)*128,128),128)
        v=normed(hrow[i//2,z,a,:].astype(f32),0)
        d=pl.ds(pl.multiple_of(i*128,128),128)
        qq[d,:]=dot(v.astype(low),wcol(0,384)).astype(low)
        lt[0,:,d]=v.T.astype(low)
        return 0
    lax.fori_loop(0,4,queries,0)
    def share(p,k,recv=False):
        r=hrow.at[1-c if recv else c,lax.rem(z+k,4),ht(p)]
        return remote(r,r,ks.at[p,k-1],kr.at[p,k-1],sib)
    def keys(r,p):
        v=jnp.concatenate([normed(hrow[r,zz,p*hp:p*hp+hp,:].astype(f32),0).astype(low) for zz in range(4)],axis=0)
        for o,w0 in ((kk,384),(vv,768)):
            d=dot(v,wcol(w0,w0+384)).astype(low)
            for zz in range(4): o[r,256*zz+p*hp:256*zz+p*hp+hp,:]=d[zz*hp:zz*hp+hp]
    def arrive(p):
        ha(p,True).wait_recv()
        @pl.when(outer)
        def _(): hc(p).wait_recv()
        for k in (1,2,3): share(p,k).start()
        keys(c,p)
    def other(p):
        for k in (1,2,3): share(p,k,True).wait_recv()
        keys(1-c,p)
    arrive(0)
    start2(4); start3(3); finish(2); forward(5); h_on(3)
    arrive(1); other(0)
    start2(5); start3(4)
    arrive(2); other(1)
    arrive(3); other(2); other(3)
    advance(6)
    for t in sorted(across)[:1]: across3(t)
    for h in range(6):
        pair=pl.ds(128*(h//2),128); odd=h%2
        bias[...]=pltpu.roll(jnp.broadcast_to(base[h:h+1,:],(256,1280)),1024,1,stride=1,stride_axis=0)
        def attend(i,_):
            r=i//2; d=pl.ds(pl.multiple_of(i*128,128),128)
            a=pl.ds(pl.multiple_of(lax.rem(i,2)*128,128),128)
            mine=(lanes((128,128))>=64) if odd else (lanes((128,128))<64)
            qh=jnp.where(mine,qq[d,pair].astype(f32),0.0).astype(low)
            s=dot_nt(qh,kk[r,:,pair])+bias[a,0:1024]
            s=jnp.where(sc[r,a,0:1]==sr[r,0:1,:],s,-1000000000.0)
            m=jnp.max(s,axis=-1,keepdims=True)
            e=jnp.exp(s-m)
            l=jnp.sum(e,axis=-1,keepdims=True)
            p=(e*(1.0/l)).astype(low)
            o=dot(p,vv[r,:,pair])
            if odd: o=jnp.where(mine,o,mx[d,pair].astype(f32))
            mx[d,pair]=o.astype(low)
            lse[r,a,:]=jnp.where(lanes((128,128))==h,m+jnp.log(l),lse[r,a,:]) if h else jnp.broadcast_to(m+jnp.log(l),(128,128))
            return 0
        lax.fori_loop(0,4,attend,0)
        if h in (1,3): advance(7+h//2)
        if h==3:
            for t in sorted(across)[:1]: across4(t)
            for t in sorted(across)[1:]: across3(t)
    def project(i,_):
        part[i//2,pl.ds(pl.multiple_of(lax.rem(i,2)*128,128),128),:]=dot_nt(mx[pl.ds(pl.multiple_of(i*128,128),128),:],wcol(1152,1536))
        return 0
    lax.fori_loop(0,4,project,0)
    give_p=remote(part,r1,xs.at[4],xr.at[4],sib); give_p.start()
    advance(9)
    outs=[pltpu.make_async_copy(a,b,lo.at[i]) for i,(a,b) in enumerate(((qq,q_o),(kk,kk_o),(vv,vv_o),(mx,mx_o),(lse,lse_o),(sr,segr_o),(sc,segc_o),(cotv,cot_o)))]
    for o in outs: o.start()
    give_p.wait_recv()
    def middle(i,_):
        a=pl.ds(pl.multiple_of(lax.rem(i,2)*128,128),128); r=i//2
        d=pl.ds(pl.multiple_of(i*128,128),128)
        v=hrow[r,z,a,:].astype(f32)+(part[r,a,:]+r1[r,a,:])
        mid[r,a,:]=v
        v=normed(v,1)
        n2[d,:]=v.astype(low)
        lt[1,:,d]=v.T.astype(low)
        return 0
    lax.fori_loop(0,4,middle,0)
    give_p.wait_send()
    give_lt=pltpu.make_async_copy(lt,lt_o,ll.at[5]); give_lt.start()
    give_mid=pltpu.make_async_copy(mid,mid_o,ll.at[12]); give_mid.start()
    gs_o[...]=gs[...]
    advance(10)
    for t in sorted(across)[1:]: across4(t)
    hout=[]
    for j in range(ff_steps):
        if j:
            for t in range(4+3*j,7+3*j) if j==ff_steps-1 else [10+j]: advance(t)
            if j==ff_steps-1:
                for t in sorted(across): across5(t)
        def load(act):
            def piece(i): each(2+3*j+i,lambda wd: act(pltpu.make_async_copy(w.at[3*j+i,:,:,:,pl.ds(0,wd)],wf.at[i,:,:,:,pl.ds(0,wd)],ll.at[6+i])))
            for i in range(3): piece(i)
        if 2+3*j in narrow:
            @pl.when(c==1)
            def _(): wf[:,:,:,:,tail:512]=jnp.zeros((3,8,4,48,512-tail),low)
        load(lambda m: m.start())
        b=j%2
        if j>=2: hout[j-2].wait()
        load(lambda m: m.wait())
        def feed(i,_):
            d=pl.ds(pl.multiple_of(i*256,256),256)
            v=n2[d,:]
            wg=wf[0].reshape(1536,512); wu=wf[1].reshape(1536,512); wd=wf[2].reshape(1536,512)
            gate=dot(v,wg); up=dot(v,wu)
            gh=dot(cotv[i],wd).astype(low).astype(f32)
            u2=gate*gate
            th=jnp.tanh(gelu_c*(gate+0.044715*(gate*u2)))
            act=0.5*gate*(1.0+th)
            slope=0.5*(1.0+th)+0.5*gate*(1.0-th*th)*(gelu_c*(1.0+3*0.044715*u2))
            hm=(act*up).astype(low); dg=(gh*up*slope).astype(low); du=(gh*act).astype(low)
            hd[b,0,d,:]=hm; hd[b,1,d,:]=dg; hd[b,2,d,:]=du
            yp=dot_nt(hm,wd); gp=dot_nt(dg,wg)+dot_nt(du,wu)
            if j: yp=yp+yy[i]; gp=gp+part[i]
            yy[i]=yp; part[i]=gp
            return 0
        lax.fori_loop(0,2,feed,0)
        o=pltpu.make_async_copy(hd.at[b],hdg_o.at[:,:,pl.ds(512*j,512)],lo.at[8+b]); o.start(); hout.append(o)
    give_m=[pltpu.make_async_copy(part,gnf_o,ll.at[9]),pltpu.make_async_copy(yy,yy_o,ll.at[10])]
    for g in give_m: g.start()
    for o in outs+hout[-2:]: o.wait()
    give_lt.wait(); give_mid.wait()
    for g in give_m: g.wait()
    give_c.wait_send(); give_r.wait_send(); give_s.wait_send()
    for g in give_h: g.wait_send()
    for p in range(h_parts):
        for k in (1,2,3): share(p,k).wait_send()
        ha(p).wait_send(); hb(p).wait_send()
        @pl.when(inner)
        def _(): hc(p).wait_send()
    for t in range(n):
        s0(t).wait_send()
        each(t,lambda wd: [g.wait_send() for g in (s1a(t,wd),s1b(t,wd),s2(t,0,wd),s2(t,1,wd),s3(t,0,wd),s3(t,1,wd))])
        @pl.when(inner)
        def _(): each(t,lambda wd: s1c(t,wd).wait_send())

def forward_call(weights, gains, hid, cot, segr, segc, base, ff_steps, cid=0):
    n=2+3*ff_steps
    S=jax.ShapeDtypeStruct; V=pltpu.VMEM; D=pltpu.SemaphoreType.DMA
    fw=512*ff_steps
    hbm=pl.BlockSpec(memory_space=pltpu.HBM); vm=pl.BlockSpec(memory_space=pltpu.VMEM)
    outs=(S((8,4,48,768),low),S((8,4,48,896),low),S((3*ff_steps,8,4,48,512),low),S((3,1536,512),low),S((3,512,fw),low),S((512,384),low),S((2,1024,384),low),S((2,1024,384),low),
          S((512,384),low),S((2,256,128),f32),S((2,256,1536),f32),S((2,256,1536),f32),S((8,1536),f32),S((2,8,1024),f32),S((2,256,128),f32),S((2,256,1536),f32),S((2,256,1536),low))
    ospec=[hbm]*17; ospec[12]=vm
    scratch=[V((2,4,256,1536),low),V((2,256,1536),low),V((2,8,1024),f32),V((2,256,128),f32),V((8,4,48,1664),low),V((3,8,4,48,512),low),
             V((512,384),low),V((2,1024,384),low),V((2,1024,384),low),V((512,384),low),V((2,256,128),f32),V((256,1280),f32),
             V((2,256,1536),f32),V((2,256,1536),f32),V((512,1536),low),V((2,3,512,512),low),V((2,256,1536),f32),V((3,1536,512),low),V((8,1536),f32),
             V((2,256,1536),f32),V((2,48,1664+1536*ff_steps),low),
             D((n,)),D((n,)),D((n,)),D((n,3)),D((n,4)),D((n,2)),D((n,2)),D((n,2)),D((n,2)),D((h_parts,3)),D((h_parts,4)),D((10,)),D((10,)),D((h_parts,3)),D((h_parts,3)),D((13,)),D((10,))]
    return pl.pallas_call(functools.partial(forward_kernel,ff_steps),out_shape=outs,
        in_specs=[vm]*8+[hbm]*4+[vm],out_specs=tuple(ospec),scratch_shapes=scratch,
        compiler_params=pltpu.CompilerParams(collective_id=cid,has_side_effects=True,vmem_limit_bytes=62*2**20))(*weights,gains,hid,cot,segr,segc,base)

def dot_tn(a,b):
    return lax.dot_general(a,b,(((0,),(0,)),((),())),preferred_element_type=jnp.float32)

part_slots=2
sum_slots=3
lag=7
def backward_kernel(chunks, ff_steps, w1, w2, lt_h, hdg, q_h, kk_h, vv_h, mx_h, lse_h, gnf_h, yy_h, mid_h, cot_h, segr_h, segc_h, hid_h, base, gains,
                    og, ou, od, oo, oq, ok, ov, oe, gin_o, bo_o, xg, xy, *rest):
    n=len(chunks)
    ra1=rest[0:n]; rb1=rest[n:2*n]; ra2=rest[2*n:3*n]; rb2=rest[3*n:4*n]; rz=rest[4*n:5*n]
    (fin,p,lt,gat,rbuf,wa,qq,kk,vv,mx,gm,lse,sr,sc,bias,dbias,dq,acc,dkv,rka,rkb,rkc,dk,dv,part,r3,hid,dtab,ext,cb,
     ll,lr,lo,s1,v1,s2,v2,s3,v3,s4,v4,ks,kr,xs,xr,lb)=rest[5*n:]
    dp,z,c,x,y=peers_of()
    sib=(dp+1-2*c,z); dx=(dp+2-4*x,z); dy=(lax.rem(dp+4,8),z)
    zs=[lax.rem(z+k,4) for k in (1,2,3)]; dz=[(dp,zz) for zz in zs]
    zb=lax.rem(z,2); pe=z+1-2*zb; mo=2-z//2; zo=2-2*(z//2)
    inner=(z==1)|(z==2); outer=(z==0)|(z==3)
    def ka(pp,recv=False): return remote(dkv.at[pp,pe],rka.at[pp],ks.at[pp,0],kr.at[pp,0],(dp,pe))
    def kc(pp): return remote(dkv.at[pp,pl.ds(zo,2)],rkc.at[pp],ks.at[pp,1],kr.at[pp,1],(dp,pe))
    def kb(pp,k): return remote(dkv.at[pp,zo+k],rkb.at[pp],ks.at[pp,2+k],kr.at[pp,2],(dp,zo+k))
    def relay(pp):
        @pl.when(inner)
        def _():
            kc(pp).wait_recv()
            for k in range(2):
                for j in range(2):
                    for r in range(2):
                        dkv[pp,zo+k,j,r]=(dkv[pp,zo+k,j,r].astype(f32)+rkc[pp,k,j,r].astype(f32)).astype(low)
                kb(pp,k).start()
    loads=[pltpu.make_async_copy(a,b,ll.at[i]) for i,(a,b) in enumerate((
        (lt_h.at[pl.ds(1,2)],lt),(w2.at[:,:,:,pl.ds(384,384)],wa.at[:,:,:,pl.ds(0,384)]),(q_h,qq),(kk_h,kk),(vv_h,vv),(mx_h,mx),(lse_h,lse),(segr_h,sr),(segc_h,sc),(hid_h,hid)))]
    for l in loads: l.start()
    slots=rbuf.shape[0]
    def fetch(t):
        kind,i,j=chunks[t][3]
        return pltpu.make_async_copy(hdg.at[i,:,pl.ds(512*j,512)],rbuf.at[t%slots],lr.at[t])
    feeds=[t for t in range(n) if chunks[t][3][0]=="feed"]
    for t in feeds[:slots]: fetch(t).start()
    greet([sib,dx,dy]+dz)()
    load_n=pltpu.make_async_copy(lt_h.at[0],lt.at[1],ll.at[14])
    done=set()
    def once(*k):
        if k in done: return False
        done.add(k); return True
    def each(t,act):
        width,fw=chunks[t][4][2]; tail=chunks[t][4][3]-fw-chunks[t][4][1]
        if 0<tail<width:
            @pl.when(c==0)
            def _(): act(pl.ds(0,width))
            @pl.when(c==1)
            def _(): act(pl.ds(0,tail))
        else: act(pl.ds(0,width))
    def hop1(t,wd):
        b=t%part_slots
        return (remote(p.at[b,:,1-x,0,:,:,wd],ra1[t].at[:,:,:,wd],s1.at[t,0],v1.at[t,0],dx),
                remote(p.at[b,1-y,:,1,:,:,wd],rb1[t].at[:,:,:,wd],s1.at[t,1],v1.at[t,1],dy))
    def hop2(t,wd):
        return (remote(ra1[t].at[1-y,:,:,wd],ra2[t].at[:,:,wd],s2.at[t,0],v2.at[t,0],dy),
                remote(rb1[t].at[1-x,:,:,wd],rb2[t].at[:,:,wd],s2.at[t,1],v2.at[t,1],dx))
    def hop3(t,wd):
        return [remote(r[t].at[zs[k],:,wd],rz[t].at[k,i,:,wd],s3.at[t,k,i],v3.at[t,k,i],dz[k]) for k in range(3) for i,r in enumerate((ra2,rb2))]
    def go(t,f): each(t,lambda wd: [d.start() for d in f(t,wd)])
    def came(t,f): each(t,lambda wd: [d.wait_recv() for d in f(t,wd)])
    def went(t,f): each(t,lambda wd: [d.wait_send() for d in f(t,wd)])
    def stage1(t):
        left,off,wd,src=chunks[t][:4]; b=t%part_slots
        if t>=part_slots:
            went(t-part_slots,hop1)
        if src[0]=="feed":
            fetch(t).wait()
            right=lambda: rbuf[t%slots]
        else:
            right=(lambda: mx[...],lambda: dq[...],lambda: dk[...],lambda: dv[...],None)[src[1]]
        if src==("ref",1,0): load_n.wait()
        if right is None:
            p[b,:,:,:,:,:,0:wd]=ext[...].T.astype(low).reshape(2,2,2,4,48,wd)
        else:
            def body(i,_):
                rs=pl.ds(pl.multiple_of(i*192,192),192)
                lhs=gat[rs,:] if left==3 else lt[left,rs,:]
                p[b,i//4,lax.rem(i//2,2),lax.rem(i,2),:,:,0:wd]=dot(lhs,right()).astype(low).reshape(4,48,wd)
                return 0
            lax.fori_loop(0,8,body,0)
        if t==feeds[-1]:
            load_n.start()
        if src[0]=="feed" and t+slots<n and chunks[t+slots][3][0]=="feed": fetch(t+slots).start()
        go(t,hop1)
    def stage2(t):
        wd=chunks[t][2]; b=t%part_slots
        came(t,hop1)
        def body(i,_):
            h=i//4; zz=lax.rem(i,4)
            ra1[t][h,zz]=ra1[t][h,zz]+p[b,h,x,0,zz,:,0:wd]
            rb1[t][h,zz]=rb1[t][h,zz]+p[b,y,h,1,zz,:,0:wd]
            return 0
        lax.fori_loop(0,8,body,0)
        go(t,hop2)
    def stage3(t):
        came(t,hop2)
        def body(zz,_):
            ra2[t][zz]=ra2[t][zz]+ra1[t][y,zz]
            rb2[t][zz]=rb2[t][zz]+rb1[t][x,zz]
            return 0
        lax.fori_loop(0,4,body,0)
        go(t,hop3)
    def place(t,pair,acts,half):
        o,offset,width,total=chunks[t][4]
        o=(og,ou,od,oo,oq,ok,ov,oe)[o]
        last=total-(width[1]+offset)
        def act(size):
            cols=pl.ds(pl.multiple_of(half*width[1]+offset,128),size)
            for m,how in zip(pair(None,size,cols,o),acts):
                if how: getattr(m,how)()
        if last>=width[0]: act(width[0])
        else:
            @pl.when(half==0)
            def _(): act(width[0])
            if last>0:
                @pl.when(half==1)
                def _(): act(last)
    def drain(t):
        place(t,lambda _,width,cols,o: (
            remote(fin.at[0,0,:,pl.ds(0,width)],o.at[:,cols],s4.at[t],v4.at[t],sib),
            pltpu.make_async_copy(fin.at[0,0,:,pl.ds(0,width)],o.at[:,cols],lo.at[t])),("wait_send","wait"),c)
    def arrive(t):
        place(t,lambda _,width,cols,o: (remote(fin.at[0,0,:,pl.ds(0,width)],o.at[:,cols],s4.at[t],v4.at[t],sib),),("wait_recv",),1-c)
    def stage4(t):
        wd=chunks[t][2]
        came(t,hop3)
        f0=ra2[t][z].astype(f32); f1=rb2[t][z].astype(f32)
        for k in range(3):
            f0=f0+rz[t][k,0].astype(f32); f1=f1+rz[t][k,1].astype(f32)
        b=t%sum_slots
        if t>=sum_slots:
            drain(t-sum_slots)
        fin[b,0,:,0:wd]=f0; fin[b,1,:,0:wd]=f1
        place(t,lambda _,width,cols,o: (
            remote(fin.at[b,1-c,:,pl.ds(0,width)],o.at[:,cols],s4.at[t],v4.at[t],sib),
            pltpu.make_async_copy(fin.at[b,c,:,pl.ds(0,width)],o.at[:,cols],lo.at[t])),("start","start"),c)
    def step(s):
        for f,t in ((stage2,s),(stage1,s+2),(stage3,s-1),(stage4,s-lag)):
            if 0<=t<n and once(f.__name__,t): f(t)
    give_g=remote(gnf_h,xg,xs.at[1],xr.at[1],sib); give_g.start()
    give_y=remote(yy_h.at[1-c],xy,xs.at[2],xr.at[2],sib); give_y.start()
    loads[0].wait()
    stage1(0); stage1(1); once("stage1",0); once("stage1",1)
    for l in loads[1:]: l.wait()
    def wcol(a,b): return wa[:,:,:,a:b].reshape(1536,b-a)
    give_g.wait_recv()
    total=jnp.zeros((1,1536),f32)
    for i in range(4):
        r=i//2; a=pl.ds(128*(i%2),128); d=pl.ds(128*i,128)
        first=part.at[0,pl.ds(0,128)]; second=part.at[0,pl.ds(128,128)]; third=part.at[1,pl.ds(0,128)]
        moves=[pltpu.make_async_copy(f,g,lb.at[k]) for k,(f,g) in enumerate(((mid_h.at[r,a],first),(gnf_h.at[r,a],second),(xg.at[r,a],third),(cot_h.at[r,a],cb)))]
        for m in moves: m.start()
        for m in moves: m.wait()
        v=part[0,0:128,:]; gn=part[0,128:256,:]+part[1,0:128,:]
        s=lax.rsqrt(jnp.mean(v*v,axis=-1,keepdims=True)+epsilon)
        wg=gn*gains[1:2,:]
        g=cb[...].astype(f32)+(s*wg-v*(s*s*s)*jnp.mean(wg*v,axis=-1,keepdims=True))
        total=total+jnp.where(c==r,1.0,0.0)*jnp.sum(gn*v*s,axis=0,keepdims=True)
        part[1,128:256,:]=g
        @pl.when(c==r)
        def _():
            back=pltpu.make_async_copy(part.at[1,pl.ds(128,128)],gin_o.at[a],lb.at[4]); back.start(); back.wait()
        gat[:,d]=g.T.astype(low)
        gm[d,:]=dot(g.astype(low),wcol(0,384)).astype(low)
    ext[...]=jnp.zeros((128,1536),f32)
    def spread(v,row):
        upper=v.astype(low)
        ext[row:row+8,:]=upper.astype(f32)
        ext[row+8:row+16,:]=v-upper.astype(f32)
    spread(jnp.broadcast_to(total,(8,1536)),32)
    load_w=[pltpu.make_async_copy(w1,wa.at[:,:,:,pl.ds(0,768)],ll.at[13]),pltpu.make_async_copy(w2.at[:,:,:,pl.ds(0,384)],wa.at[:,:,:,pl.ds(768,384)],ll.at[15])]
    for l in load_w: l.start()
    step(0)
    dbias[...]=jnp.zeros((256,1280),f32)
    dtab[...]=jnp.zeros((8,1280),f32)
    at=1
    for h in range(6):
        odd=h%2; pair=pl.ds(128*(h//2),128); pp=h//2
        bias[...]=pltpu.roll(jnp.broadcast_to(base[h:h+1,:],(256,1280)),1024,1,stride=1,stride_axis=0)
        if not odd: acc[...]=jnp.zeros((2,2,1024,128),f32)
        def attend(i,_):
            r=i//2; d=pl.ds(pl.multiple_of(i*128,128),128)
            a=pl.ds(pl.multiple_of(lax.rem(i,2)*128,128),128)
            mine=(lanes((128,128))>=64) if odd else (lanes((128,128))<64)
            qh=jnp.where(mine,qq[d,pair].astype(f32),0.0).astype(low)
            gh=jnp.where(mine,gm[d,pair].astype(f32),0.0).astype(low)
            s=dot_nt(qh,kk[r,:,pair])+bias[a,0:1024]
            s=jnp.where(sc[r,a,0:1]==sr[r,0:1,:],s,-1000000000.0)
            pr=jnp.exp(s-lse[r,a,h:h+1])
            gp=dot_nt(gh,vv[r,:,pair])
            gl=(pr*(gp-jnp.sum(pr*gp,axis=-1,keepdims=True))).astype(low)
            wide=gl.astype(f32)
            dbias[a,0:1024]=wide+jnp.where(r==0,0.0,1.0)*dbias[a,0:1024]
            g=jnp.where(mine,dot(gl,kk[r,:,pair]),0.0)
            if odd: g=g+dq[d,pair].astype(f32)
            dq[d,pair]=g.astype(low)
            acc[0,r]=acc[0,r]+dot_tn(gl,qh)
            acc[1,r]=acc[1,r]+dot_tn(pr.astype(low),gh)
            return 0
        lax.fori_loop(0,4,attend,0)
        m=128
        v=dbias[0:128,:]+pltpu.roll(dbias[128:256,:],1280-128,1)
        while m>1:
            m//=2
            v=v[0:m]+pltpu.roll(v[m:2*m],1280-m,1)
        dtab[h:h+1,:]=pltpu.roll(v,256,1)
        if odd:
            for j in range(2):
                for r in range(2):
                    for zz in range(4):
                        dkv[pp,zz,j,r]=acc[j,r,256*zz:256*zz+256,:].astype(low)
            ka(pp).start()
            @pl.when(outer)
            def _(): kc(pp).start()
            step(at); at+=1
            if pp: relay(pp-1)
    tab=dtab[...]
    high=tab.astype(low); rest1=tab-high.astype(f32); mid1=rest1.astype(low); last=(rest1-mid1.astype(f32)).astype(low)
    shift=lax.broadcasted_iota(jnp.int32,(1280,128),0)-256-256*z
    spots=jnp.where(bucket_table(shift)==lanes((1280,128)),1.0,0.0).astype(low)
    tile=jnp.where(lax.rem(lanes((128,1536)),48)==lax.broadcasted_iota(jnp.int32,(128,1536),0),1.0,0.0).astype(low)
    found=dot(high,spots)+dot(mid1,spots)+dot(last,spots)
    upper=found.astype(low)
    ext[0:8,:]=dot(upper,tile)
    ext[8:16,:]=dot((found-upper.astype(f32)).astype(low),tile)
    give_y.wait_recv()
    for i in range(2):
        a=pl.ds(128*i,128)
        first=part.at[0,pl.ds(0,128)]; second=part.at[0,pl.ds(128,128)]; third=part.at[1,pl.ds(0,128)]
        moves=[pltpu.make_async_copy(f,g,lb.at[k]) for k,(f,g) in enumerate(((mid_h.at[c,a],first),(yy_h.at[c,a],second),(xy.at[a],third)))]
        for m in moves: m.start()
        for m in moves: m.wait()
        part[1,128:256,:]=part[0,0:128,:]+(part[0,128:256,:]+part[1,0:128,:])
        back=pltpu.make_async_copy(part.at[1,pl.ds(128,128)],bo_o.at[a],lb.at[4]); back.start(); back.wait()
    step(at); at+=1
    relay(2)
    while at<9:
        step(at); at+=1
    for pp in range(3):
        ka(pp).wait_recv(); kb(pp,0).wait_recv()
        for j,o in enumerate((dk,dv)):
            for r in range(2):
                v=dkv[pp,z,j,r].astype(f32)+rka[pp,j,r].astype(f32)+rkb[pp,j,r].astype(f32)
                o[256*r:256*r+256,128*pp:128*pp+128]=v.astype(low)
    step(at); at+=1
    for l in load_w: l.wait()
    def input_grad(i,_):
        d=pl.ds(pl.multiple_of(i*128,128),128); a=pl.ds(pl.multiple_of(lax.rem(i,2)*128,128),128)
        part[i//2,a,:]=dot_nt(dq[d,:],wcol(0,384))+dot_nt(dk[d,:],wcol(384,768))+dot_nt(dv[d,:],wcol(768,1152))
        return 0
    lax.fori_loop(0,4,input_grad,0)
    give=remote(part.at[1-c],r3,xs.at[0],xr.at[0],sib); give.start()
    step(at); at+=1
    give.wait_send()
    load_i=pltpu.make_async_copy(gin_o,part.at[1-c],lb.at[0]); load_i.start()
    give.wait_recv(); load_i.wait()
    def last_grad(i,total):
        a=pl.ds(pl.multiple_of(i*128,128),128)
        v=hid[a,:].astype(f32); gn=part[c,a,:]+r3[a,:]
        s=lax.rsqrt(jnp.mean(v*v,axis=-1,keepdims=True)+epsilon)
        wg=gn*gains[0:1,:]
        part[1-c,a,:]=part[1-c,a,:]+(s*wg-v*(s*s*s)*jnp.mean(wg*v,axis=-1,keepdims=True))
        return total+jnp.sum(gn*v*s,axis=0,keepdims=True)
    total=lax.fori_loop(0,2,last_grad,jnp.zeros((1,1536),f32))
    spread(jnp.broadcast_to(total,(8,1536)),16)
    give_i=pltpu.make_async_copy(part.at[1-c],gin_o,ll.at[12]); give_i.start()
    while at<n+lag:
        step(at); at+=1
    for t in range(n):
        arrive(t)
        if t>=n-sum_slots: drain(t)
        if t>=n-part_slots:
            went(t,hop1)
        went(t,hop2); went(t,hop3)
    for pp in range(3):
        ka(pp).wait_send()
        @pl.when(outer)
        def _(): kc(pp).wait_send()
        @pl.when(inner)
        def _(): kb(pp,0).wait_send(); kb(pp,1).wait_send()
    give_i.wait(); give_g.wait_send(); give_y.wait_send()

def backward_chunks(ff_steps,ff):
    fw=512*ff_steps
    chunks=[]
    for j in range(ff_steps):
        for left,i,o in ((0,1,0),(0,2,1),(1,0,2)):
            chunks.append((left,0,512,("feed",i,j),(o,512*j,(512,fw),ff)))
    for k in range(4): chunks.append((3 if k==0 else 1,0,384,("ref",k,0),(3+k,0,(384,384),768)))
    chunks.append((1,0,128,("ref",4,0),(7,0,(128,128),256)))
    return chunks

def backward_call(w1,w2,lt,hdg,q,kk,vv,mx,lse,gnf,yy,mid,cot,segr,segc,hid,base,gains,ff_steps,ff,cid=1):
    chunks=backward_chunks(ff_steps,ff); n=len(chunks)
    S=jax.ShapeDtypeStruct; V=pltpu.VMEM; D=pltpu.SemaphoreType.DMA
    hbm=pl.BlockSpec(memory_space=pltpu.HBM); vm=pl.BlockSpec(memory_space=pltpu.VMEM)
    ws=[k[2] for k in chunks]
    scratch=[V((2,4,48,k),low) for k in ws]*1+[V((2,4,48,k),low) for k in ws]+[V((4,48,k),low) for k in ws]+[V((4,48,k),low) for k in ws]+[V((3,2,48,k),low) for k in ws]
    scratch+=[V((sum_slots,2,48,512),f32),V((part_slots,2,2,2,4,48,512),low),V((2,1536,512),low),V((1536,512),low),V((2,512,512),low),V((8,4,48,1152),low),
      V((512,384),low),V((2,1024,384),low),V((2,1024,384),low),V((512,384),low),V((512,384),low),V((2,256,128),f32),V((2,8,1024),f32),V((2,256,128),f32),
      V((256,1280),f32),V((256,1280),f32),V((512,384),low),V((2,2,1024,128),f32),V((3,4,2,2,256,128),low),V((3,2,2,256,128),low),V((3,2,2,256,128),low),V((3,2,2,2,256,128),low),V((512,384),low),V((512,384),low),
      V((2,256,1536),f32),V((256,1536),f32),V((256,1536),low),V((8,1280),f32),V((128,1536),f32),V((128,1536),low)]
    scratch+=[D((16,)),D((n,)),D((n,)),D((n,2)),D((n,2)),D((n,2)),D((n,2)),D((n,3,2)),D((n,3,2)),D((n,)),D((n,)),D((3,4)),D((3,3)),D((3,)),D((3,)),D((5,))]
    return pl.pallas_call(functools.partial(backward_kernel,chunks,ff_steps),out_shape=(S((48,ff),f32),)*3+(S((48,768),f32),)*4+(S((48,256),f32),S((256,1536),f32),S((256,1536),f32),S((2,256,1536),f32),S((256,1536),f32)),
        in_specs=[hbm]*16+[vm]*2,out_specs=(hbm,)*12,scratch_shapes=scratch,
        compiler_params=pltpu.CompilerParams(collective_id=cid,has_side_effects=True,vmem_limit_bytes=62*2**20))(w1,w2,lt,hdg,q,kk,vv,mx,lse,gnf,yy,mid,cot,segr,segc,hid,base,gains)

def settle_kernel(count,*refs):
    given,kept,held,sem_in,sem_out=refs[:count],refs[count:2*count],refs[2*count:3*count],refs[3*count],refs[3*count+1]
    ins=[pltpu.make_async_copy(a,b,sem_in.at[i]) for i,(a,b) in enumerate(zip(given,held))]
    outs=[pltpu.make_async_copy(a,b,sem_out.at[i]) for i,(a,b) in enumerate(zip(held,kept))]
    for m in ins: m.start()
    for m,o in zip(ins,outs):
        m.wait(); o.start()
    for o in outs: o.wait()

def settle(arrays):
    hbm=pl.BlockSpec(memory_space=pltpu.HBM); count=len(arrays)
    return pl.pallas_call(functools.partial(settle_kernel,count),out_shape=tuple(jax.ShapeDtypeStruct(a.shape,a.dtype) for a in arrays),
        in_specs=[hbm]*count,out_specs=(hbm,)*count,
        scratch_shapes=[pltpu.VMEM(a.shape,a.dtype) for a in arrays]+[pltpu.SemaphoreType.DMA((count,))]*2,
        compiler_params=pltpu.CompilerParams(vmem_limit_bytes=62*2**20))(*arrays)

def cut(v,h,w):
    n=v.shape[1]
    a=min(h*w,n); b=min((h+1)*w,n)
    p=v[:,a:b]
    return jnp.pad(p,((0,0),(0,w-(b-a)))) if b-a<w else p
def pack(wq,wk,wv,wo,ga,gf,wg,wu,wd,steps):
    gains=jnp.pad(jnp.stack([ga,gf],axis=1),((0,0),(0,126)))
    fw=512*steps
    rows=[]
    for h in (0,1):
        m=[cut(v,h,384) for v in (wq,wk,wv,wo.T)]+[gains]
        f=[cut(v,h,fw) for v in (wg,wu,wd.T)]
        for j in range(steps):
            m+=[v[:,512*j:512*j+512] for v in f]
        rows.append(jnp.concatenate(m,axis=1))
    return jnp.stack(rows)
def seg_ids(seg):
    n=seg.shape[1]
    place=jnp.arange(n,dtype=jnp.int32)
    ids=jnp.where(seg[0]>0,seg[0],-1-place).astype(jnp.float32)
    r=jnp.broadcast_to(ids[None],(8,n))
    mine=lax.dynamic_slice_in_dim(ids,lax.axis_index("seq")*256,256,0)
    return r, jnp.broadcast_to(mine[:,None],(256,128))
def base_of(table):
    off=jnp.arange(1280,dtype=jnp.int32)-256-256*lax.axis_index("seq")
    oh=(bucket_table(off)[:,None]==jnp.arange(32,dtype=jnp.int32)).astype(jnp.float32)
    c=lax.rem(lax.axis_index("dp"),2)
    tab=table.astype(jnp.float32)
    mine=jnp.where(c==0,tab[:,:6],tab[:,6:])
    b=jnp.einsum("ub,bh->hu",oh,mine,precision=lax.Precision.HIGHEST)
    return jnp.pad(b,((0,2),(0,0))), oh

def kernel_local(hid,seg,ga,wq,wk,wv,wo,tab,gf,wg,wu,wd,cot):
    ff=wg.shape[1]; steps=-(-ff//1024)
    gain_cols=jnp.stack([ga,gf],axis=1)
    r,s=seg_ids(seg); b=base_of(tab)[0]
    w1,w2,w,lt,hdg,q,kk,vv,mx,lse,gnf,yy,gains,segr,segc,mid,cot2=forward_call((wq,wk,wv,wo.T,wg,wu,wd.T),gain_cols,hid[0],cot[0],r,s,b,steps)
    og,ou,od,oo,oq,ok,ov,oe,gin,bo,_,_=backward_call(w1,w2,lt,hdg,q,kk,vv,mx,lse,gnf,yy,mid,cot2,segr,segc,hid[0],b,gains,steps,ff)
    og,ou,od,oo,oq,ok,ov,gin,bo=settle((og,ou,od,oo,oq,ok,ov,gin,bo))
    e=oe.reshape(48,2,128)
    t=e[:32,:,0:8]+e[:32,:,8:16]
    table=t[:,:,:6].reshape(32,12)
    g=e[:,0]+e[:,1]
    gg=lambda a: g[:,a]+g[:,a+8]
    return (bo[None],gin[None],gg(16),oq,ok,ov,oo.T,table,gg(32),og,ou,od.T)


def solution(mesh):
    in_specs = (
        P("dp", "seq", None),
        P("dp", None),
        P(("dp", "seq")),
        P(("dp", "seq"), None),
        P(("dp", "seq"), None),
        P(("dp", "seq"), None),
        P(None, ("dp", "seq")),
        P(),
        P(("dp", "seq")),
        P(("dp", "seq"), None),
        P(("dp", "seq"), None),
        P(None, ("dp", "seq")),
        P("dp", "seq", None),
    )
    out_specs = (
        P("dp", "seq", None),
        P("dp", "seq", None),
        P(("dp", "seq")),
        P(("dp", "seq"), None),
        P(("dp", "seq"), None),
        P(("dp", "seq"), None),
        P(None, ("dp", "seq")),
        P(),
        P(("dp", "seq")),
        P(("dp", "seq"), None),
        P(("dp", "seq"), None),
        P(None, ("dp", "seq")),
    )
    small = mesh.shape["dp"] == 8 and mesh.shape["seq"] == 4
    local = kernel_local if small else plain_local
    return jax.shard_map(local, mesh=mesh, in_specs=in_specs, out_specs=out_specs, check_vma=False)
```

```python
import functools

import jax
import jax.numpy as jnp
from jax import lax
from jax.experimental import pallas as pl
from jax.experimental.pallas import tpu as pltpu
from jax.sharding import PartitionSpec as P

epsilon = 1e-06
far_bounds = (12, 16, 23, 32, 46, 64, 91)
highest = lax.Precision.HIGHEST
mesh_ids = pl.DeviceIdType.MESH


def bucket_table(offset):
    magnitude = jnp.abs(offset)
    distant = 8 + sum(((magnitude >= bound).astype(jnp.int32) for bound in far_bounds))
    signed_part = jnp.where(offset > 0, 16, 0).astype(jnp.int32)
    return signed_part + jnp.where(magnitude < 8, magnitude, distant)


def norm_scale(hidden):
    return lax.rsqrt(jnp.mean(hidden * hidden, axis=-1, keepdims=True) + epsilon)


def norm_backward(grad_normed, hidden, scale, gain):
    weighted = grad_normed * gain
    grad_gain = jnp.sum(grad_normed * hidden * scale, axis=0)
    grad_hidden = scale * weighted - hidden * (scale * scale * scale) * jnp.mean(
        weighted * hidden, axis=-1, keepdims=True
    )
    return (grad_hidden, grad_gain)


def scores_of(query_heads, key_heads, bias, allowed):
    raw_scores = jnp.einsum(
        "rqhd,rkhd->rhqk", query_heads, key_heads, preferred_element_type=jnp.float32
    )
    return jnp.where(allowed, raw_scores + bias[None], -1000000000.0)


def gather_rows(shard):
    return lax.all_gather(shard, ("dp", "seq"), axis=0, tiled=True)


def scatter_sum(parts):
    data_count = lax.axis_size("dp")
    piece_count = lax.axis_size("seq")
    shard_width = parts.shape[0] // (data_count * piece_count)
    split = parts.reshape(data_count, piece_count, shard_width, parts.shape[1])
    half = lax.psum_scatter(split, "dp", scatter_dimension=0, tiled=True)
    return lax.psum_scatter(half, "seq", scatter_dimension=1, tiled=True)[0, 0]


def plain_sums(pairs, extra):
    found = []
    for left, rights in pairs:
        for right in rights:
            part = jnp.einsum("td,tf->df", left, right, preferred_element_type=jnp.float32)
            found.append(scatter_sum(part.astype(jnp.bfloat16)).astype(jnp.float32))
    return found, scatter_sum(extra.astype(jnp.bfloat16)).astype(jnp.float32)


def plain_local(
    hidden_in,
    segment_ids,
    gain_attn,
    w_query,
    w_key,
    w_value,
    w_out,
    rel_table,
    gain_ff,
    w_gate,
    w_up,
    w_down,
    cotangent,
):
    row_count, local_len, model_width = hidden_in.shape
    row_length = segment_ids.shape[1]
    bucket_count, head_count = rel_table.shape
    token_count = row_count * local_len
    data_count = lax.axis_size("dp")
    piece_count = lax.axis_size("seq")
    shard_width = model_width // (data_count * piece_count)
    first_place = lax.axis_index("seq") * local_len
    query_place = first_place + jnp.arange(local_len, dtype=jnp.int32)
    key_place = jnp.arange(row_length, dtype=jnp.int32)
    buckets = bucket_table(key_place[None, :] - query_place[:, None])
    onehot = (buckets[:, :, None] == jnp.arange(bucket_count, dtype=jnp.int32)).astype(jnp.float32)
    bias = jnp.einsum("qkb,bh->hqk", onehot, rel_table.astype(jnp.float32), precision=highest)
    query_segs = lax.dynamic_slice_in_dim(segment_ids, first_place, local_len, 1)
    same_doc = query_segs[:, :, None] == segment_ids[:, None, :]
    visible = (segment_ids[:, None, :] > 0) | (query_place[:, None] == key_place[None, :])[None]
    allowed = (same_doc & visible)[:, None]
    inner = w_query.shape[1]
    ff_width = w_gate.shape[1]
    gains = jnp.pad(jnp.stack([gain_attn, gain_ff], axis=1), ((0, 0), (0, 126)))
    attn_full = gather_rows(jnp.concatenate([w_query, w_key, w_value, w_out.T, gains], axis=1))
    feed_full = gather_rows(jnp.concatenate([w_gate, w_up, w_down.T], axis=1))
    query_full = attn_full[:, :inner]
    key_full = attn_full[:, inner : 2 * inner]
    value_full = attn_full[:, 2 * inner : 3 * inner]
    out_full = attn_full[:, 3 * inner : 4 * inner].T
    gain_one = attn_full[:, 4 * inner]
    gain_two = attn_full[:, 4 * inner + 1]
    gate_full = feed_full[:, :ff_width]
    up_full = feed_full[:, ff_width : 2 * ff_width]
    down_full = feed_full[:, 2 * ff_width :].T
    gain_first = gain_one.astype(jnp.float32)
    residual_in = hidden_in.astype(jnp.float32).reshape(token_count, model_width)
    scale_first = norm_scale(residual_in)
    normed_first = (residual_in * scale_first * gain_first).astype(jnp.bfloat16)
    queries = jnp.dot(normed_first, query_full, preferred_element_type=jnp.float32).astype(
        jnp.bfloat16
    )
    keys_local = jnp.dot(normed_first, key_full, preferred_element_type=jnp.float32).astype(
        jnp.bfloat16
    )
    values_local = jnp.dot(normed_first, value_full, preferred_element_type=jnp.float32).astype(
        jnp.bfloat16
    )
    head_size = inner // head_count
    keys_row, values_row = (
        lax.all_gather(keys_local.reshape(row_count, local_len, inner), "seq", axis=1, tiled=True),
        lax.all_gather(
            values_local.reshape(row_count, local_len, inner), "seq", axis=1, tiled=True
        ),
    )
    query_heads = queries.reshape(row_count, local_len, head_count, head_size)
    key_heads = keys_row.reshape(row_count, row_length, head_count, head_size)
    value_heads = values_row.reshape(row_count, row_length, head_count, head_size)
    logits = scores_of(query_heads, key_heads, bias, allowed)
    row_max = jnp.max(logits, axis=-1, keepdims=True)
    exp_scores = jnp.exp(logits - row_max)
    denominator = jnp.sum(exp_scores, axis=-1, keepdims=True)
    probs_low = (exp_scores / denominator).astype(jnp.bfloat16)
    log_total = row_max + jnp.log(denominator)
    mixed = (
        jnp.einsum("rhqk,rkhd->rqhd", probs_low, value_heads, preferred_element_type=jnp.float32)
        .astype(jnp.bfloat16)
        .reshape(token_count, inner)
    )
    middle = residual_in + jnp.dot(mixed, out_full, preferred_element_type=jnp.float32)
    gain_second = gain_two.astype(jnp.float32)
    scale_second = norm_scale(middle)
    normed_second = (middle * scale_second * gain_second).astype(jnp.bfloat16)
    gate_pre = jnp.dot(normed_second, gate_full, preferred_element_type=jnp.float32)
    up_pre = jnp.dot(normed_second, up_full, preferred_element_type=jnp.float32)
    activated = jax.nn.gelu(gate_pre, approximate=True)
    hidden_mid = (activated * up_pre).astype(jnp.bfloat16)
    block_out = middle + jnp.dot(hidden_mid, down_full, preferred_element_type=jnp.float32)
    gain_second = gain_two.astype(jnp.float32)
    grad_out = cotangent.reshape(token_count, model_width)
    grad_hidden = (
        jnp.einsum("td,fd->tf", grad_out, down_full, preferred_element_type=jnp.float32)
        .astype(jnp.bfloat16)
        .astype(jnp.float32)
    )
    gelu_value, gelu_pull = jax.vjp(lambda value: jax.nn.gelu(value, approximate=True), gate_pre)
    grad_gate = gelu_pull(grad_hidden * up_pre)[0].astype(jnp.bfloat16)
    grad_up = (grad_hidden * gelu_value).astype(jnp.bfloat16)
    grad_normed_second = jnp.einsum(
        "tf,df->td", grad_gate, gate_full, preferred_element_type=jnp.float32
    ) + jnp.einsum("tf,df->td", grad_up, up_full, preferred_element_type=jnp.float32)
    grad_middle_norm, grad_gain_two = norm_backward(
        grad_normed_second, middle, scale_second, gain_second
    )
    grad_middle = grad_out.astype(jnp.float32) + grad_middle_norm
    grad_attended = grad_middle.astype(jnp.bfloat16)
    grad_mixed = jnp.einsum(
        "td,id->ti", grad_attended, out_full, preferred_element_type=jnp.float32
    ).astype(jnp.bfloat16)
    grad_heads = grad_mixed.reshape(row_count, local_len, head_count, head_size)
    logits_again = scores_of(query_heads, key_heads, bias, allowed)
    probs_again = jnp.exp(logits_again - log_total)
    probs_again_low = probs_again.astype(jnp.bfloat16)
    grad_probs = jnp.einsum(
        "rqhd,rkhd->rhqk", grad_heads, value_heads, preferred_element_type=jnp.float32
    )
    row_dot = jnp.sum(probs_again * grad_probs, axis=-1, keepdims=True)
    grad_logits = (probs_again * (grad_probs - row_dot)).astype(jnp.bfloat16)
    grad_bias = jnp.sum(grad_logits.astype(jnp.float32), axis=0)
    grad_table = jnp.einsum("qkb,hqk->bh", onehot, grad_bias, precision=highest)
    grad_queries = (
        jnp.einsum("rhqk,rkhd->rqhd", grad_logits, key_heads, preferred_element_type=jnp.float32)
        .astype(jnp.bfloat16)
        .reshape(token_count, inner)
    )
    grad_keys_row = jnp.einsum(
        "rhqk,rqhd->rkhd", grad_logits, query_heads, preferred_element_type=jnp.float32
    )
    grad_values_row = jnp.einsum(
        "rhqk,rqhd->rkhd", probs_again_low, grad_heads, preferred_element_type=jnp.float32
    )
    grad_keys_part, grad_values_part = (
        lax.psum_scatter(
            grad_keys_row.astype(jnp.bfloat16), "seq", scatter_dimension=1, tiled=True
        ).astype(jnp.float32),
        lax.psum_scatter(
            grad_values_row.astype(jnp.bfloat16), "seq", scatter_dimension=1, tiled=True
        ).astype(jnp.float32),
    )
    grad_keys = grad_keys_part.astype(jnp.bfloat16).reshape(token_count, inner)
    grad_values = grad_values_part.astype(jnp.bfloat16).reshape(token_count, inner)
    grad_normed_first = jnp.einsum(
        "ti,di->td", grad_queries, query_full, preferred_element_type=jnp.float32
    )
    grad_normed_first = grad_normed_first + jnp.einsum(
        "ti,di->td", grad_keys, key_full, preferred_element_type=jnp.float32
    )
    grad_normed_first = grad_normed_first + jnp.einsum(
        "ti,di->td", grad_values, value_full, preferred_element_type=jnp.float32
    )
    grad_first, grad_gain_one = norm_backward(
        grad_normed_first, residual_in, scale_first, gain_first
    )
    grad_input = grad_middle + grad_first
    device_count = data_count * piece_count
    table_size = bucket_count * head_count
    table_rows = -(-table_size // shard_width)
    table_block = jnp.pad(grad_table.reshape(-1), (0, table_rows * shard_width - table_size))
    table_block = jnp.broadcast_to(
        table_block.reshape(1, table_rows, shard_width), (device_count, table_rows, shard_width)
    )
    gain_block = jnp.stack([grad_gain_one, grad_gain_two], axis=0)
    gain_block = gain_block.reshape(2, device_count, shard_width).transpose(1, 0, 2)
    extra = jnp.concatenate([table_block, gain_block], axis=1).transpose(0, 2, 1)
    extra = extra.reshape(model_width, table_rows + 2)
    extra = jnp.pad(extra, ((0, 0), (0, -(table_rows + 2) % 128)))
    pairs = (
        (normed_second, (grad_gate, grad_up)),
        (grad_out, (hidden_mid,)),
        (grad_attended, (mixed,)),
        (normed_first, (grad_queries, grad_keys, grad_values)),
    )
    (gate_sum, up_sum, down_sum, out_sum, query_sum, key_sum, value_sum), extra_sum = plain_sums(
        pairs, extra
    )
    table_total = extra_sum[:, :table_rows].T.reshape(-1)[:table_size]
    table_total = table_total.reshape(bucket_count, head_count)
    grad_gain_one_shard = extra_sum[:, table_rows]
    grad_gain_two_shard = extra_sum[:, table_rows + 1]
    return (
        block_out.reshape(row_count, local_len, model_width),
        grad_input.reshape(row_count, local_len, model_width),
        grad_gain_one_shard,
        query_sum,
        key_sum,
        value_sum,
        out_sum.T,
        table_total,
        grad_gain_two_shard,
        gate_sum,
        up_sum,
        down_sum.T,
    )


gelu_c=0.7978845608028654

def peers_of():
    dp=lax.axis_index("dp"); z=lax.axis_index("seq")
    c=lax.rem(dp,2); x=lax.rem(dp//2,2); y=dp//4
    return dp,z,c,x,y

def remote(src,dst,ss,rs,dev):
    return pltpu.make_async_remote_copy(src_ref=src,dst_ref=dst,send_sem=ss,recv_sem=rs,device_id=dev,device_id_type=mesh_ids)

def dot(a,b):
    return jnp.dot(a,b,preferred_element_type=jnp.float32)

def dot_nt(a,b):
    return lax.dot_general(a,b,(((1,),(1,)),((),())),preferred_element_type=jnp.float32)

def lanes(shape):
    return lax.broadcasted_iota(jnp.int32,shape,len(shape)-1)

def greet(devices):
    bar=pltpu.get_barrier_semaphore()
    for d in devices: pl.semaphore_signal(bar,inc=1,device_id=d,device_id_type=mesh_ids)
    return lambda: pl.semaphore_wait(bar,len(devices))

low=jnp.bfloat16
f32=jnp.float32

h_parts=4
across_first=2
def forward_kernel(ff_steps, w_q, w_k, w_v, w_o, w_g, w_u, w_d, gains, hid, cot, segr, segc, base,
                   w1, w2, w, lt_o, hdg_o, q_o, kk_o, vv_o, mx_o, lse_o, gnf_o, yy_o, gs_o, segr_o, segc_o, mid_o, cot_o,
                   hrow, cotv, sr, sc, wa, wf, qq, kk, vv, mx, lse, bias, part, mid, n2, hd, yy, lt, gs, r1, wp,
                   s0s, s0r, l0, s1s, s1r, s2s, s2r, s3s, s3r, hs, hr, xs, xr, ks, kr, ll, lo):
    cols=[(0,768),(768,896)]+[(1664+512*i,512) for i in range(3*ff_steps)]
    n=len(cols)
    dp,z,c,x,y=peers_of()
    q=dp//2; qx=2*y+1-x; qy=lax.rem(q+2,4); qd=3-q
    sib=(dp+1-2*c,z); dx=(2*qx+c,z); dy=(2*qy+c,z); dxy=(dx,dy)
    zb=lax.rem(z,2); pe=z+1-2*zb; mo=2-z//2; zo=2-2*(z//2)
    inner=(z==1)|(z==2); outer=(z==0)|(z==3)
    dpe=(dp,pe); dmo=(dp,mo)
    all_in=greet([sib,dx,dy]+[(dp,lax.rem(z+k,4)) for k in (1,2,3)])
    def cs(t): return pl.ds(cols[t][0],cols[t][1])
    def wr(t): return (w1,w2)[t] if t<2 else w.at[t-2]
    def s0(t,recv=False):
        return remote(wp.at[1-c,:,cs(t)], wr(t).at[(dp+1-2*c) if recv else dp,z], s0s.at[t], s0r.at[t], sib)
    def keep(t): return pltpu.make_async_copy(wp.at[c,:,cs(t)], wr(t).at[dp,z], l0.at[t])
    across=set(range(n-across_first,n))
    def group(t): return pl.ds(0,8) if t in across else pl.ds(2*q,2)
    def span(t): return z if t in across else pl.ds(0,4)
    tail=w_g.shape[1]-512*(2*ff_steps-1)
    narrow=set(range(n-3,n)) if 0<tail<512 and tail%128==0 else set()
    def each(t,act):
        if t in narrow:
            @pl.when(c==0)
            def _(): act(512)
            @pl.when(c==1)
            def _(): act(tail)
        else: act(cols[t][1])
    def s1a(t,wd,recv=False):
        r=wr(t).at[group(t), pe if recv else z, :, pl.ds(0,wd)]
        return remote(r,r,s1s.at[t,0],s1r.at[t,0],dpe)
    def s1b(t,wd):
        r=wr(t).at[group(t), z, :, pl.ds(0,wd)]
        return remote(r,r,s1s.at[t,1],s1r.at[t,1+zb],dmo)
    def s1bw(t,k,wd):
        r=wr(t).at[group(t), zo+k, :, pl.ds(0,wd)]
        return remote(r,r,s1s.at[t,1],s1r.at[t,1+k],dmo)
    def s1c(t,wd):
        r=wr(t).at[group(t), pl.ds(zo,2), :, pl.ds(0,wd)]
        return remote(r,r,s1s.at[t,2],s1r.at[t,3],dpe)
    def s2(t,a,wd,recv=False):
        r=wr(t).at[pl.ds(2*((qx,qy)[a] if recv else q),2), span(t), :, pl.ds(0,wd)]
        return remote(r,r,s2s.at[t,a],s2r.at[t,a],dxy[a])
    def s3(t,a,wd,recv=False):
        r=wr(t).at[2*(qd if recv else (qy,qx)[a])+a, span(t), :, pl.ds(0,wd)]
        return remote(r,r,s3s.at[t,a],s3r.at[t,a],dxy[a])
    def z_go(t): each(t,lambda wd: (s1a(t,wd).start(),s1b(t,wd).start()))
    def z_on(t):
        @pl.when(inner)
        def _(): each(t,lambda wd: (s1bw(t,0,wd).wait_recv(),s1bw(t,1,wd).wait_recv(),s1c(t,wd).start()))
    def z_in(t):
        each(t,lambda wd: s1a(t,wd,True).wait_recv())
        @pl.when(outer)
        def _(): each(t,lambda wd: s1c(t,wd).wait_recv())
    def xy_go(t,f): each(t,lambda wd: [f(t,a,wd).start() for a in range(2)])
    def xy_in(t,f): each(t,lambda wd: [f(t,a,wd,True).wait_recv() for a in range(2)])
    hp=hrow.shape[2]//h_parts
    def ht(p): return pl.ds(p*hp,hp)
    def ha(p,recv=False): return remote(hid.at[ht(p)],hrow.at[c,pe if recv else z,ht(p)],hs.at[p,0],hr.at[p,0],dpe)
    def hb(p): return remote(hid.at[ht(p)],hrow.at[c,z,ht(p)],hs.at[p,1],hr.at[p,1+zb],dmo)
    def hbw(p,k): return remote(hid.at[ht(p)],hrow.at[c,zo+k,ht(p)],hs.at[p,1],hr.at[p,1+k],dmo)
    def hc(p):
        r=hrow.at[c,pl.ds(zo,2),ht(p)]
        return remote(r,r,hs.at[p,2],hr.at[p,3],dpe)
    done=set()
    def once(*k):
        if k in done: return False
        done.add(k); return True
    def start1(t):
        if t<n and t not in across and once(1,t):
            keep(t).wait(); s0(t,True).wait_recv(); z_go(t)
    def across1(t):
        keep(t).wait(); s0(t,True).wait_recv(); xy_go(t,s2)
    def across2(t): xy_in(t,s2); xy_go(t,s3)
    def across3(t): xy_in(t,s3); z_go(t)
    def across4(t): z_on(t)
    def across5(t): z_in(t)
    def forward(t):
        if t<n and t not in across and once(5,t): z_on(t)
    def start2(t):
        forward(t)
        if t<n and t not in across and once(2,t):
            z_in(t); xy_go(t,s2)
    def start3(t):
        if 0<=t<n and t not in across and once(3,t):
            xy_in(t,s2); xy_go(t,s3)
    def finish(t):
        if 0<=t<n and t not in across and once(4,t): xy_in(t,s3)
    def advance(t):
        for u in range(t+4): start1(u)
        for f,u in ((forward,t+1),(start2,t),(start3,t-1),(finish,t-2)):
            for v in range(u+1): f(v)
    def h_go(p): ha(p).start(); hb(p).start()
    def h_on(p):
        @pl.when(inner)
        def _():
            hbw(p,0).wait_recv(); hbw(p,1).wait_recv(); hc(p).start()
    for h in range(2):
        for i,v in enumerate((w_q,w_k,w_v,w_o)): wp[h,:,384*i:384*i+384]=v[:,384*h:384*h+384]
        wp[h,:,1536:1664]=jnp.zeros((48,128),low)
        wp[h,:,1536:1538]=gains[...]
        for j in range(ff_steps):
            for i,v in enumerate((w_g,w_u,w_d)):
                a=1664+1536*j+512*i; f=512*(ff_steps*h+j); g=min(512,v.shape[1]-f)
                if g>0: wp[h,:,a:a+g]=v[:,f:f+g]
                if g<512: wp[h,:,a+max(g,0):a+512]=jnp.zeros((48,512-max(g,0)),low)
    keep_h=pltpu.make_async_copy(hid,hrow.at[c,z],ll.at[0]); keep_h.start()
    keep_c=pltpu.make_async_copy(cot,cotv.at[c],ll.at[1]); keep_c.start()
    keep_r=pltpu.make_async_copy(segr,sr.at[c],ll.at[2]); keep_r.start()
    keep_s=pltpu.make_async_copy(segc,sc.at[c],ll.at[3]); keep_s.start()
    for t in range(n): keep(t).start()
    all_in()
    for t in [*range(3),*sorted(across)]: s0(t).start()
    give_h=[remote(hid,hrow.at[c,z],xs.at[3],xr.at[3],sib)]; give_h[0].start()
    give_c=remote(cot,cotv.at[c],xs.at[0],xr.at[0],sib); give_c.start()
    give_r=remote(segr,sr.at[c],xs.at[1],xr.at[1],sib); give_r.start()
    give_s=remote(segc,sc.at[c],xs.at[2],xr.at[2],sib); give_s.start()
    for t in range(3,n-across_first): s0(t).start()
    start1(0); start1(1); start1(2); h_go(0)
    for t in sorted(across): across1(t)
    forward(0); start2(0); forward(1); start2(1); forward(2)
    h_on(0); start1(3); h_go(1)
    for t in sorted(across): across2(t)
    start3(0); start2(2)
    keep_h.wait(); keep_c.wait(); keep_r.wait(); keep_s.wait()
    remote(segr,sr.at[1-c],xs.at[1],xr.at[1],sib).wait_recv()
    remote(segc,sc.at[1-c],xs.at[2],xr.at[2],sib).wait_recv()
    remote(cot,cotv.at[1-c],xs.at[0],xr.at[0],sib).wait_recv()
    remote(hid,hrow.at[1-c,z],xs.at[3],xr.at[3],sib).wait_recv()
    start3(1); forward(3); h_on(1); start1(4); h_go(2)
    finish(0); finish(1)
    load_a=[pltpu.make_async_copy(w1,wa.at[:,:,:,pl.ds(0,768)],ll.at[4]),pltpu.make_async_copy(w2,wa.at[:,:,:,pl.ds(768,896)],ll.at[11])]
    for l in load_a: l.start()
    start3(2); start2(3); forward(4); h_on(2); start1(5); h_go(3)
    for l in load_a: l.wait()
    def wcol(a,b): return wa[:,:,:,a:b].reshape(1536,b-a)
    pick=(lanes((8,128))==lax.broadcasted_iota(jnp.int32,(8,128),0)).astype(low)
    gs[...]=dot_nt(pick,wcol(1536,1664))
    def transpose_cot(i,_):
        lt[2,:,pl.ds(pl.multiple_of(i*128,128),128)]=cotv[i//2,pl.ds(pl.multiple_of(lax.rem(i,2)*128,128),128),:].astype(f32).T.astype(low)
        return 0
    lax.fori_loop(0,4,transpose_cot,0)
    def normed(v,row):
        s=lax.rsqrt(jnp.mean(v*v,axis=-1,keepdims=True)+epsilon)
        return v*s*gs[row:row+1,:]
    def queries(i,_):
        a=pl.ds(pl.multiple_of(lax.rem(i,2)*128,128),128)
        v=normed(hrow[i//2,z,a,:].astype(f32),0)
        d=pl.ds(pl.multiple_of(i*128,128),128)
        qq[d,:]=dot(v.astype(low),wcol(0,384)).astype(low)
        lt[0,:,d]=v.T.astype(low)
        return 0
    lax.fori_loop(0,4,queries,0)
    def share(p,k,recv=False):
        r=hrow.at[1-c if recv else c,lax.rem(z+k,4),ht(p)]
        return remote(r,r,ks.at[p,k-1],kr.at[p,k-1],sib)
    def keys(r,p):
        v=jnp.concatenate([normed(hrow[r,zz,p*hp:p*hp+hp,:].astype(f32),0).astype(low) for zz in range(4)],axis=0)
        for o,w0 in ((kk,384),(vv,768)):
            d=dot(v,wcol(w0,w0+384)).astype(low)
            for zz in range(4): o[r,256*zz+p*hp:256*zz+p*hp+hp,:]=d[zz*hp:zz*hp+hp]
    def arrive(p):
        ha(p,True).wait_recv()
        @pl.when(outer)
        def _(): hc(p).wait_recv()
        for k in (1,2,3): share(p,k).start()
        keys(c,p)
    def other(p):
        for k in (1,2,3): share(p,k,True).wait_recv()
        keys(1-c,p)
    arrive(0)
    start2(4); start3(3); finish(2); forward(5); h_on(3)
    arrive(1); other(0)
    start2(5); start3(4)
    arrive(2); other(1)
    arrive(3); other(2); other(3)
    advance(6)
    for t in sorted(across)[:1]: across3(t)
    for h in range(6):
        pair=pl.ds(128*(h//2),128); odd=h%2
        bias[...]=pltpu.roll(jnp.broadcast_to(base[h:h+1,:],(256,1280)),1024,1,stride=1,stride_axis=0)
        def attend(i,_):
            r=i//2; d=pl.ds(pl.multiple_of(i*128,128),128)
            a=pl.ds(pl.multiple_of(lax.rem(i,2)*128,128),128)
            mine=(lanes((128,128))>=64) if odd else (lanes((128,128))<64)
            qh=jnp.where(mine,qq[d,pair].astype(f32),0.0).astype(low)
            s=dot_nt(qh,kk[r,:,pair])+bias[a,0:1024]
            s=jnp.where(sc[r,a,0:1]==sr[r,0:1,:],s,-1000000000.0)
            m=jnp.max(s,axis=-1,keepdims=True)
            e=jnp.exp(s-m)
            l=jnp.sum(e,axis=-1,keepdims=True)
            p=(e*(1.0/l)).astype(low)
            o=dot(p,vv[r,:,pair])
            if odd: o=jnp.where(mine,o,mx[d,pair].astype(f32))
            mx[d,pair]=o.astype(low)
            lse[r,a,:]=jnp.where(lanes((128,128))==h,m+jnp.log(l),lse[r,a,:]) if h else jnp.broadcast_to(m+jnp.log(l),(128,128))
            return 0
        lax.fori_loop(0,4,attend,0)
        if h in (1,3): advance(7+h//2)
        if h==3:
            for t in sorted(across)[:1]: across4(t)
        if h==5:
            for t in sorted(across)[1:]: across3(t)
    def project(i,_):
        part[i//2,pl.ds(pl.multiple_of(lax.rem(i,2)*128,128),128),:]=dot_nt(mx[pl.ds(pl.multiple_of(i*128,128),128),:],wcol(1152,1536))
        return 0
    lax.fori_loop(0,4,project,0)
    give_p=remote(part,r1,xs.at[4],xr.at[4],sib); give_p.start()
    advance(9)
    outs=[pltpu.make_async_copy(a,b,lo.at[i]) for i,(a,b) in enumerate(((qq,q_o),(kk,kk_o),(vv,vv_o),(mx,mx_o),(lse,lse_o),(sr,segr_o),(sc,segc_o),(cotv,cot_o)))]
    for o in outs: o.start()
    give_p.wait_recv()
    def middle(i,_):
        a=pl.ds(pl.multiple_of(lax.rem(i,2)*128,128),128); r=i//2
        d=pl.ds(pl.multiple_of(i*128,128),128)
        v=hrow[r,z,a,:].astype(f32)+(part[r,a,:]+r1[r,a,:])
        mid[r,a,:]=v
        v=normed(v,1)
        n2[d,:]=v.astype(low)
        lt[1,:,d]=v.T.astype(low)
        return 0
    lax.fori_loop(0,4,middle,0)
    give_p.wait_send()
    give_lt=pltpu.make_async_copy(lt,lt_o,ll.at[5]); give_lt.start()
    give_mid=pltpu.make_async_copy(mid,mid_o,ll.at[12]); give_mid.start()
    gs_o[...]=gs[...]
    advance(10)
    hout=[]
    for j in range(ff_steps):
        if j:
            for t in range(4+3*j,7+3*j) if j==ff_steps-1 else [10+j]: advance(t)
            if j==ff_steps-1:
                for t in sorted(across): across5(t)
        def load(act):
            def piece(i): each(2+3*j+i,lambda wd: act(pltpu.make_async_copy(w.at[3*j+i,:,:,:,pl.ds(0,wd)],wf.at[i,:,:,:,pl.ds(0,wd)],ll.at[6+i])))
            for i in range(3): piece(i)
        if 2+3*j in narrow:
            @pl.when(c==1)
            def _(): wf[:,:,:,:,tail:512]=jnp.zeros((3,8,4,48,512-tail),low)
        load(lambda m: m.start())
        b=j%2
        if j>=2: hout[j-2].wait()
        load(lambda m: m.wait())
        def feed(i,_):
            d=pl.ds(pl.multiple_of(i*256,256),256)
            v=n2[d,:]
            wg=wf[0].reshape(1536,512); wu=wf[1].reshape(1536,512); wd=wf[2].reshape(1536,512)
            gate=dot(v,wg); up=dot(v,wu)
            gh=dot(cotv[i],wd).astype(low).astype(f32)
            u2=gate*gate
            th=jnp.tanh(gelu_c*(gate+0.044715*(gate*u2)))
            act=0.5*gate*(1.0+th)
            slope=0.5*(1.0+th)+0.5*gate*(1.0-th*th)*(gelu_c*(1.0+3*0.044715*u2))
            hm=(act*up).astype(low); dg=(gh*up*slope).astype(low); du=(gh*act).astype(low)
            hd[b,0,d,:]=hm; hd[b,1,d,:]=dg; hd[b,2,d,:]=du
            yp=dot_nt(hm,wd); gp=dot_nt(dg,wg)+dot_nt(du,wu)
            if j: yp=yp+yy[i]; gp=gp+part[i]
            yy[i]=yp; part[i]=gp
            return 0
        lax.fori_loop(0,2,feed,0)
        if j==0:
            for t in sorted(across)[1:]: across4(t)
        o=pltpu.make_async_copy(hd.at[b],hdg_o.at[:,:,pl.ds(512*j,512)],lo.at[8+b]); o.start(); hout.append(o)
    give_m=[pltpu.make_async_copy(part,gnf_o,ll.at[9]),pltpu.make_async_copy(yy,yy_o,ll.at[10])]
    for g in give_m: g.start()
    for o in outs+hout[-2:]: o.wait()
    give_lt.wait(); give_mid.wait()
    for g in give_m: g.wait()
    give_c.wait_send(); give_r.wait_send(); give_s.wait_send()
    for g in give_h: g.wait_send()
    for p in range(h_parts):
        for k in (1,2,3): share(p,k).wait_send()
        ha(p).wait_send(); hb(p).wait_send()
        @pl.when(inner)
        def _(): hc(p).wait_send()
    for t in range(n):
        s0(t).wait_send()
        each(t,lambda wd: [g.wait_send() for g in (s1a(t,wd),s1b(t,wd),s2(t,0,wd),s2(t,1,wd),s3(t,0,wd),s3(t,1,wd))])
        @pl.when(inner)
        def _(): each(t,lambda wd: s1c(t,wd).wait_send())

def forward_call(weights, gains, hid, cot, segr, segc, base, ff_steps, cid=0):
    n=2+3*ff_steps
    S=jax.ShapeDtypeStruct; V=pltpu.VMEM; D=pltpu.SemaphoreType.DMA
    fw=512*ff_steps
    hbm=pl.BlockSpec(memory_space=pltpu.HBM); vm=pl.BlockSpec(memory_space=pltpu.VMEM)
    outs=(S((8,4,48,768),low),S((8,4,48,896),low),S((3*ff_steps,8,4,48,512),low),S((3,1536,512),low),S((3,512,fw),low),S((512,384),low),S((2,1024,384),low),S((2,1024,384),low),
          S((512,384),low),S((2,256,128),f32),S((2,256,1536),f32),S((2,256,1536),f32),S((8,1536),f32),S((2,8,1024),f32),S((2,256,128),f32),S((2,256,1536),f32),S((2,256,1536),low))
    ospec=[hbm]*17; ospec[12]=vm
    scratch=[V((2,4,256,1536),low),V((2,256,1536),low),V((2,8,1024),f32),V((2,256,128),f32),V((8,4,48,1664),low),V((3,8,4,48,512),low),
             V((512,384),low),V((2,1024,384),low),V((2,1024,384),low),V((512,384),low),V((2,256,128),f32),V((256,1280),f32),
             V((2,256,1536),f32),V((2,256,1536),f32),V((512,1536),low),V((2,3,512,512),low),V((2,256,1536),f32),V((3,1536,512),low),V((8,1536),f32),
             V((2,256,1536),f32),V((2,48,1664+1536*ff_steps),low),
             D((n,)),D((n,)),D((n,)),D((n,3)),D((n,4)),D((n,2)),D((n,2)),D((n,2)),D((n,2)),D((h_parts,3)),D((h_parts,4)),D((10,)),D((10,)),D((h_parts,3)),D((h_parts,3)),D((13,)),D((10,))]
    return pl.pallas_call(functools.partial(forward_kernel,ff_steps),out_shape=outs,
        in_specs=[vm]*8+[hbm]*4+[vm],out_specs=tuple(ospec),scratch_shapes=scratch,
        compiler_params=pltpu.CompilerParams(collective_id=cid,has_side_effects=True,vmem_limit_bytes=62*2**20))(*weights,gains,hid,cot,segr,segc,base)

def dot_tn(a,b):
    return lax.dot_general(a,b,(((0,),(0,)),((),())),preferred_element_type=jnp.float32)

part_slots=2
sum_slots=3
lag=8
def backward_kernel(chunks, ff_steps, w1, w2, lt_h, hdg, q_h, kk_h, vv_h, mx_h, lse_h, gnf_h, yy_h, mid_h, cot_h, segr_h, segc_h, hid_h, base, gains,
                    og, ou, od, oo, oq, ok, ov, oe, gin_o, bo_o, xg, xy, *rest):
    n=len(chunks)
    ra1=rest[0:n]; rb1=rest[n:2*n]; ra2=rest[2*n:3*n]; rb2=rest[3*n:4*n]; rz=rest[4*n:5*n]
    (fin,p,lt,gat,rbuf,wa,qq,kk,vv,mx,gm,lse,sr,sc,bias,dbias,dq,acc,dkv,rka,rkb,rkc,dk,dv,part,r3,hid,dtab,ext,cb,
     ll,lr,lo,s1,v1,s2,v2,s3,v3,s4,v4,ks,kr,xs,xr,lb)=rest[5*n:]
    dp,z,c,x,y=peers_of()
    sib=(dp+1-2*c,z); dx=(dp+2-4*x,z); dy=(lax.rem(dp+4,8),z)
    zs=[lax.rem(z+k,4) for k in (1,2,3)]; dz=[(dp,zz) for zz in zs]
    zb=lax.rem(z,2); pe=z+1-2*zb; mo=2-z//2; zo=2-2*(z//2)
    inner=(z==1)|(z==2); outer=(z==0)|(z==3)
    def ka(pp,recv=False): return remote(dkv.at[pp,pe],rka.at[pp],ks.at[pp,0],kr.at[pp,0],(dp,pe))
    def kc(pp): return remote(dkv.at[pp,pl.ds(zo,2)],rkc.at[pp],ks.at[pp,1],kr.at[pp,1],(dp,pe))
    def kb(pp,k): return remote(dkv.at[pp,zo+k],rkb.at[pp],ks.at[pp,2+k],kr.at[pp,2],(dp,zo+k))
    def relay(pp):
        @pl.when(inner)
        def _():
            kc(pp).wait_recv()
            for k in range(2):
                for j in range(2):
                    for r in range(2):
                        dkv[pp,zo+k,j,r]=(dkv[pp,zo+k,j,r].astype(f32)+rkc[pp,k,j,r].astype(f32)).astype(low)
                kb(pp,k).start()
    loads=[pltpu.make_async_copy(a,b,ll.at[i]) for i,(a,b) in enumerate((
        (lt_h.at[pl.ds(1,2)],lt),(w2.at[:,:,:,pl.ds(384,384)],wa.at[:,:,:,pl.ds(0,384)]),(q_h,qq),(kk_h,kk),(vv_h,vv),(mx_h,mx),(lse_h,lse),(segr_h,sr),(segc_h,sc),(hid_h,hid)))]
    for l in loads: l.start()
    slots=rbuf.shape[0]
    def fetch(t):
        kind,i,j=chunks[t][3]
        return pltpu.make_async_copy(hdg.at[i,:,pl.ds(512*j,512)],rbuf.at[t%slots],lr.at[t])
    feeds=[t for t in range(n) if chunks[t][3][0]=="feed"]
    for t in feeds[:slots]: fetch(t).start()
    greet([sib,dx,dy]+dz)()
    load_n=pltpu.make_async_copy(lt_h.at[0],lt.at[1],ll.at[14])
    done=set()
    def once(*k):
        if k in done: return False
        done.add(k); return True
    def each(t,act):
        width,fw=chunks[t][4][2]; tail=chunks[t][4][3]-fw-chunks[t][4][1]
        if 0<tail<width:
            @pl.when(c==0)
            def _(): act(pl.ds(0,width))
            @pl.when(c==1)
            def _(): act(pl.ds(0,tail))
        else: act(pl.ds(0,width))
    def hop1(t,wd):
        b=t%part_slots
        return (remote(p.at[b,:,1-x,0,:,:,wd],ra1[t].at[:,:,:,wd],s1.at[t,0],v1.at[t,0],dx),
                remote(p.at[b,1-y,:,1,:,:,wd],rb1[t].at[:,:,:,wd],s1.at[t,1],v1.at[t,1],dy))
    def hop2(t,wd):
        return (remote(ra1[t].at[1-y,:,:,wd],ra2[t].at[:,:,wd],s2.at[t,0],v2.at[t,0],dy),
                remote(rb1[t].at[1-x,:,:,wd],rb2[t].at[:,:,wd],s2.at[t,1],v2.at[t,1],dx))
    def hop3(t,wd):
        return [remote(r[t].at[zs[k],:,wd],rz[t].at[k,i,:,wd],s3.at[t,k,i],v3.at[t,k,i],dz[k]) for k in range(3) for i,r in enumerate((ra2,rb2))]
    def go(t,f): each(t,lambda wd: [d.start() for d in f(t,wd)])
    def came(t,f): each(t,lambda wd: [d.wait_recv() for d in f(t,wd)])
    def went(t,f): each(t,lambda wd: [d.wait_send() for d in f(t,wd)])
    def stage1(t):
        left,off,wd,src=chunks[t][:4]; b=t%part_slots
        if t>=part_slots:
            went(t-part_slots,hop1)
        if src[0]=="feed":
            fetch(t).wait()
            right=lambda: rbuf[t%slots]
        else:
            right=(lambda: mx[...],lambda: dq[...],lambda: dk[...],lambda: dv[...],None)[src[1]]
        if src==("ref",1,0): load_n.wait()
        if right is None:
            p[b,:,:,:,:,:,0:wd]=ext[...].T.astype(low).reshape(2,2,2,4,48,wd)
        else:
            def body(i,_):
                rs=pl.ds(pl.multiple_of(i*192,192),192)
                lhs=gat[rs,:] if left==3 else lt[left,rs,:]
                p[b,i//4,lax.rem(i//2,2),lax.rem(i,2),:,:,0:wd]=dot(lhs,right()).astype(low).reshape(4,48,wd)
                return 0
            lax.fori_loop(0,8,body,0)
        if t==feeds[-1]:
            load_n.start()
        if src[0]=="feed" and t+slots<n and chunks[t+slots][3][0]=="feed": fetch(t+slots).start()
        go(t,hop1)
    def stage2(t):
        wd=chunks[t][2]; b=t%part_slots
        came(t,hop1)
        def body(i,_):
            h=i//4; zz=lax.rem(i,4)
            ra1[t][h,zz]=ra1[t][h,zz]+p[b,h,x,0,zz,:,0:wd]
            rb1[t][h,zz]=rb1[t][h,zz]+p[b,y,h,1,zz,:,0:wd]
            return 0
        lax.fori_loop(0,8,body,0)
        go(t,hop2)
    def stage3(t):
        came(t,hop2)
        def body(zz,_):
            ra2[t][zz]=ra2[t][zz]+ra1[t][y,zz]
            rb2[t][zz]=rb2[t][zz]+rb1[t][x,zz]
            return 0
        lax.fori_loop(0,4,body,0)
        go(t,hop3)
    def place(t,pair,acts,half):
        o,offset,width,total=chunks[t][4]
        o=(og,ou,od,oo,oq,ok,ov,oe)[o]
        last=total-(width[1]+offset)
        def act(size):
            cols=pl.ds(pl.multiple_of(half*width[1]+offset,128),size)
            for m,how in zip(pair(None,size,cols,o),acts):
                if how: getattr(m,how)()
        if last>=width[0]: act(width[0])
        else:
            @pl.when(half==0)
            def _(): act(width[0])
            if last>0:
                @pl.when(half==1)
                def _(): act(last)
    def drain(t):
        place(t,lambda _,width,cols,o: (
            remote(fin.at[0,0,:,pl.ds(0,width)],o.at[:,cols],s4.at[t],v4.at[t],sib),
            pltpu.make_async_copy(fin.at[0,0,:,pl.ds(0,width)],o.at[:,cols],lo.at[t])),("wait_send","wait"),c)
    def arrive(t):
        place(t,lambda _,width,cols,o: (remote(fin.at[0,0,:,pl.ds(0,width)],o.at[:,cols],s4.at[t],v4.at[t],sib),),("wait_recv",),1-c)
    def stage4(t):
        wd=chunks[t][2]
        came(t,hop3)
        f0=ra2[t][z].astype(f32); f1=rb2[t][z].astype(f32)
        for k in range(3):
            f0=f0+rz[t][k,0].astype(f32); f1=f1+rz[t][k,1].astype(f32)
        b=t%sum_slots
        if t>=sum_slots:
            drain(t-sum_slots)
        fin[b,0,:,0:wd]=f0; fin[b,1,:,0:wd]=f1
        place(t,lambda _,width,cols,o: (
            remote(fin.at[b,1-c,:,pl.ds(0,width)],o.at[:,cols],s4.at[t],v4.at[t],sib),
            pltpu.make_async_copy(fin.at[b,c,:,pl.ds(0,width)],o.at[:,cols],lo.at[t])),("start","start"),c)
    def step(s):
        for f,t in ((stage2,s),(stage1,s+2),(stage3,s-1),(stage4,s-lag)):
            if 0<=t<n and once(f.__name__,t): f(t)
    give_g=remote(gnf_h,xg,xs.at[1],xr.at[1],sib); give_g.start()
    give_y=remote(yy_h.at[1-c],xy,xs.at[2],xr.at[2],sib); give_y.start()
    loads[0].wait()
    stage1(0); stage1(1); once("stage1",0); once("stage1",1)
    for l in loads[1:]: l.wait()
    def wcol(a,b): return wa[:,:,:,a:b].reshape(1536,b-a)
    give_g.wait_recv()
    total=jnp.zeros((1,1536),f32)
    for i in range(4):
        r=i//2; a=pl.ds(128*(i%2),128); d=pl.ds(128*i,128)
        first=part.at[0,pl.ds(0,128)]; second=part.at[0,pl.ds(128,128)]; third=part.at[1,pl.ds(0,128)]
        moves=[pltpu.make_async_copy(f,g,lb.at[k]) for k,(f,g) in enumerate(((mid_h.at[r,a],first),(gnf_h.at[r,a],second),(xg.at[r,a],third),(cot_h.at[r,a],cb)))]
        for m in moves: m.start()
        for m in moves: m.wait()
        v=part[0,0:128,:]; gn=part[0,128:256,:]+part[1,0:128,:]
        s=lax.rsqrt(jnp.mean(v*v,axis=-1,keepdims=True)+epsilon)
        wg=gn*gains[1:2,:]
        g=cb[...].astype(f32)+(s*wg-v*(s*s*s)*jnp.mean(wg*v,axis=-1,keepdims=True))
        total=total+jnp.where(c==r,1.0,0.0)*jnp.sum(gn*v*s,axis=0,keepdims=True)
        part[1,128:256,:]=g
        @pl.when(c==r)
        def _():
            back=pltpu.make_async_copy(part.at[1,pl.ds(128,128)],gin_o.at[a],lb.at[4]); back.start(); back.wait()
        gat[:,d]=g.T.astype(low)
        gm[d,:]=dot(g.astype(low),wcol(0,384)).astype(low)
    ext[...]=jnp.zeros((128,1536),f32)
    def spread(v,row):
        upper=v.astype(low)
        ext[row:row+8,:]=upper.astype(f32)
        ext[row+8:row+16,:]=v-upper.astype(f32)
    spread(jnp.broadcast_to(total,(8,1536)),32)
    load_w=[pltpu.make_async_copy(w1,wa.at[:,:,:,pl.ds(0,768)],ll.at[13]),pltpu.make_async_copy(w2.at[:,:,:,pl.ds(0,384)],wa.at[:,:,:,pl.ds(768,384)],ll.at[15])]
    for l in load_w: l.start()
    step(0)
    dbias[...]=jnp.zeros((256,1280),f32)
    dtab[...]=jnp.zeros((8,1280),f32)
    at=1
    for h in range(6):
        odd=h%2; pair=pl.ds(128*(h//2),128); pp=h//2
        bias[...]=pltpu.roll(jnp.broadcast_to(base[h:h+1,:],(256,1280)),1024,1,stride=1,stride_axis=0)
        if not odd: acc[...]=jnp.zeros((2,2,1024,128),f32)
        def attend(i,_):
            r=i//2; d=pl.ds(pl.multiple_of(i*128,128),128)
            a=pl.ds(pl.multiple_of(lax.rem(i,2)*128,128),128)
            mine=(lanes((128,128))>=64) if odd else (lanes((128,128))<64)
            qh=jnp.where(mine,qq[d,pair].astype(f32),0.0).astype(low)
            gh=jnp.where(mine,gm[d,pair].astype(f32),0.0).astype(low)
            s=dot_nt(qh,kk[r,:,pair])+bias[a,0:1024]
            s=jnp.where(sc[r,a,0:1]==sr[r,0:1,:],s,-1000000000.0)
            pr=jnp.exp(s-lse[r,a,h:h+1])
            gp=dot_nt(gh,vv[r,:,pair])
            gl=(pr*(gp-jnp.sum(pr*gp,axis=-1,keepdims=True))).astype(low)
            wide=gl.astype(f32)
            dbias[a,0:1024]=wide+jnp.where(r==0,0.0,1.0)*dbias[a,0:1024]
            g=jnp.where(mine,dot(gl,kk[r,:,pair]),0.0)
            if odd: g=g+dq[d,pair].astype(f32)
            dq[d,pair]=g.astype(low)
            acc[0,r]=acc[0,r]+dot_tn(gl,qh)
            acc[1,r]=acc[1,r]+dot_tn(pr.astype(low),gh)
            return 0
        lax.fori_loop(0,4,attend,0)
        m=128
        v=dbias[0:128,:]+pltpu.roll(dbias[128:256,:],1280-128,1)
        while m>1:
            m//=2
            v=v[0:m]+pltpu.roll(v[m:2*m],1280-m,1)
        dtab[h:h+1,:]=pltpu.roll(v,256,1)
        if odd:
            for j in range(2):
                for r in range(2):
                    for zz in range(4):
                        dkv[pp,zz,j,r]=acc[j,r,256*zz:256*zz+256,:].astype(low)
            ka(pp).start()
            @pl.when(outer)
            def _(): kc(pp).start()
            step(at); at+=1
            if pp: relay(pp-1)
    tab=dtab[...]
    high=tab.astype(low); rest1=tab-high.astype(f32); mid1=rest1.astype(low); last=(rest1-mid1.astype(f32)).astype(low)
    shift=lax.broadcasted_iota(jnp.int32,(1280,128),0)-256-256*z
    spots=jnp.where(bucket_table(shift)==lanes((1280,128)),1.0,0.0).astype(low)
    tile=jnp.where(lax.rem(lanes((128,1536)),48)==lax.broadcasted_iota(jnp.int32,(128,1536),0),1.0,0.0).astype(low)
    found=dot(high,spots)+dot(mid1,spots)+dot(last,spots)
    upper=found.astype(low)
    ext[0:8,:]=dot(upper,tile)
    ext[8:16,:]=dot((found-upper.astype(f32)).astype(low),tile)
    give_y.wait_recv()
    for i in range(2):
        a=pl.ds(128*i,128)
        first=part.at[0,pl.ds(0,128)]; second=part.at[0,pl.ds(128,128)]; third=part.at[1,pl.ds(0,128)]
        moves=[pltpu.make_async_copy(f,g,lb.at[k]) for k,(f,g) in enumerate(((mid_h.at[c,a],first),(yy_h.at[c,a],second),(xy.at[a],third)))]
        for m in moves: m.start()
        for m in moves: m.wait()
        part[1,128:256,:]=part[0,0:128,:]+(part[0,128:256,:]+part[1,0:128,:])
        back=pltpu.make_async_copy(part.at[1,pl.ds(128,128)],bo_o.at[a],lb.at[4]); back.start(); back.wait()
    step(at); at+=1
    relay(2)
    while at<9:
        step(at); at+=1
    for pp in range(3):
        ka(pp).wait_recv(); kb(pp,0).wait_recv()
        for j,o in enumerate((dk,dv)):
            for r in range(2):
                v=dkv[pp,z,j,r].astype(f32)+rka[pp,j,r].astype(f32)+rkb[pp,j,r].astype(f32)
                o[256*r:256*r+256,128*pp:128*pp+128]=v.astype(low)
    step(at); at+=1
    for l in load_w: l.wait()
    def input_grad(i,_):
        d=pl.ds(pl.multiple_of(i*128,128),128); a=pl.ds(pl.multiple_of(lax.rem(i,2)*128,128),128)
        part[i//2,a,:]=dot_nt(dq[d,:],wcol(0,384))+dot_nt(dk[d,:],wcol(384,768))+dot_nt(dv[d,:],wcol(768,1152))
        return 0
    lax.fori_loop(0,4,input_grad,0)
    give=remote(part.at[1-c],r3,xs.at[0],xr.at[0],sib); give.start()
    step(at); at+=1
    give.wait_send()
    load_i=pltpu.make_async_copy(gin_o,part.at[1-c],lb.at[0]); load_i.start()
    give.wait_recv(); load_i.wait()
    def last_grad(i,total):
        a=pl.ds(pl.multiple_of(i*128,128),128)
        v=hid[a,:].astype(f32); gn=part[c,a,:]+r3[a,:]
        s=lax.rsqrt(jnp.mean(v*v,axis=-1,keepdims=True)+epsilon)
        wg=gn*gains[0:1,:]
        part[1-c,a,:]=part[1-c,a,:]+(s*wg-v*(s*s*s)*jnp.mean(wg*v,axis=-1,keepdims=True))
        return total+jnp.sum(gn*v*s,axis=0,keepdims=True)
    total=lax.fori_loop(0,2,last_grad,jnp.zeros((1,1536),f32))
    spread(jnp.broadcast_to(total,(8,1536)),16)
    give_i=pltpu.make_async_copy(part.at[1-c],gin_o,ll.at[12]); give_i.start()
    while at<n+lag:
        step(at); at+=1
    for t in range(n):
        arrive(t)
        if t>=n-sum_slots: drain(t)
        if t>=n-part_slots:
            went(t,hop1)
        went(t,hop2); went(t,hop3)
    for pp in range(3):
        ka(pp).wait_send()
        @pl.when(outer)
        def _(): kc(pp).wait_send()
        @pl.when(inner)
        def _(): kb(pp,0).wait_send(); kb(pp,1).wait_send()
    give_i.wait(); give_g.wait_send(); give_y.wait_send()

def backward_chunks(ff_steps,ff):
    fw=512*ff_steps
    chunks=[]
    for j in range(ff_steps):
        for left,i,o in ((0,1,0),(0,2,1),(1,0,2)):
            chunks.append((left,0,512,("feed",i,j),(o,512*j,(512,fw),ff)))
    for k in range(4): chunks.append((3 if k==0 else 1,0,384,("ref",k,0),(3+k,0,(384,384),768)))
    chunks.append((1,0,128,("ref",4,0),(7,0,(128,128),256)))
    return chunks

def backward_call(w1,w2,lt,hdg,q,kk,vv,mx,lse,gnf,yy,mid,cot,segr,segc,hid,base,gains,ff_steps,ff,cid=1):
    chunks=backward_chunks(ff_steps,ff); n=len(chunks)
    S=jax.ShapeDtypeStruct; V=pltpu.VMEM; D=pltpu.SemaphoreType.DMA
    hbm=pl.BlockSpec(memory_space=pltpu.HBM); vm=pl.BlockSpec(memory_space=pltpu.VMEM)
    ws=[k[2] for k in chunks]
    scratch=[V((2,4,48,k),low) for k in ws]*1+[V((2,4,48,k),low) for k in ws]+[V((4,48,k),low) for k in ws]+[V((4,48,k),low) for k in ws]+[V((3,2,48,k),low) for k in ws]
    scratch+=[V((sum_slots,2,48,512),f32),V((part_slots,2,2,2,4,48,512),low),V((2,1536,512),low),V((1536,512),low),V((2,512,512),low),V((8,4,48,1152),low),
      V((512,384),low),V((2,1024,384),low),V((2,1024,384),low),V((512,384),low),V((512,384),low),V((2,256,128),f32),V((2,8,1024),f32),V((2,256,128),f32),
      V((256,1280),f32),V((256,1280),f32),V((512,384),low),V((2,2,1024,128),f32),V((3,4,2,2,256,128),low),V((3,2,2,256,128),low),V((3,2,2,256,128),low),V((3,2,2,2,256,128),low),V((512,384),low),V((512,384),low),
      V((2,256,1536),f32),V((256,1536),f32),V((256,1536),low),V((8,1280),f32),V((128,1536),f32),V((128,1536),low)]
    scratch+=[D((16,)),D((n,)),D((n,)),D((n,2)),D((n,2)),D((n,2)),D((n,2)),D((n,3,2)),D((n,3,2)),D((n,)),D((n,)),D((3,4)),D((3,3)),D((3,)),D((3,)),D((5,))]
    return pl.pallas_call(functools.partial(backward_kernel,chunks,ff_steps),out_shape=(S((48,ff),f32),)*3+(S((48,768),f32),)*4+(S((48,256),f32),S((256,1536),f32),S((256,1536),f32),S((2,256,1536),f32),S((256,1536),f32)),
        in_specs=[hbm]*16+[vm]*2,out_specs=(hbm,)*12,scratch_shapes=scratch,
        compiler_params=pltpu.CompilerParams(collective_id=cid,has_side_effects=True,vmem_limit_bytes=62*2**20))(w1,w2,lt,hdg,q,kk,vv,mx,lse,gnf,yy,mid,cot,segr,segc,hid,base,gains)

def settle_kernel(count,*refs):
    given,kept,held,sem_in,sem_out=refs[:count],refs[count:2*count],refs[2*count:3*count],refs[3*count],refs[3*count+1]
    ins=[pltpu.make_async_copy(a,b,sem_in.at[i]) for i,(a,b) in enumerate(zip(given,held))]
    outs=[pltpu.make_async_copy(a,b,sem_out.at[i]) for i,(a,b) in enumerate(zip(held,kept))]
    for m in ins: m.start()
    for m,o in zip(ins,outs):
        m.wait(); o.start()
    for o in outs: o.wait()

def settle(arrays):
    hbm=pl.BlockSpec(memory_space=pltpu.HBM); count=len(arrays)
    return pl.pallas_call(functools.partial(settle_kernel,count),out_shape=tuple(jax.ShapeDtypeStruct(a.shape,a.dtype) for a in arrays),
        in_specs=[hbm]*count,out_specs=(hbm,)*count,
        scratch_shapes=[pltpu.VMEM(a.shape,a.dtype) for a in arrays]+[pltpu.SemaphoreType.DMA((count,))]*2,
        compiler_params=pltpu.CompilerParams(vmem_limit_bytes=62*2**20))(*arrays)

def cut(v,h,w):
    n=v.shape[1]
    a=min(h*w,n); b=min((h+1)*w,n)
    p=v[:,a:b]
    return jnp.pad(p,((0,0),(0,w-(b-a)))) if b-a<w else p
def pack(wq,wk,wv,wo,ga,gf,wg,wu,wd,steps):
    gains=jnp.pad(jnp.stack([ga,gf],axis=1),((0,0),(0,126)))
    fw=512*steps
    rows=[]
    for h in (0,1):
        m=[cut(v,h,384) for v in (wq,wk,wv,wo.T)]+[gains]
        f=[cut(v,h,fw) for v in (wg,wu,wd.T)]
        for j in range(steps):
            m+=[v[:,512*j:512*j+512] for v in f]
        rows.append(jnp.concatenate(m,axis=1))
    return jnp.stack(rows)
def seg_ids(seg):
    n=seg.shape[1]
    place=jnp.arange(n,dtype=jnp.int32)
    ids=jnp.where(seg[0]>0,seg[0],-1-place).astype(jnp.float32)
    r=jnp.broadcast_to(ids[None],(8,n))
    mine=lax.dynamic_slice_in_dim(ids,lax.axis_index("seq")*256,256,0)
    return r, jnp.broadcast_to(mine[:,None],(256,128))
def base_of(table):
    off=jnp.arange(1280,dtype=jnp.int32)-256-256*lax.axis_index("seq")
    oh=(bucket_table(off)[:,None]==jnp.arange(32,dtype=jnp.int32)).astype(jnp.float32)
    c=lax.rem(lax.axis_index("dp"),2)
    tab=table.astype(jnp.float32)
    mine=jnp.where(c==0,tab[:,:6],tab[:,6:])
    b=jnp.einsum("ub,bh->hu",oh,mine,precision=lax.Precision.HIGHEST)
    return b, oh

def kernel_local(hid,seg,ga,wq,wk,wv,wo,tab,gf,wg,wu,wd,cot):
    ff=wg.shape[1]; steps=-(-ff//1024)
    gain_cols=jnp.stack([ga,gf],axis=1)
    r,s=seg_ids(seg); b=base_of(tab)[0]
    w1,w2,w,lt,hdg,q,kk,vv,mx,lse,gnf,yy,gains,segr,segc,mid,cot2=forward_call((wq,wk,wv,wo.T,wg,wu,wd.T),gain_cols,hid[0],cot[0],r,s,b,steps)
    og,ou,od,oo,oq,ok,ov,oe,gin,bo,_,_=backward_call(w1,w2,lt,hdg,q,kk,vv,mx,lse,gnf,yy,mid,cot2,segr,segc,hid[0],b,gains,steps,ff)
    og,ou,od,oo,oq,ok,ov,gin,bo=settle((og,ou,od,oo,oq,ok,ov,gin,bo))
    e=oe.reshape(48,2,128)
    t=e[:32,:,0:8]+e[:32,:,8:16]
    table=t[:,:,:6].reshape(32,12)
    g=e[:,0]+e[:,1]
    gg=lambda a: g[:,a]+g[:,a+8]
    return (bo[None],gin[None],gg(16),oq,ok,ov,oo.T,table,gg(32),og,ou,od.T)


def solution(mesh):
    in_specs = (
        P("dp", "seq", None),
        P("dp", None),
        P(("dp", "seq")),
        P(("dp", "seq"), None),
        P(("dp", "seq"), None),
        P(("dp", "seq"), None),
        P(None, ("dp", "seq")),
        P(),
        P(("dp", "seq")),
        P(("dp", "seq"), None),
        P(("dp", "seq"), None),
        P(None, ("dp", "seq")),
        P("dp", "seq", None),
    )
    out_specs = (
        P("dp", "seq", None),
        P("dp", "seq", None),
        P(("dp", "seq")),
        P(("dp", "seq"), None),
        P(("dp", "seq"), None),
        P(("dp", "seq"), None),
        P(None, ("dp", "seq")),
        P(),
        P(("dp", "seq")),
        P(("dp", "seq"), None),
        P(("dp", "seq"), None),
        P(None, ("dp", "seq")),
    )
    small = mesh.shape["dp"] == 8 and mesh.shape["seq"] == 4
    local = kernel_local if small else plain_local
    return jax.shard_map(local, mesh=mesh, in_specs=in_specs, out_specs=out_specs, check_vma=False)
```
